128 devices in a mesh: child: 2 (over z_lo), row: 16 (over x, y), col: 4 (over z_hi, core).
Axes of the slice: x: 4, y: 4, z: 4 (z_hi: 2, z_lo: 2; z = z_hi * 2 + z_lo), core: 2. Of those that a mesh axis runs over, the one named last changes fastest.
Arguments:
- child_fronts: float32 [2, 4096, 4096], P('child', 'row', 'col'), as said below
- root_front: float32 [8192, 8192], P('col', ('child', 'row')), as said below
- block_maps: int32 [2, 24], replicated, may hold values from 0 to 63, as said below
Outputs:
- child_factor: float32 [2, 4096, 1024], P('child', 'row')
- root_factor: float32 [8192, 512], P('col')
- root_trailing: float32 [8192, 8192], P('col', ('child', 'row'))
The draws below stay inside these ranges and needn't reach their ends.
Inputs may be any that keep to these rules, and one draw needn't show every extreme that they name: `block_maps`: row c lists 24 different root blocks in increasing order; block 0 appears in the first row and the last root block in the last row. `child_fronts`: each front is symmetric and positive definite. `root_front`: symmetric and positive definite.
All inputs are finite; a program needn't handle non-finite values.
Results may differ from the reference program's by a relative error of at most 0.0003.
Values may be sent and summed in bfloat16 or wider, within the bound.
No kernel may reach another device: no remote copies, remote signals or barrier semaphores. Data moves between devices by JAX's collectives and lax.ppermute only.
A program may use at most 128 MiB of HBM per device.

```python
import math
import jax
import jax.numpy as jnp
from jax import lax

FC = 4096
R = 8192
PANEL = 512
CPAN = 2
RPAN = 1
BLK = 128
CHILDREN = 2
PIV = 1024
NCB = 24


def symmetric_front(key, count, order):
    base = jax.random.uniform(jax.random.fold_in(key, 11), (count, order, order), jnp.float32, -1.0, 1.0)
    mirrored = 0.5 * (base + jnp.swapaxes(base, 1, 2))
    diag_values = jax.random.uniform(jax.random.fold_in(key, 12), (count, order), jnp.float32, 1.3, 2.9) * math.sqrt(order)
    on_diag = jnp.eye(order, dtype=jnp.bool_)
    front = jnp.where(on_diag[None], diag_values[:, :, None], mirrored)
    factor_scale = 0.06 * math.sqrt(math.sqrt(order))
    loadings = jax.random.normal(jax.random.fold_in(key, 14), (count, order, 8), jnp.float32) * factor_scale
    for term_index in range(8):
        column = loadings[:, :, term_index]
        front = front + column[:, :, None] * column[:, None, :]
    return front


def draw_child_fronts(key, part):
    return symmetric_front(key, CHILDREN, FC)


def draw_root_front(key, part):
    return symmetric_front(key, 1, R)[0]


def draw_block_maps(key, part):
    block_count = R // BLK
    row_list = []
    for child_index in range(CHILDREN):
        shuffled = jax.random.permutation(jax.random.fold_in(key, child_index), block_count)
        chosen = jnp.sort(shuffled[:NCB])
        if child_index == 0:
            chosen = chosen.at[0].set(0)
        if child_index == CHILDREN - 1:
            chosen = chosen.at[NCB - 1].set(block_count - 1)
        row_list.append(chosen)
    return jnp.stack(row_list).astype(jnp.int32)


def setup_inputs(seed: int = 0) -> dict:
    keys = jax.random.split(jax.random.key(seed), 4)
    return {
        "child_fronts": draw_child_fronts(jax.random.fold_in(keys[3], 71), 0),
        "root_front": draw_root_front(jax.random.fold_in(keys[3], 71), 0),
        "block_maps": draw_block_maps(jax.random.fold_in(keys[3], 71), 0),
    }


def factor_panels(front, panel_count):
    order = front.shape[0]
    row_ids = jnp.arange(order, dtype=jnp.int32)
    columns = []
    for panel_index in range(panel_count):
        first_col = panel_index * PANEL
        diagonal = front[first_col:first_col + PANEL, first_col:first_col + PANEL]
        diag_factor = jnp.linalg.cholesky(diagonal)
        solved = lax.linalg.triangular_solve(diag_factor, front[:, first_col:first_col + PANEL], left_side=False, lower=True, transpose_a=True)
        factor_rows = jnp.where(row_ids[:, None] >= first_col, solved, 0.0)
        update_rows = jnp.where(row_ids[:, None] >= first_col + PANEL, solved, 0.0).astype(jnp.bfloat16)
        front = front - jnp.dot(update_rows.astype(jnp.float32), update_rows.T.astype(jnp.float32), preferred_element_type=jnp.float32)
        columns.append(factor_rows)
    return (front, jnp.concatenate(columns, axis=1))

def reference(child_fronts, root_front, block_maps):
    assembled = root_front
    factors = []
    offsets = jnp.arange(BLK, dtype=jnp.int32)
    for child_index in range(CHILDREN):
        trailing, factor = factor_panels(child_fronts[child_index], CPAN)
        factors.append(factor)
        targets = (block_maps[child_index][:, None] * BLK + offsets[None, :]).reshape(-1).astype(jnp.int32)
        assembled = assembled.at[targets[:, None], targets[None, :]].add(trailing[PIV:, PIV:])
    root_trailing, root_factor = factor_panels(assembled, RPAN)
    return (jnp.stack(factors), root_factor, root_trailing)
```

```python
import jax
import jax.numpy as jnp
from jax import lax
from jax.experimental import pallas as pl
from jax.experimental.pallas import tpu as pltpu
from jax.sharding import PartitionSpec as P

F32 = jnp.float32
BF16 = jnp.bfloat16
HI = lax.Precision.HIGHEST
ROWS, COLS = 16, 4
NCB = 24
VM = pltpu.CompilerParams(vmem_limit_bytes=56 << 20)


def lane_copy(v, k):
    return jnp.broadcast_to(v[:, k:k + 1], (8, 128))


def sub_copy(v, k):
    return jnp.broadcast_to(v[k:k + 1, :], (8, 128))


def dot(a, b, ca, cb):
    return lax.dot_general(a, b, (((ca,), (cb,)), ((), ())), precision=HI, preferred_element_type=F32)


def dot16(a, b, ca, cb):
    return lax.dot_general(a, b, (((ca,), (cb,)), ((), ())), preferred_element_type=F32)


def inverse_factor128(block):
    lane = lax.broadcasted_iota(jnp.int32, (8, 128), 1)
    sub = lax.broadcasted_iota(jnp.int32, (8, 128), 0)
    w = [block[8 * t:8 * t + 8, :] for t in range(16)]
    for s in range(16):
        c = {t: [lane_copy(w[t], 8 * s + j) for j in range(8)] for t in range(s, 16)}
        inside = (lane >= 8 * s) & (lane < 8 * s + 8)
        w[s] = jnp.where(inside, (lane - 8 * s == sub).astype(F32), w[s])
        for t in range(s + 1, 16):
            w[t] = jnp.where(inside, 0.0, w[t])
        for j in range(8):
            scale = lax.rsqrt(sub_copy(c[s][j], j))
            pivot_row = sub_copy(w[s], j) * scale
            ahead = {k: sub_copy(c[s][j], k) * scale for k in range(j + 1, 8)}
            for t in range(s, 16):
                l = c[t][j] * scale
                if t == s:
                    l = jnp.where(sub > j, l, 0.0)
                for k in range(j + 1, 8):
                    c[t][k] = c[t][k] - l * ahead[k]
                w[t] = w[t] - l * pivot_row
            w[s] = jnp.where(sub == j, pivot_row, w[s])
    return jnp.concatenate([jnp.where(lane <= sub + 8 * t, w[t], 0.0) for t in range(16)], axis=0)


def inverse_factor512(a, b):
    n = 512
    b[...] = jnp.zeros((n, n), F32)
    for k in range(n // 128):
        o = 128 * k
        g = inverse_factor128(a[o:o + 128, o:o + 128])
        if k > 0:
            b[o:o + 128, 0:o] = dot(g, b[o:o + 128, 0:o], 1, 0)
        b[o:o + 128, o:o + 128] = g
        r = o + 128
        if r < n:
            l = dot(a[r:n, o:o + 128], g, 1, 1)
            a[r:n, r:n] = a[r:n, r:n] - dot(l, l, 1, 1)
            b[r:n, 0:r] = b[r:n, 0:r] - dot(l, b[o:o + 128, 0:r], 1, 0)


def head_kernel(d_ref, inv_ref, a):
    for s in range(16):
        for h in range(2):
            a[256 * h + 16 * s:256 * h + 16 * s + 16, :] = d_ref[s, h]
    inverse_factor512(a, inv_ref)


def second_kernel(mask_ref, d_ref, inv0_ref, c_ref, p_ref, u_ref, d10, a, inv1):
    for s in range(16):
        for h in range(2):
            o = 256 * h + 16 * s
            d10[o:o + 16, :] = d_ref[s, h, :, 0:512]
            a[o:o + 16, :] = d_ref[s, h, :, 512:1024]
    inv0 = inv0_ref[...]
    u10 = dot(d10[...], inv0, 1, 1).astype(BF16)
    a[...] = a[...] - dot16(u10, u10, 1, 1)
    p0 = dot(c_ref[:, 0:512], inv0, 1, 1)
    u0 = p0.astype(BF16)
    c1 = c_ref[:, 512:1024] - dot16(u0, u10, 1, 1)
    inverse_factor512(a, inv1)
    p1 = dot(c1, inv1[...], 1, 1)
    p_ref[:, 0:512] = p0
    p_ref[:, 512:1024] = jnp.where(mask_ref[0] > 0, p1, 0.0)
    u_ref[:, 0:512] = u0
    u_ref[:, 512:1024] = p1.astype(BF16)


def place_kernel(bulk_ref, panel_ref, y_ref, o_ref, p_ref):
    def one(slot, carry):
        b = bulk_ref[slot]
        col = pl.multiple_of(jnp.maximum(b, 0) * 128, 128)
        v = y_ref[:, pl.ds(col, 128)]
        out = pl.multiple_of((slot % 4) * 128, 128)
        o_ref[slot // 4, :, pl.ds(out, 128)] = jnp.where(b >= 0, v, 0.0)
        return carry

    lax.fori_loop(0, 64, one, 0)
    for m in range(4):
        b = panel_ref[m]
        col = pl.multiple_of(jnp.maximum(b, 0) * 128, 128)
        p_ref[:, 128 * m:128 * m + 128] = jnp.where(b >= 0, y_ref[:, pl.ds(col, 128)], 0.0)


def select_kernel(idx_ref, u_ref, o_ref):
    for i in range(8):
        b = idx_ref[i]
        v = u_ref[jnp.maximum(b, 0) + 8]
        o_ref[i] = jnp.where(b >= 0, v, jnp.zeros_like(v))


def schur_kernel(rows_ref, panel_ref, u_ref, ucol_ref, f_ref, fp_ref, own_ref, other_ref, z_ref, t_ref):
    upan = jnp.concatenate([ucol_ref[q, 4 + m] for m in range(4) for q in range(4)], axis=0)
    ubulk = jnp.concatenate([ucol_ref[q, j] for j in range(4) for q in range(4)], axis=0)

    def picked(ref, i):
        b = ref[i]
        u = u_ref[jnp.maximum(b, 0) + 8]
        f = fp_ref[jnp.maximum(b, 0) + 8]
        return jnp.where(b >= 0, u, jnp.zeros_like(u)), jnp.where(b >= 0, f, 0.0)

    for ref, out in ((panel_ref, t_ref), (rows_ref, z_ref)):
        us, fs = zip(*[picked(ref, i) for i in range(4)])
        out[...] = jnp.concatenate(fs, axis=0) - dot16(jnp.concatenate(us, axis=0), upan, 1, 1)
    rows = u_ref[8:32].reshape(768, 1024)
    s = f_ref[8:32].reshape(768, 512) - dot16(rows, ubulk, 1, 1)
    own_ref[...] = s[:, 0:256]
    other_ref[...] = s[:, 256:512]


def root_kernel(t_ref, inv_ref, a):
    for q in range(4):
        for m in range(4):
            a[128 * m + 32 * q:128 * m + 32 * q + 32, :] = t_ref[q, m]
    inverse_factor512(a, inv_ref)


def spread_kernel(mine_ref, theirs_ref, own_ref, got_ref, o_ref):
    def one(m, carry):
        i = mine_ref[m]
        j = theirs_ref[m]
        v = own_ref[jnp.maximum(i, 0)]
        w = got_ref[jnp.maximum(j, 0)]
        o_ref[m] = jnp.where(i >= 0, v, 0.0) + jnp.where(j >= 0, w, 0.0)
        return carry

    lax.fori_loop(0, 64, one, 0)


def last_kernel(flag_ref, panel_ref, inv_ref, cp_ref, root_ref, got_ref, p_ref, o_ref, ug, cps):
    step = pl.program_id(0)

    @pl.when(step == 0)
    def _():
        for q in range(4):
            for m in range(4):
                cps[128 * m + 32 * q:128 * m + 32 * q + 32, :] = cp_ref[q, m]
        v = dot(inv_ref[...], cps[...], 1, 0).astype(BF16)
        ug[...] = jnp.where(flag_ref[0] > 0, v, jnp.zeros_like(v))

    p = dot(panel_ref[...], inv_ref[...], 1, 1)
    p_ref[...] = p
    u = p.astype(BF16)
    u = jnp.where((flag_ref[1] > 0) | (step >= 2), u, jnp.zeros_like(u))
    upd = dot16(u, ug[...], 1, 0)
    for m in range(2):
        for q in range(4):
            o = 128 * m + 32 * q
            o_ref[o:o + 32, :] = root_ref[o:o + 32, :] + got_ref[q, m] - upd[o:o + 32, :]


def vmem():
    return pl.BlockSpec(memory_space=pltpu.VMEM)


def smem():
    return pl.BlockSpec(memory_space=pltpu.SMEM)


def call(kernel, outs, n_scalar, n_vector, scratch=(), flops=0, name=None):
    return pl.pallas_call(
        kernel,
        out_shape=outs,
        in_specs=[smem()] * n_scalar + [vmem()] * n_vector,
        out_specs=jax.tree.map(lambda _: vmem(), outs),
        scratch_shapes=list(scratch),
        compiler_params=VM,
        cost_estimate=pl.CostEstimate(flops=flops, transcendentals=0, bytes_accessed=1 << 20),
        name=name,
    )


def sds(shape, dtype=F32):
    return jax.ShapeDtypeStruct(shape, dtype)


def exchange(x, axis):
    return lax.all_to_all(x, axis, split_axis=0, concat_axis=0, tiled=True)


def gather(x, axis, n):
    return exchange(jnp.broadcast_to(x[None], (n,) + x.shape), axis)


def from_first_col(x, q):
    got = lax.ppermute(x, "col", [(0, 2)])
    x = jnp.where(q == 2, got, x)
    got = lax.ppermute(x, "col", [(0, 1), (2, 3)])
    return jnp.where(q % 2 == 1, got, x)


def swap_child(x):
    return lax.ppermute(x, "child", [(0, 1), (1, 0)])


def local(child_fronts, root_front, block_maps):
    front = child_fronts[0]
    child = lax.axis_index("child")
    r = lax.axis_index("row")
    q = lax.axis_index("col")
    blocks = jnp.arange(64, dtype=jnp.int32)
    order = jnp.arange(1, NCB + 1, dtype=jnp.int32)
    inverse = jnp.sum(jnp.where(block_maps[:, :, None] == blocks, order[None, :, None], 0), axis=1) - 1
    mine = jnp.where(child == 0, inverse[0], inverse[1])
    theirs = jnp.where(child == 0, inverse[1], inverse[0])

    def pick(idx):
        return jnp.sum(jnp.where(idx[:, None] == blocks[None, :], mine[None, :], 0), axis=1)

    slot = jnp.arange(64, dtype=jnp.int32)
    half = jnp.where(slot % 4 >= 2, 1 - child, child)
    bulk_idx = pick(32 * half + 2 * (slot // 4) + slot % 2)
    panel_idx = mine[0:4]
    four = jnp.arange(4, dtype=jnp.int32)
    col_idx = jnp.concatenate([pick(32 * jnp.where(four >= 2, 1 - child, child) + 2 * r + four % 2), panel_idx])
    row_idx = pick(16 * four + r)

    first = exchange(front[:, 0:512].reshape(16, 16, 512), "row")[0:2]
    first = from_first_col(first, q)
    d00 = gather(first, "row", ROWS)
    second = exchange(front.reshape(16, 16, 1024), "row")[2:4]
    second = from_first_col(second, q)
    d1 = gather(second, "row", ROWS)

    y = exchange(front.reshape(2, 4, 32, 1024).transpose(1, 0, 2, 3), "col").reshape(4, 64, 1024)
    wide = jnp.concatenate([y[1], y[2], y[3]], axis=1)
    placed, placed_panel = call(place_kernel, (sds((16, 64, 512)), sds((64, 512))), 2, 1, name="place")(
        bulk_idx, panel_idx, wide)
    f_bulk = exchange(placed, "row").reshape(32, 32, 512)
    f_panel = gather(placed_panel, "row", ROWS).reshape(32, 32, 512)

    raw_rows = exchange(root_front.reshape(16, 128, 256), "row")[0:2]
    raw_rows = jnp.where(child == 0, jnp.concatenate([raw_rows[0], raw_rows[1]], axis=1), 0.0)
    top = root_front[0:512].reshape(4, 4, 32, 256).transpose(1, 0, 2, 3)
    top = exchange(top, "col")[0].reshape(128, 256)
    at_left = jnp.where((child == 0) & (r == 0), top, 0.0)
    at_right = jnp.where((child == 0) & (r == 1), top, 0.0)
    raw_diag = lax.psum(jnp.concatenate([at_left, at_right], axis=1), "row")

    inv0 = call(head_kernel, sds((512, 512)), 0, 1, [pltpu.VMEM((512, 512), F32)], 2 * 10**10, "head")(d00)
    below = (r >= 2).astype(jnp.int32)[None]
    p, u = call(
        second_kernel, (sds((64, 1024)), sds((64, 1024), BF16)), 1, 3,
        [pltpu.VMEM((512, 512), F32)] * 3, 3 * 10**10, "second")(below, d1, inv0, y[0])
    child_factor = gather(p.reshape(2, 32, 1024), "col", COLS).transpose(1, 0, 2, 3).reshape(1, 256, 1024)
    u_all = gather(u.reshape(2, 32, 1024), "row", ROWS).reshape(32, 32, 1024)
    u_sel = call(select_kernel, sds((8, 32, 1024), BF16), 1, 1, name="select")(col_idx, u_all)
    u_col = gather(u_sel, "col", COLS)
    own, other, z, t = call(
        schur_kernel, (sds((768, 256)), sds((768, 256)), sds((128, 512)), sds((128, 512))), 2, 4,
        flops=3 * 10**9, name="schur")(row_idx, panel_idx, u_all, u_col, f_bulk, f_panel)

    t = t + raw_diag
    t = t + swap_child(t)
    t_all = gather(t.reshape(4, 32, 512), "col", COLS)
    inv_root = call(root_kernel, sds((512, 512)), 0, 1, [pltpu.VMEM((512, 512), F32)], 2 * 10**10, "root")(t_all)

    z = exchange(z.reshape(4, 32, 512), "col").reshape(128, 512) + raw_rows
    z = z + swap_child(z)
    panel = gather(z, "row", ROWS).reshape(2048, 512)

    got = swap_child(other)
    spread = call(spread_kernel, sds((64, 32, 256)), 2, 2, name="spread")(
        mine, theirs, own.reshape(24, 32, 256), got.reshape(24, 32, 256))
    head_cols = top.reshape(4, 32, 256) + spread[0:4]
    head_cols = gather(head_cols, "col", COLS)
    arrived = exchange(spread.reshape(4, 16, 32, 256), "col")

    flags = jnp.stack([16 * child + r >= 2, q > 0]).astype(jnp.int32)
    root_factor, trailing = pl.pallas_call(
        last_kernel,
        out_shape=(sds((2048, 512)), sds((2048, 256))),
        grid=(8,),
        in_specs=[
            smem(),
            pl.BlockSpec((256, 512), lambda i: (i, 0)),
            pl.BlockSpec((512, 512), lambda i: (0, 0)),
            pl.BlockSpec((4, 4, 32, 256), lambda i: (0, 0, 0, 0)),
            pl.BlockSpec((256, 256), lambda i: (i, 0)),
            pl.BlockSpec((4, 2, 32, 256), lambda i: (0, i, 0, 0)),
        ],
        out_specs=(pl.BlockSpec((256, 512), lambda i: (i, 0)), pl.BlockSpec((256, 256), lambda i: (i, 0))),
        scratch_shapes=[pltpu.VMEM((512, 256), BF16), pltpu.VMEM((512, 256), F32)],
        compiler_params=VM,
        name="last",
    )(flags, panel, inv_root, head_cols, root_front, arrived)
    return (child_factor, root_factor, trailing)


def solution(mesh):
    return jax.shard_map(
        local,
        mesh=mesh,
        in_specs=(P("child", "row", "col"), P("col", ("child", "row")), P()),
        out_specs=(P("child", "row", None), P("col", None), P("col", ("child", "row"))),
        check_vma=False,
    )
```

```python
import functools

import jax
import jax.numpy as jnp
from jax import lax
from jax.experimental import pallas as pl
from jax.experimental.pallas import tpu as pltpu
from jax.sharding import PartitionSpec as P

F32 = jnp.float32
BF16 = jnp.bfloat16
HI = lax.Precision.HIGHEST
ROWS, COLS = 16, 4
NCB = 24
VM = pltpu.CompilerParams(vmem_limit_bytes=56 << 20)


def lane_copy(v, k):
    return jnp.broadcast_to(v[:, k:k + 1], (8, 128))


def sub_copy(v, k):
    return jnp.broadcast_to(v[k:k + 1, :], (8, 128))


def dot(a, b, ca, cb):
    return lax.dot_general(a, b, (((ca,), (cb,)), ((), ())), precision=HI, preferred_element_type=F32)


def dot16(a, b, ca, cb):
    return lax.dot_general(a, b, (((ca,), (cb,)), ((), ())), preferred_element_type=F32)


def inverse_factor128(block):
    lane = lax.broadcasted_iota(jnp.int32, (8, 128), 1)
    sub = lax.broadcasted_iota(jnp.int32, (8, 128), 0)
    w = [block[8 * t:8 * t + 8, :] for t in range(16)]
    for s in range(16):
        c = {t: [lane_copy(w[t], 8 * s + j) for j in range(8)] for t in range(s, 16)}
        inside = (lane >= 8 * s) & (lane < 8 * s + 8)
        w[s] = jnp.where(inside, (lane - 8 * s == sub).astype(F32), w[s])
        for t in range(s + 1, 16):
            w[t] = jnp.where(inside, 0.0, w[t])
        for j in range(8):
            scale = lax.rsqrt(sub_copy(c[s][j], j))
            pivot_row = sub_copy(w[s], j) * scale
            ahead = {k: sub_copy(c[s][j], k) * scale for k in range(j + 1, 8)}
            for t in range(s, 16):
                l = c[t][j] * scale
                if t == s:
                    l = jnp.where(sub > j, l, 0.0)
                for k in range(j + 1, 8):
                    c[t][k] = c[t][k] - l * ahead[k]
                w[t] = w[t] - l * pivot_row
            w[s] = jnp.where(sub == j, pivot_row, w[s])
    return jnp.concatenate([jnp.where(lane <= sub + 8 * t, w[t], 0.0) for t in range(16)], axis=0)


def inverse_factor512(a, b, g):
    n = 512
    b[...] = jnp.zeros((n, n), F32)

    def block(k, carry):
        o = pl.multiple_of(128 * k, 128)
        g[...] = inverse_factor128(a[pl.ds(o, 128), pl.ds(o, 128)])
        for step in range(n // 128):
            pl.when(k == step)(functools.partial(outer, 128 * step))
        return carry

    def outer(o):
        inv = g[...]
        if o > 0:
            b[o:o + 128, 0:o] = dot(inv, b[o:o + 128, 0:o], 1, 0)
        b[o:o + 128, o:o + 128] = inv
        r = o + 128
        if r < n:
            l = dot(a[r:n, o:o + 128], inv, 1, 1)
            a[r:n, r:n] = a[r:n, r:n] - dot(l, l, 1, 1)
            b[r:n, 0:r] = b[r:n, 0:r] - dot(l, b[o:o + 128, 0:r], 1, 0)

    lax.fori_loop(0, n // 128, block, 0)


def head_kernel(d_ref, inv_ref, a, g):
    for s in range(16):
        for h in range(2):
            a[256 * h + 16 * s:256 * h + 16 * s + 16, :] = d_ref[s, h]
    inverse_factor512(a, inv_ref, g)


def second_kernel(mask_ref, d_ref, inv0_ref, c_ref, p_ref, u_ref, d10, a, inv1, g):
    for s in range(16):
        for h in range(2):
            o = 256 * h + 16 * s
            d10[o:o + 16, :] = d_ref[s, h, :, 0:512]
            a[o:o + 16, :] = d_ref[s, h, :, 512:1024]
    inv0 = inv0_ref[...]
    u10 = dot(d10[...], inv0, 1, 1).astype(BF16)
    a[...] = a[...] - dot16(u10, u10, 1, 1)
    p0 = dot(c_ref[:, 0:512], inv0, 1, 1)
    u0 = p0.astype(BF16)
    c1 = c_ref[:, 512:1024] - dot16(u0, u10, 1, 1)
    inverse_factor512(a, inv1, g)
    p1 = dot(c1, inv1[...], 1, 1)
    p_ref[:, 0:512] = p0
    p_ref[:, 512:1024] = jnp.where(mask_ref[0] > 0, p1, 0.0)
    u_ref[:, 0:512] = u0
    u_ref[:, 512:1024] = p1.astype(BF16)


def place_kernel(bulk_ref, panel_ref, y_ref, o_ref, p_ref):
    def one(slot, carry):
        b = bulk_ref[slot]
        col = pl.multiple_of(jnp.maximum(b, 0) * 128, 128)
        v = y_ref[:, pl.ds(col, 128)]
        out = pl.multiple_of((slot % 4) * 128, 128)
        o_ref[slot // 4, :, pl.ds(out, 128)] = jnp.where(b >= 0, v, 0.0)
        return carry

    lax.fori_loop(0, 64, one, 0)
    for m in range(4):
        b = panel_ref[m]
        col = pl.multiple_of(jnp.maximum(b, 0) * 128, 128)
        p_ref[:, 128 * m:128 * m + 128] = jnp.where(b >= 0, y_ref[:, pl.ds(col, 128)], 0.0)


def select_kernel(idx_ref, u_ref, o_ref):
    for i in range(8):
        b = idx_ref[i]
        v = u_ref[jnp.maximum(b, 0) + 8]
        o_ref[i] = jnp.where(b >= 0, v, jnp.zeros_like(v))


def schur_kernel(rows_ref, panel_ref, u_ref, ucol_ref, f_ref, fp_ref, own_ref, other_ref, z_ref, t_ref):
    upan = jnp.concatenate([ucol_ref[q, 4 + m] for m in range(4) for q in range(4)], axis=0)
    ubulk = jnp.concatenate([ucol_ref[q, j] for j in range(4) for q in range(4)], axis=0)

    def picked(ref, i):
        b = ref[i]
        u = u_ref[jnp.maximum(b, 0) + 8]
        f = fp_ref[jnp.maximum(b, 0) + 8]
        return jnp.where(b >= 0, u, jnp.zeros_like(u)), jnp.where(b >= 0, f, 0.0)

    for ref, out in ((panel_ref, t_ref), (rows_ref, z_ref)):
        us, fs = zip(*[picked(ref, i) for i in range(4)])
        out[...] = jnp.concatenate(fs, axis=0) - dot16(jnp.concatenate(us, axis=0), upan, 1, 1)
    rows = u_ref[8:32].reshape(768, 1024)
    s = f_ref[8:32].reshape(768, 512) - dot16(rows, ubulk, 1, 1)
    own_ref[...] = s[:, 0:256]
    other_ref[...] = s[:, 256:512]


def root_kernel(t_ref, inv_ref, a, g):
    for q in range(4):
        for m in range(4):
            a[128 * m + 32 * q:128 * m + 32 * q + 32, :] = t_ref[q, m]
    inverse_factor512(a, inv_ref, g)


def spread_kernel(mine_ref, theirs_ref, own_ref, got_ref, o_ref):
    def one(m, carry):
        i = mine_ref[m]
        j = theirs_ref[m]
        v = own_ref[jnp.maximum(i, 0)]
        w = got_ref[jnp.maximum(j, 0)]
        o_ref[m] = jnp.where(i >= 0, v, 0.0) + jnp.where(j >= 0, w, 0.0)
        return carry

    lax.fori_loop(0, 64, one, 0)


def last_kernel(flag_ref, panel_ref, inv_ref, cp_ref, root_ref, got_ref, p_ref, o_ref, ug, cps):
    step = pl.program_id(0)

    @pl.when(step == 0)
    def _():
        for q in range(4):
            for m in range(4):
                cps[128 * m + 32 * q:128 * m + 32 * q + 32, :] = cp_ref[q, m]
        v = dot(inv_ref[...], cps[...], 1, 0).astype(BF16)
        ug[...] = jnp.where(flag_ref[0] > 0, v, jnp.zeros_like(v))

    p = dot(panel_ref[...], inv_ref[...], 1, 1)
    p_ref[...] = p
    u = p.astype(BF16)
    u = jnp.where((flag_ref[1] > 0) | (step >= 2), u, jnp.zeros_like(u))
    upd = dot16(u, ug[...], 1, 0)
    for m in range(2):
        for q in range(4):
            o = 128 * m + 32 * q
            o_ref[o:o + 32, :] = root_ref[o:o + 32, :] + got_ref[q, m] - upd[o:o + 32, :]


def vmem():
    return pl.BlockSpec(memory_space=pltpu.VMEM)


def smem():
    return pl.BlockSpec(memory_space=pltpu.SMEM)


def call(kernel, outs, n_scalar, n_vector, scratch=(), flops=0, name=None):
    return pl.pallas_call(
        kernel,
        out_shape=outs,
        in_specs=[smem()] * n_scalar + [vmem()] * n_vector,
        out_specs=jax.tree.map(lambda _: vmem(), outs),
        scratch_shapes=list(scratch),
        compiler_params=VM,
        cost_estimate=pl.CostEstimate(flops=flops, transcendentals=0, bytes_accessed=1 << 20),
        name=name,
    )


def sds(shape, dtype=F32):
    return jax.ShapeDtypeStruct(shape, dtype)


CHOL = [pltpu.VMEM((512, 512), F32), pltpu.VMEM((128, 128), F32)]


def exchange(x, axis):
    return lax.all_to_all(x, axis, split_axis=0, concat_axis=0, tiled=True)


def gather(x, axis, n):
    return exchange(jnp.broadcast_to(x[None], (n,) + x.shape), axis)


def from_first_col(x, q):
    got = lax.ppermute(x, "col", [(0, 2)])
    x = jnp.where(q == 2, got, x)
    got = lax.ppermute(x, "col", [(0, 1), (2, 3)])
    return jnp.where(q % 2 == 1, got, x)


def in_order(own, near, far, corner, q):
    even = q % 2 == 0
    low = q < 2
    a0, a1 = jnp.where(even, own, near), jnp.where(even, near, own)
    b0, b1 = jnp.where(even, far, corner), jnp.where(even, corner, far)
    return jnp.stack([jnp.where(low, a0, b0), jnp.where(low, a1, b1), jnp.where(low, b0, a0), jnp.where(low, b1, a1)])


def across(x, k):
    return lax.ppermute(x, "col", [(i, i ^ k) for i in range(4)])


def gather_col(x, q):
    far = across(x, 2)
    near = across(jnp.stack([x, far]), 1)
    return in_order(x, near[0], far, near[1], q)


def exchange_col(x, q):
    parts = [lax.dynamic_index_in_dim(x, q ^ k, 0, keepdims=False) for k in range(4)]
    return in_order(parts[0], *[across(parts[k], k) for k in (1, 2, 3)], q)


def after(x, *earlier):
    return lax.optimization_barrier((x,) + earlier)[0]


def swap_child(x):
    return lax.ppermute(x, "child", [(0, 1), (1, 0)])


def local(child_fronts, root_front, block_maps):
    front = child_fronts[0]
    child = lax.axis_index("child")
    r = lax.axis_index("row")
    q = lax.axis_index("col")
    blocks = jnp.arange(64, dtype=jnp.int32)
    order = jnp.arange(1, NCB + 1, dtype=jnp.int32)
    inverse = jnp.sum(jnp.where(block_maps[:, :, None] == blocks, order[None, :, None], 0), axis=1) - 1
    mine = jnp.where(child == 0, inverse[0], inverse[1])
    theirs = jnp.where(child == 0, inverse[1], inverse[0])

    def pick(idx):
        return jnp.sum(jnp.where(idx[:, None] == blocks[None, :], mine[None, :], 0), axis=1)

    slot = jnp.arange(64, dtype=jnp.int32)
    half = jnp.where(slot % 4 >= 2, 1 - child, child)
    bulk_idx = pick(32 * half + 2 * (slot // 4) + slot % 2)
    panel_idx = mine[0:4]
    four = jnp.arange(4, dtype=jnp.int32)
    col_idx = jnp.concatenate([pick(32 * jnp.where(four >= 2, 1 - child, child) + 2 * r + four % 2), panel_idx])
    row_idx = pick(16 * four + r)

    heads = exchange(front.reshape(16, 16, 1024), "row")
    first = from_first_col(heads[0:2, :, 0:512], q)
    second = from_first_col(heads[2:4], q)
    second = jnp.broadcast_to(second[None], (ROWS,) + second.shape)
    d00 = gather(first, "row", ROWS)

    later = after(front, heads)
    y = exchange_col(later.reshape(2, 4, 32, 1024).transpose(1, 0, 2, 3), q).reshape(4, 64, 1024)
    d00, second = lax.optimization_barrier((d00, second))
    d1 = exchange(second, "row")

    inv0 = call(head_kernel, sds((512, 512)), 0, 1, CHOL, 2 * 10**10, "head")(d00)

    wide = after(jnp.concatenate([y[1], y[2], y[3]], axis=1), inv0)
    placed, placed_panel = call(place_kernel, (sds((16, 64, 512)), sds((64, 512))), 2, 1, name="place")(
        bulk_idx, panel_idx, wide)
    f_panel = lax.all_gather(placed_panel, "row").reshape(32, 32, 512)
    top = after(root_front[0:512], d00)
    raw_rows = 0.0
    for j in range(2):
        pairs = []
        for g in range(32):
            m = 2 * g + j
            pairs.append((4 * g, (m // 32 * 16 + m % 16) * 4 + m // 16))
        raw_rows += lax.ppermute(top[:, 128 * j:128 * j + 128], ("child", "row", "col"), pairs)
    top = exchange_col(top.reshape(4, 4, 32, 256).transpose(1, 0, 2, 3), q)[0].reshape(128, 256)
    d1, placed, top, raw_rows = lax.optimization_barrier((d1, placed, top, raw_rows))
    raw_rows = raw_rows.T
    f_bulk = exchange(placed, "row").reshape(32, 32, 512)

    below = (r >= 2).astype(jnp.int32)[None]
    p, u = call(
        second_kernel, (sds((64, 1024)), sds((64, 1024), BF16)), 1, 3,
        [pltpu.VMEM((512, 512), F32)] * 2 + CHOL, 3 * 10**10, "second")(below, d1, inv0, y[0])
    u, f_bulk = lax.optimization_barrier((u, f_bulk))
    u_all = gather(u.reshape(2, 32, 1024), "row", ROWS).reshape(32, 32, 1024)
    u_sel = call(select_kernel, sds((8, 32, 1024), BF16), 1, 1, name="select")(col_idx, u_all)
    raw_diag = exchange(after(top, u_sel).reshape(16, 8, 256), "row")[0:2]
    raw_diag = gather(raw_diag, "row", ROWS).transpose(0, 2, 1, 3).reshape(128, 512)
    raw_diag = jnp.where(child == 0, raw_diag, 0.0)
    u_far, raw_diag = lax.optimization_barrier((across(u_sel, 2), raw_diag))
    u_near = across(jnp.stack([u_sel, u_far]), 1)
    u_col = in_order(u_sel, u_near[0], u_far, u_near[1], q)
    own, other, z, t = call(
        schur_kernel, (sds((768, 256)), sds((768, 256)), sds((128, 512)), sds((128, 512))), 2, 4,
        flops=3 * 10**9, name="schur")(row_idx, panel_idx, u_all, u_col, f_bulk, f_panel)

    t = t + raw_diag
    t = t + swap_child(t)
    t_all = gather_col(t.reshape(4, 32, 512), q)

    z = exchange_col(z.reshape(4, 32, 512), q).reshape(128, 512) + raw_rows
    z = z + swap_child(z)
    z = jnp.broadcast_to(z[None], (ROWS,) + z.shape)

    got = swap_child(other)
    spread = call(spread_kernel, sds((64, 32, 256)), 2, 2, name="spread")(
        mine, theirs, own.reshape(24, 32, 256), got.reshape(24, 32, 256))
    t_all, spread, z = lax.optimization_barrier((t_all, spread, z))
    panel = exchange(z, "row").reshape(2048, 512)
    arrived = exchange_col(spread.reshape(4, 16, 32, 256), q)
    inv_root = call(root_kernel, sds((512, 512)), 0, 1, CHOL, 2 * 10**10, "root")(t_all)
    head_cols = top.reshape(4, 32, 256) + spread[0:4]
    head_cols = gather_col(head_cols, q)
    child_factor = gather_col(after(p, t_all).reshape(2, 32, 1024), q).transpose(1, 0, 2, 3).reshape(1, 256, 1024)

    flags = jnp.stack([16 * child + r >= 2, q > 0]).astype(jnp.int32)
    root_factor, trailing = pl.pallas_call(
        last_kernel,
        out_shape=(sds((2048, 512)), sds((2048, 256))),
        grid=(8,),
        in_specs=[
            smem(),
            pl.BlockSpec((256, 512), lambda i: (i, 0)),
            pl.BlockSpec((512, 512), lambda i: (0, 0)),
            pl.BlockSpec((4, 4, 32, 256), lambda i: (0, 0, 0, 0)),
            pl.BlockSpec((256, 256), lambda i: (i, 0)),
            pl.BlockSpec((4, 2, 32, 256), lambda i: (0, i, 0, 0)),
        ],
        out_specs=(pl.BlockSpec((256, 512), lambda i: (i, 0)), pl.BlockSpec((256, 256), lambda i: (i, 0))),
        scratch_shapes=[pltpu.VMEM((512, 256), BF16), pltpu.VMEM((512, 256), F32)],
        compiler_params=VM,
        name="last",
    )(flags, panel, inv_root, head_cols, root_front, arrived)
    return (child_factor, root_factor, trailing)


def solution(mesh):
    return jax.shard_map(
        local,
        mesh=mesh,
        in_specs=(P("child", "row", "col"), P("col", ("child", "row")), P()),
        out_specs=(P("child", "row", None), P("col", None), P("col", ("child", "row"))),
        check_vma=False,
    )
```

```python
import functools

import jax
import jax.numpy as jnp
from jax import lax
from jax.experimental import pallas as pl
from jax.experimental.pallas import tpu as pltpu
from jax.sharding import PartitionSpec as P

F32 = jnp.float32
BF16 = jnp.bfloat16
HI = lax.Precision.HIGHEST
ROWS, COLS = 16, 4
NCB = 24
VM = pltpu.CompilerParams(vmem_limit_bytes=56 << 20)


def lane_copy(v, k):
    return jnp.broadcast_to(v[:, k:k + 1], (8, 128))


def sub_copy(v, k):
    return jnp.broadcast_to(v[k:k + 1, :], (8, 128))


def dot(a, b, ca, cb):
    return lax.dot_general(a, b, (((ca,), (cb,)), ((), ())), precision=HI, preferred_element_type=F32)


def dot16(a, b, ca, cb):
    return lax.dot_general(a, b, (((ca,), (cb,)), ((), ())), preferred_element_type=F32)


def inverse_factor128(block):
    lane = lax.broadcasted_iota(jnp.int32, (8, 128), 1)
    sub = lax.broadcasted_iota(jnp.int32, (8, 128), 0)
    w = [block[8 * t:8 * t + 8, :] for t in range(16)]
    for s in range(16):
        c = {t: [lane_copy(w[t], 8 * s + j) for j in range(8)] for t in range(s, 16)}
        inside = (lane >= 8 * s) & (lane < 8 * s + 8)
        w[s] = jnp.where(inside, (lane - 8 * s == sub).astype(F32), w[s])
        for t in range(s + 1, 16):
            w[t] = jnp.where(inside, 0.0, w[t])
        for j in range(8):
            scale = lax.rsqrt(sub_copy(c[s][j], j))
            pivot_row = sub_copy(w[s], j) * scale
            ahead = {k: sub_copy(c[s][j], k) * scale for k in range(j + 1, 8)}
            for t in range(s, 16):
                l = c[t][j] * scale
                if t == s:
                    l = jnp.where(sub > j, l, 0.0)
                for k in range(j + 1, 8):
                    c[t][k] = c[t][k] - l * ahead[k]
                w[t] = w[t] - l * pivot_row
            w[s] = jnp.where(sub == j, pivot_row, w[s])
    return jnp.concatenate([jnp.where(lane <= sub + 8 * t, w[t], 0.0) for t in range(16)], axis=0)


def inverse_factor512(a, b, g):
    n = 512
    b[...] = jnp.zeros((n, n), F32)

    def block(k, carry):
        o = pl.multiple_of(128 * k, 128)
        g[...] = inverse_factor128(a[pl.ds(o, 128), pl.ds(o, 128)])
        for step in range(n // 128):
            pl.when(k == step)(functools.partial(outer, 128 * step))
        return carry

    def outer(o):
        inv = g[...]
        if o > 0:
            b[o:o + 128, 0:o] = dot(inv, b[o:o + 128, 0:o], 1, 0)
        b[o:o + 128, o:o + 128] = inv
        r = o + 128
        if r < n:
            l = dot(a[r:n, o:o + 128], inv, 1, 1)
            a[r:n, r:n] = a[r:n, r:n] - dot(l, l, 1, 1)
            b[r:n, 0:r] = b[r:n, 0:r] - dot(l, b[o:o + 128, 0:r], 1, 0)

    lax.fori_loop(0, n // 128, block, 0)


def head_rows():
    for q in range(4):
        for s in range(16):
            for h in range(2):
                yield 256 * h + 128 * (s // 8) + 32 * q + 4 * (s % 8), (q, s, h)


def head_kernel(d_ref, inv_ref, a, g):
    for o, piece in head_rows():
        a[o:o + 4, :] = d_ref[piece]
    inverse_factor512(a, inv_ref, g)


def second_kernel(mask_ref, d_ref, inv0_ref, c_ref, p_ref, u_ref, d10, inv1, a, g):
    for o, (q, s, h) in head_rows():
        d10[o:o + 4, :] = d_ref[q, s, h, :, 0:512]
        a[o:o + 4, :] = d_ref[q, s, h, :, 512:1024]
    inv0 = inv0_ref[...]
    u10 = dot(d10[...], inv0, 1, 1).astype(BF16)
    a[...] = a[...] - dot16(u10, u10, 1, 1)
    p0 = dot(c_ref[:, 0:512], inv0, 1, 1)
    u0 = p0.astype(BF16)
    c1 = c_ref[:, 512:1024] - dot16(u0, u10, 1, 1)
    inverse_factor512(a, inv1, g)
    p1 = dot(c1, inv1[...], 1, 1)
    p_ref[:, 0:512] = p0
    p_ref[:, 512:1024] = jnp.where(mask_ref[0] > 0, p1, 0.0)
    u_ref[:, 0:512] = u0
    u_ref[:, 512:1024] = p1.astype(BF16)


def place_kernel(bulk_ref, panel_ref, y_ref, o_ref, p_ref):
    def one(slot, carry):
        b = bulk_ref[slot]
        col = pl.multiple_of(jnp.maximum(b, 0) * 128, 128)
        v = y_ref[:, pl.ds(col, 128)]
        out = pl.multiple_of((slot % 4) * 128, 128)
        o_ref[slot // 4, :, pl.ds(out, 128)] = jnp.where(b >= 0, v, 0.0)
        return carry

    lax.fori_loop(0, 64, one, 0)
    for m in range(4):
        b = panel_ref[m]
        col = pl.multiple_of(jnp.maximum(b, 0) * 128, 128)
        p_ref[:, 128 * m:128 * m + 128] = jnp.where(b >= 0, y_ref[:, pl.ds(col, 128)], 0.0)


def select_kernel(panel_ref, bulk_ref, u_ref, p_ref, o_ref):
    for ref, out in ((panel_ref, p_ref), (bulk_ref, o_ref)):
        for i in range(4):
            b = ref[i]
            v = u_ref[jnp.maximum(b, 0) + 8]
            out[i] = jnp.where(b >= 0, v, jnp.zeros_like(v))


def panel_kernel(rows_ref, panel_ref, u_ref, ucol_ref, fp_ref, z_ref, t_ref):
    upan = jnp.concatenate([ucol_ref[q, m] for m in range(4) for q in range(4)], axis=0)

    def picked(ref, i):
        b = ref[i]
        u = u_ref[jnp.maximum(b, 0) + 8]
        f = fp_ref[jnp.maximum(b, 0) + 8]
        return jnp.where(b >= 0, u, jnp.zeros_like(u)), jnp.where(b >= 0, f, 0.0)

    for ref, out in ((panel_ref, t_ref), (rows_ref, z_ref)):
        us, fs = zip(*[picked(ref, i) for i in range(4)])
        out[...] = jnp.concatenate(fs, axis=0) - dot16(jnp.concatenate(us, axis=0), upan, 1, 1)


def bulk_kernel(u_ref, ucol_ref, f_ref, own_ref, other_ref):
    ubulk = jnp.concatenate([ucol_ref[q, j] for j in range(4) for q in range(4)], axis=0)
    rows = u_ref[8:32].reshape(768, 1024)
    s = f_ref[8:32].reshape(768, 512) - dot16(rows, ubulk, 1, 1)
    own_ref[...] = s[:, 0:256]
    other_ref[...] = s[:, 256:512]


def root_kernel(t_ref, inv_ref, a, g):
    for q in range(4):
        for m in range(4):
            a[128 * m + 32 * q:128 * m + 32 * q + 32, :] = t_ref[q, m]
    inverse_factor512(a, inv_ref, g)


def spread_kernel(mine_ref, theirs_ref, own_ref, got_ref, o_ref):
    def one(m, carry):
        i = mine_ref[m]
        j = theirs_ref[m]
        v = own_ref[jnp.maximum(i, 0)]
        w = got_ref[jnp.maximum(j, 0)]
        o_ref[m] = jnp.where(i >= 0, v, 0.0) + jnp.where(j >= 0, w, 0.0)
        return carry

    lax.fori_loop(0, 64, one, 0)


def last_kernel(flag_ref, panel_ref, inv_ref, cp_ref, root_ref, got_ref, p_ref, o_ref, ug, cps):
    step = pl.program_id(0)

    @pl.when(step == 0)
    def _():
        for q in range(4):
            for m in range(4):
                cps[128 * m + 32 * q:128 * m + 32 * q + 32, :] = cp_ref[q, m]
        v = dot(inv_ref[...], cps[...], 1, 0).astype(BF16)
        ug[...] = jnp.where(flag_ref[0] > 0, v, jnp.zeros_like(v))

    p = dot(panel_ref[...], inv_ref[...], 1, 1)
    p_ref[...] = p
    u = p.astype(BF16)
    u = jnp.where((flag_ref[1] > 0) | (step >= 2), u, jnp.zeros_like(u))
    upd = dot16(u, ug[...], 1, 0)
    for m in range(2):
        for q in range(4):
            o = 128 * m + 32 * q
            o_ref[o:o + 32, :] = root_ref[o:o + 32, :] + got_ref[q, m] - upd[o:o + 32, :]


def vmem():
    return pl.BlockSpec(memory_space=pltpu.VMEM)


def smem():
    return pl.BlockSpec(memory_space=pltpu.SMEM)


def call(kernel, outs, n_scalar, n_vector, scratch=(), flops=0, name=None):
    return pl.pallas_call(
        kernel,
        out_shape=outs,
        in_specs=[smem()] * n_scalar + [vmem()] * n_vector,
        out_specs=jax.tree.map(lambda _: vmem(), outs),
        scratch_shapes=list(scratch),
        compiler_params=VM,
        cost_estimate=pl.CostEstimate(flops=flops, transcendentals=0, bytes_accessed=1 << 20),
        name=name,
    )


def sds(shape, dtype=F32):
    return jax.ShapeDtypeStruct(shape, dtype)


CHOL = [pltpu.VMEM((512, 512), F32), pltpu.VMEM((128, 128), F32)]


def exchange(x, axis):
    return lax.all_to_all(x, axis, split_axis=0, concat_axis=0, tiled=True)


def gather(x, axis, n):
    return exchange(jnp.broadcast_to(x[None], (n,) + x.shape), axis)


def in_order(own, near, far, corner, q):
    even = q % 2 == 0
    low = q < 2
    a0, a1 = jnp.where(even, own, near), jnp.where(even, near, own)
    b0, b1 = jnp.where(even, far, corner), jnp.where(even, corner, far)
    return jnp.stack([jnp.where(low, a0, b0), jnp.where(low, a1, b1), jnp.where(low, b0, a0), jnp.where(low, b1, a1)])


def across(x, k):
    return lax.ppermute(x, "col", [(i, i ^ k) for i in range(4)])


def gather_col(x, q, hold=None, far=None):
    if far is None:
        far = across(x, 2)
    pair = jnp.stack([x, far])
    near = across(pair if hold is None else after(pair, hold), 1)
    return in_order(x, near[0], far, near[1], q)


def exchange_col(x, q):
    parts = [lax.dynamic_index_in_dim(x, q ^ k, 0, keepdims=False) for k in range(4)]
    return in_order(parts[0], *[across(parts[k], k) for k in (1, 2, 3)], q)


def after(x, *earlier):
    return lax.optimization_barrier((x,) + earlier)[0]


def swap_child(x):
    return lax.ppermute(x, "child", [(0, 1), (1, 0)])


def local(child_fronts, root_front, block_maps):
    front = child_fronts[0]
    child = lax.axis_index("child")
    r = lax.axis_index("row")
    q = lax.axis_index("col")
    blocks = jnp.arange(64, dtype=jnp.int32)
    order = jnp.arange(1, NCB + 1, dtype=jnp.int32)
    inverse = jnp.sum(jnp.where(block_maps[:, :, None] == blocks, order[None, :, None], 0), axis=1) - 1
    mine = jnp.where(child == 0, inverse[0], inverse[1])
    theirs = jnp.where(child == 0, inverse[1], inverse[0])

    def pick(idx):
        return jnp.sum(jnp.where(idx[:, None] == blocks[None, :], mine[None, :], 0), axis=1)

    slot = jnp.arange(64, dtype=jnp.int32)
    half = jnp.where(slot % 4 >= 2, 1 - child, child)
    bulk_idx = pick(32 * half + 2 * (slot // 4) + slot % 2)
    panel_idx = mine[0:4]
    four = jnp.arange(4, dtype=jnp.int32)
    col_idx = pick(32 * jnp.where(four >= 2, 1 - child, child) + 2 * r + four % 2)
    row_idx = pick(16 * four + r)

    quarters = root_front[0:512].reshape(4, 4, 32, 256).transpose(1, 0, 2, 3).reshape(4, 2, 64, 256)
    pack = jnp.concatenate([
        front.reshape(2, 4, 32, 1024).transpose(1, 0, 2, 3).reshape(4, 64, 1024), quarters[:, 0], quarters[:, 1],
    ], axis=2)
    sent = [lax.ppermute(pack[k], "col", [(0, k)]) for k in (1, 2, 3)]
    pack = jnp.where(q == 0, pack[0], sent[0] + sent[1] + sent[2])
    columns = pack[:, 0:1024]
    top = jnp.concatenate([pack[:, 1024:1280], pack[:, 1280:1536]], axis=0)

    heads = exchange(pack.reshape(16, 4, 1536), "row")
    d00 = gather(heads[0:2, :, 0:512], "row", ROWS)
    later = after(front, heads)
    y = exchange_col(later.reshape(2, 4, 32, 1024).transpose(1, 0, 2, 3), q).reshape(4, 64, 1024)
    lower, corner = lax.optimization_barrier((heads[2:4, :, 0:1024], heads[0:2, :, 1024:1536]))
    second = gather(jnp.concatenate([lower, corner], axis=2), "row", ROWS)
    d00 = gather_col(d00, q)
    d1 = second[:, :, :, 0:1024]
    raw_diag = jnp.concatenate([
        jnp.concatenate([second[:, h, :, c:c + 256] for h in range(2)], axis=2).reshape(64, 512) for c in (1024, 1280)
    ], axis=0)
    raw_diag = jnp.where(child == 0, raw_diag, 0.0)
    d00, d1 = lax.optimization_barrier((d00, d1))

    inv0 = call(head_kernel, sds((512, 512)), 0, 1, CHOL, 2 * 10**10, "head")(d00)
    d1 = gather_col(d1, q, inv0)

    wide = after(jnp.concatenate([y[1], y[2], y[3]], axis=1), inv0)
    placed, placed_panel = call(place_kernel, (sds((16, 64, 512)), sds((64, 512))), 2, 1, name="place")(
        bulk_idx, panel_idx, wide)
    f_panel = lax.all_gather(placed_panel, "row").reshape(32, 32, 512)
    raw_rows = 0.0
    tile_top = after(root_front[0:512], d00)
    for j in range(2):
        pairs = []
        for g in range(32):
            m = 2 * g + j
            pairs.append((4 * g, (m // 32 * 16 + m % 16) * 4 + m // 16))
        raw_rows += lax.ppermute(tile_top[:, 128 * j:128 * j + 128], ("child", "row", "col"), pairs)
    d1, placed = lax.optimization_barrier((d1, placed))
    f_bulk = exchange(placed, "row").reshape(32, 32, 512)

    below = (r >= 2).astype(jnp.int32)[None]
    p, u = call(
        second_kernel, (sds((64, 1024)), sds((64, 1024), BF16)), 1, 3,
        [pltpu.VMEM((512, 512), F32)] * 2 + CHOL, 3 * 10**10, "second")(below, d1, inv0, columns)
    u, f_bulk, raw_rows = lax.optimization_barrier((u, f_bulk, raw_rows))
    raw_rows = raw_rows.T
    u_all = gather(u.reshape(2, 32, 1024), "row", ROWS).reshape(32, 32, 1024)
    some = sds((4, 32, 1024), BF16)
    u_panel, u_bulk = call(select_kernel, (some, some), 2, 1, name="select")(panel_idx, col_idx, u_all)
    far = across(u_panel, 2)
    bulk_far = across(after(u_bulk, far), 2)
    u_panel, bulk_far = lax.optimization_barrier((gather_col(u_panel, q, None, far), bulk_far))
    z, t = call(panel_kernel, (sds((128, 512)), sds((128, 512))), 2, 3, flops=10**9, name="panel")(
        row_idx, panel_idx, u_all, u_panel, f_panel)

    t = t + raw_diag
    t = t + swap_child(t)
    z = exchange_col(z.reshape(4, 32, 512), q).reshape(128, 512) + raw_rows
    z = after(z, t)
    z_swapped = swap_child(z)
    z = z + z_swapped
    t_all = gather_col(t.reshape(4, 32, 512), q)
    panel = lax.all_gather(z, "row", tiled=True)

    own, other = call(bulk_kernel, (sds((768, 256)), sds((768, 256))), 0, 3, flops=2 * 10**9, name="bulk")(
        u_all, gather_col(u_bulk, q, None, bulk_far), f_bulk)
    got = swap_child(after(other, z_swapped))
    t_all, z = lax.optimization_barrier((t_all, z))
    inv_root = call(root_kernel, sds((512, 512)), 0, 1, CHOL, 2 * 10**10, "root")(t_all)
    spread = call(spread_kernel, sds((64, 32, 256)), 2, 2, name="spread")(
        mine, theirs, own.reshape(24, 32, 256), got.reshape(24, 32, 256))
    arrived = exchange_col(spread.reshape(4, 16, 32, 256), q)
    head_cols = gather_col(top.reshape(4, 32, 256) + spread[0:4], q)
    child_factor = gather_col(after(p, t_all).reshape(2, 32, 1024), q).transpose(1, 0, 2, 3).reshape(1, 256, 1024)

    flags = jnp.stack([16 * child + r >= 2, q > 0]).astype(jnp.int32)
    root_factor, trailing = pl.pallas_call(
        last_kernel,
        out_shape=(sds((2048, 512)), sds((2048, 256))),
        grid=(8,),
        in_specs=[
            smem(),
            pl.BlockSpec((256, 512), lambda i: (i, 0)),
            pl.BlockSpec((512, 512), lambda i: (0, 0)),
            pl.BlockSpec((4, 4, 32, 256), lambda i: (0, 0, 0, 0)),
            pl.BlockSpec((256, 256), lambda i: (i, 0)),
            pl.BlockSpec((4, 2, 32, 256), lambda i: (0, i, 0, 0)),
        ],
        out_specs=(pl.BlockSpec((256, 512), lambda i: (i, 0)), pl.BlockSpec((256, 256), lambda i: (i, 0))),
        scratch_shapes=[pltpu.VMEM((512, 256), BF16), pltpu.VMEM((512, 256), F32)],
        compiler_params=VM,
        name="last",
    )(flags, panel, inv_root, head_cols, root_front, arrived)
    return (child_factor, root_factor, trailing)


def solution(mesh):
    return jax.shard_map(
        local,
        mesh=mesh,
        in_specs=(P("child", "row", "col"), P("col", ("child", "row")), P()),
        out_specs=(P("child", "row", None), P("col", None), P("col", ("child", "row"))),
        check_vma=False,
    )
```

```python
import functools

import jax
import jax.numpy as jnp
from jax import lax
from jax.experimental import pallas as pl
from jax.experimental.pallas import tpu as pltpu
from jax.sharding import PartitionSpec as P

F32 = jnp.float32
BF16 = jnp.bfloat16
HI = lax.Precision.HIGHEST
ROWS, COLS = 16, 4
NCB = 24
VM = pltpu.CompilerParams(vmem_limit_bytes=56 << 20)


def lane_copy(v, k):
    return jnp.broadcast_to(v[:, k:k + 1], (8, 128))


def sub_copy(v, k):
    return jnp.broadcast_to(v[k:k + 1, :], (8, 128))


def dot(a, b, ca, cb):
    return lax.dot_general(a, b, (((ca,), (cb,)), ((), ())), precision=HI, preferred_element_type=F32)


def dot16(a, b, ca, cb):
    return lax.dot_general(a, b, (((ca,), (cb,)), ((), ())), preferred_element_type=F32)


def inverse_factor128(block):
    lane = lax.broadcasted_iota(jnp.int32, (8, 128), 1)
    sub = lax.broadcasted_iota(jnp.int32, (8, 128), 0)
    w = [block[8 * t:8 * t + 8, :] for t in range(16)]
    for s in range(16):
        c = {t: [lane_copy(w[t], 8 * s + j) for j in range(8)] for t in range(s, 16)}
        inside = (lane >= 8 * s) & (lane < 8 * s + 8)
        w[s] = jnp.where(inside, (lane - 8 * s == sub).astype(F32), w[s])
        for t in range(s + 1, 16):
            w[t] = jnp.where(inside, 0.0, w[t])
        for j in range(8):
            scale = lax.rsqrt(sub_copy(c[s][j], j))
            pivot_row = sub_copy(w[s], j) * scale
            ahead = {k: sub_copy(c[s][j], k) * scale for k in range(j + 1, 8)}
            for t in range(s, 16):
                l = c[t][j] * scale
                if t == s:
                    l = jnp.where(sub > j, l, 0.0)
                for k in range(j + 1, 8):
                    c[t][k] = c[t][k] - l * ahead[k]
                w[t] = w[t] - l * pivot_row
            w[s] = jnp.where(sub == j, pivot_row, w[s])
    return jnp.concatenate([jnp.where(lane <= sub + 8 * t, w[t], 0.0) for t in range(16)], axis=0)


def inverse_factor512(a, b, g):
    n = 512
    b[...] = jnp.zeros((n, n), F32)

    def block(k, carry):
        o = pl.multiple_of(128 * k, 128)
        g[...] = inverse_factor128(a[pl.ds(o, 128), pl.ds(o, 128)])
        for step in range(n // 128):
            pl.when(k == step)(functools.partial(outer, 128 * step))
        return carry

    def outer(o):
        inv = g[...]
        if o > 0:
            b[o:o + 128, 0:o] = dot(inv, b[o:o + 128, 0:o], 1, 0)
        b[o:o + 128, o:o + 128] = inv
        r = o + 128
        if r < n:
            l = dot(a[r:n, o:o + 128], inv, 1, 1)
            a[r:n, r:n] = a[r:n, r:n] - dot(l, l, 1, 1)
            b[r:n, 0:r] = b[r:n, 0:r] - dot(l, b[o:o + 128, 0:r], 1, 0)

    lax.fori_loop(0, n // 128, block, 0)


def head_rows():
    for q in range(4):
        for s in range(16):
            for h in range(2):
                yield 256 * h + 128 * (s // 8) + 32 * q + 4 * (s % 8), (q, s, h)


def head_kernel(d_ref, c_ref, inv_ref, p_ref, u_ref, a, g):
    for o, piece in head_rows():
        a[o:o + 4, :] = d_ref[piece]
    inverse_factor512(a, inv_ref, g)
    p = dot(c_ref[...], inv_ref[...], 1, 1)
    p_ref[...] = p
    u_ref[...] = p.astype(BF16)


def second_kernel(mask_ref, d_ref, inv0_ref, c_ref, u0_ref, p_ref, u_ref, d10, inv1, a, g):
    for o, (q, s, h) in head_rows():
        d10[o:o + 4, :] = d_ref[q, s, h, :, 0:512]
        a[o:o + 4, :] = d_ref[q, s, h, :, 512:1024]
    u10 = dot(d10[...], inv0_ref[...], 1, 1).astype(BF16)
    a[...] = a[...] - dot16(u10, u10, 1, 1)
    c1 = c_ref[...] - dot16(u0_ref[...], u10, 1, 1)
    inverse_factor512(a, inv1, g)
    p1 = dot(c1, inv1[...], 1, 1)
    p_ref[...] = jnp.where(mask_ref[0] > 0, p1, 0.0)
    u_ref[...] = p1.astype(BF16)


def place(b, y_ref):
    col = pl.multiple_of(jnp.maximum(b, 0) * 128, 128)
    return jnp.where(b >= 0, y_ref[:, pl.ds(col, 128)], 0.0)


def place_panel_kernel(panel_ref, y_ref, p_ref):
    for m in range(4):
        p_ref[:, 128 * m:128 * m + 128] = place(panel_ref[m], y_ref)


def place_kernel(bulk_ref, y_ref, o_ref):
    def one(slot, carry):
        out = pl.multiple_of((slot % 4) * 128, 128)
        o_ref[slot // 4, :, pl.ds(out, 128)] = place(bulk_ref[slot], y_ref)
        return carry

    lax.fori_loop(0, 64, one, 0)


def picked(b, ref):
    v = ref[jnp.maximum(b, 0) + 8]
    return jnp.where(b >= 0, v, jnp.zeros_like(v))


def select_kernel(panel_ref, bulk_ref, u0_ref, u1_ref, p_ref, o_ref):
    for ref, out in ((panel_ref, p_ref), (bulk_ref, o_ref)):
        for i in range(4):
            out[i, :, 0:512] = picked(ref[i], u0_ref)
            out[i, :, 512:1024] = picked(ref[i], u1_ref)


def panel_kernel(rows_ref, panel_ref, u0_ref, u1_ref, ucol_ref, fp_ref, z_ref, t_ref):
    upan = jnp.concatenate([ucol_ref[q, m] for m in range(4) for q in range(4)], axis=0)
    for ref, out in ((panel_ref, t_ref), (rows_ref, z_ref)):
        f, u0, u1 = [jnp.concatenate([picked(ref[i], x) for i in range(4)], axis=0) for x in (fp_ref, u0_ref, u1_ref)]
        out[...] = f - dot16(jnp.concatenate([u0, u1], axis=1), upan, 1, 1)


def bulk_kernel(u0_ref, u1_ref, ucol_ref, f_ref, own_ref, other_ref):
    ubulk = jnp.concatenate([ucol_ref[q, j] for j in range(4) for q in range(4)], axis=0)
    rows = jnp.concatenate([u0_ref[8:32].reshape(768, 512), u1_ref[8:32].reshape(768, 512)], axis=1)
    s = f_ref[8:32].reshape(768, 512) - dot16(rows, ubulk, 1, 1)
    own_ref[...] = s[:, 0:256]
    other_ref[...] = s[:, 256:512]


def root_kernel(t_ref, inv_ref, a, g):
    for q in range(4):
        for m in range(4):
            a[128 * m + 32 * q:128 * m + 32 * q + 32, :] = t_ref[q, m]
    inverse_factor512(a, inv_ref, g)


def spread_kernel(mine_ref, theirs_ref, own_ref, got_ref, o_ref):
    def one(m, carry):
        i = mine_ref[m]
        j = theirs_ref[m]
        v = own_ref[jnp.maximum(i, 0)]
        w = got_ref[jnp.maximum(j, 0)]
        o_ref[m] = jnp.where(i >= 0, v, 0.0) + jnp.where(j >= 0, w, 0.0)
        return carry

    lax.fori_loop(0, 64, one, 0)


def last_kernel(flag_ref, panel_ref, inv_ref, cp_ref, root_ref, got_ref, p_ref, o_ref, ug, cps):
    step = pl.program_id(0)

    @pl.when(step == 0)
    def _():
        for q in range(4):
            for m in range(4):
                cps[128 * m + 32 * q:128 * m + 32 * q + 32, :] = cp_ref[q, m]
        v = dot(inv_ref[...], cps[...], 1, 0).astype(BF16)
        ug[...] = jnp.where(flag_ref[0] > 0, v, jnp.zeros_like(v))

    p = dot(panel_ref[...], inv_ref[...], 1, 1)
    p_ref[...] = p
    u = p.astype(BF16)
    u = jnp.where((flag_ref[1] > 0) | (step >= 2), u, jnp.zeros_like(u))
    upd = dot16(u, ug[...], 1, 0)
    for m in range(2):
        for q in range(4):
            o = 128 * m + 32 * q
            o_ref[o:o + 32, :] = root_ref[o:o + 32, :] + got_ref[q, m] - upd[o:o + 32, :]


def vmem():
    return pl.BlockSpec(memory_space=pltpu.VMEM)


def smem():
    return pl.BlockSpec(memory_space=pltpu.SMEM)


def call(kernel, outs, n_scalar, n_vector, scratch=(), flops=0, name=None):
    return pl.pallas_call(
        kernel,
        out_shape=outs,
        in_specs=[smem()] * n_scalar + [vmem()] * n_vector,
        out_specs=jax.tree.map(lambda _: vmem(), outs),
        scratch_shapes=list(scratch),
        compiler_params=VM,
        cost_estimate=pl.CostEstimate(flops=flops, transcendentals=0, bytes_accessed=1 << 20),
        name=name,
    )


def sds(shape, dtype=F32):
    return jax.ShapeDtypeStruct(shape, dtype)


CHOL = [pltpu.VMEM((512, 512), F32), pltpu.VMEM((128, 128), F32)]


def exchange(x, axis):
    return lax.all_to_all(x, axis, split_axis=0, concat_axis=0, tiled=True)


def gather(x, axis, n):
    return exchange(jnp.broadcast_to(x[None], (n,) + x.shape), axis)


def in_order(own, near, far, corner, q):
    even = q % 2 == 0
    low = q < 2
    a0, a1 = jnp.where(even, own, near), jnp.where(even, near, own)
    b0, b1 = jnp.where(even, far, corner), jnp.where(even, corner, far)
    return jnp.stack([jnp.where(low, a0, b0), jnp.where(low, a1, b1), jnp.where(low, b0, a0), jnp.where(low, b1, a1)])


def across(x, k):
    return lax.ppermute(x, "col", [(i, i ^ k) for i in range(4)])


def spread_far(x):
    return jnp.stack([x, across(x, 2)])


def spread_near(pair, q):
    near = across(pair, 1)
    return in_order(pair[0], near[0], pair[1], near[1], q)


def gather_col(x, q):
    return spread_near(spread_far(x), q)


def from_first_col(x, q):
    sent = [lax.ppermute(x[k], "col", [(0, k)]) for k in (1, 2, 3)]
    return jnp.where(q == 0, x[0], sent[0] + sent[1] + sent[2])


def exchange_col(x, q):
    parts = [lax.dynamic_index_in_dim(x, q ^ k, 0, keepdims=False) for k in range(4)]
    return in_order(parts[0], *[across(parts[k], k) for k in (1, 2, 3)], q)


def after(x, *earlier):
    return lax.optimization_barrier((x,) + earlier)[0]


def swap_child(x):
    return lax.ppermute(x, "child", [(0, 1), (1, 0)])


def local(child_fronts, root_front, block_maps):
    front = child_fronts[0]
    child = lax.axis_index("child")
    r = lax.axis_index("row")
    q = lax.axis_index("col")
    blocks = jnp.arange(64, dtype=jnp.int32)
    order = jnp.arange(1, NCB + 1, dtype=jnp.int32)
    inverse = jnp.sum(jnp.where(block_maps[:, :, None] == blocks, order[None, :, None], 0), axis=1) - 1
    mine = jnp.where(child == 0, inverse[0], inverse[1])
    theirs = jnp.where(child == 0, inverse[1], inverse[0])

    def pick(idx):
        return jnp.sum(jnp.where(idx[:, None] == blocks[None, :], mine[None, :], 0), axis=1)

    slot = jnp.arange(64, dtype=jnp.int32)
    half = jnp.where(slot % 4 >= 2, 1 - child, child)
    bulk_idx = pick(32 * half + 2 * (slot // 4) + slot % 2)
    panel_idx = mine[0:4]
    four = jnp.arange(4, dtype=jnp.int32)
    col_idx = pick(32 * jnp.where(four >= 2, 1 - child, child) + 2 * r + four % 2)
    row_idx = pick(16 * four + r)

    quarters = front.reshape(2, 4, 32, 1024).transpose(1, 0, 2, 3).reshape(4, 64, 1024)
    left = from_first_col(quarters[:, :, 0:512], q)
    d00 = gather(exchange(left.reshape(16, 4, 512), "row")[0:2], "row", ROWS)

    raw_top = root_front[0:512].reshape(4, 4, 32, 256).transpose(1, 0, 2, 3).reshape(4, 2, 64, 256)
    right = jnp.concatenate([quarters[:, :, 512:1024], raw_top[:, 0], raw_top[:, 1]], axis=2)
    right = from_first_col(after(right, left), q)
    top = jnp.concatenate([right[:, 512:768], right[:, 768:1024]], axis=0)
    heads = after(jnp.concatenate([left, right], axis=1).reshape(16, 4, 1536), d00)
    heads = exchange(heads, "row")
    lower, corner = lax.optimization_barrier((heads[2:4, :, 0:1024], heads[0:2, :, 1024:1536]))
    second = gather(jnp.concatenate([lower, corner], axis=2), "row", ROWS)
    d1 = second[:, :, :, 0:1024]
    raw_diag = jnp.concatenate([
        jnp.concatenate([second[:, h, :, c:c + 256] for h in range(2)], axis=2).reshape(64, 512) for c in (1024, 1280)
    ], axis=0)
    raw_diag = jnp.where(child == 0, raw_diag, 0.0)

    y = exchange_col(after(quarters, right), q)
    panel_y = y[1][:, 0:512]
    placed_panel = call(place_panel_kernel, sds((64, 512)), 1, 1, name="place_panel")(panel_idx, panel_y)

    d00, placed_panel = lax.optimization_barrier((gather_col(d00, q), placed_panel))
    inv0, p0, u0 = call(
        head_kernel, (sds((512, 512)), sds((64, 512)), sds((64, 512), BF16)), 0, 2, CHOL, 2 * 10**10, "head")(d00, left)
    f_panel = lax.all_gather(placed_panel, "row").reshape(32, 32, 512)
    u0_all = jnp.broadcast_to(u0.reshape(1, 2, 32, 512), (ROWS, 2, 32, 512))
    d1 = spread_near(after(spread_far(d1), inv0), q)
    d1, u0_all = lax.optimization_barrier((d1, u0_all))
    u0_all = exchange(u0_all, "row").reshape(32, 32, 512)

    below = (r >= 2).astype(jnp.int32)[None]
    p1, u1 = call(
        second_kernel, (sds((64, 512)), sds((64, 512), BF16)), 1, 4,
        [pltpu.VMEM((512, 512), F32)] * 2 + CHOL, 3 * 10**10, "second")(below, d1, inv0, right[:, 0:512], u0)
    u1, u0_all = lax.optimization_barrier((u1, u0_all))
    u1_all = gather(u1.reshape(2, 32, 512), "row", ROWS).reshape(32, 32, 512)
    raw_rows = 0.0
    tile_top = after(root_front[0:512], u1)
    for j in range(2):
        pairs = []
        for g in range(32):
            m = 2 * g + j
            pairs.append((4 * g, (m // 32 * 16 + m % 16) * 4 + m // 16))
        raw_rows += lax.ppermute(tile_top[:, 128 * j:128 * j + 128], ("child", "row", "col"), pairs)
    child_factor = gather_col(jnp.concatenate([p0, after(p1, u1)], axis=1).reshape(2, 32, 1024), q)
    wide = after(jnp.concatenate([y[1], y[2], y[3]], axis=1), u1)
    placed = call(place_kernel, sds((16, 64, 512)), 1, 1, name="place")(bulk_idx, wide)
    u1_all, child_factor, placed, raw_rows = lax.optimization_barrier((u1_all, child_factor, placed, raw_rows))
    raw_rows = raw_rows.T
    child_factor = child_factor.transpose(1, 0, 2, 3).reshape(1, 256, 1024)
    f_bulk = exchange(placed, "row").reshape(32, 32, 512)

    some = sds((4, 32, 1024), BF16)
    u_panel, u_bulk = call(select_kernel, (some, some), 2, 2, name="select")(panel_idx, col_idx, u0_all, u1_all)
    u_panel = spread_far(u_panel)
    u_bulk = spread_far(after(u_bulk, u_panel))
    z, t = call(panel_kernel, (sds((128, 512)), sds((128, 512))), 2, 4, flops=10**9, name="panel")(
        row_idx, panel_idx, u0_all, u1_all, spread_near(u_panel, q), f_panel)
    z, t, u_bulk = lax.optimization_barrier((z, t, u_bulk))
    t = t + raw_diag
    t = t + swap_child(t)
    u_bulk = spread_near(u_bulk, q)
    z = exchange_col(z.reshape(4, 32, 512), q).reshape(128, 512) + raw_rows
    z, t, u_bulk = lax.optimization_barrier((z, t, u_bulk))
    z_swapped, f_bulk = lax.optimization_barrier((swap_child(z), f_bulk))
    own, other = call(bulk_kernel, (sds((768, 256)), sds((768, 256))), 0, 4, flops=2 * 10**9, name="bulk")(
        u0_all, u1_all, u_bulk, f_bulk)
    z = z + z_swapped
    panel = lax.all_gather(z, "row", tiled=True)

    t_all = gather_col(t.reshape(4, 32, 512), q)
    got = swap_child(after(other, z_swapped))
    spread = call(spread_kernel, sds((64, 32, 256)), 2, 2, name="spread")(
        mine, theirs, own.reshape(24, 32, 256), got.reshape(24, 32, 256))
    t_all, spread, z = lax.optimization_barrier((t_all, spread, z))
    arrived = exchange_col(spread.reshape(4, 16, 32, 256), q)
    inv_root = call(root_kernel, sds((512, 512)), 0, 1, CHOL, 2 * 10**10, "root")(t_all)
    head_cols = gather_col(top.reshape(4, 32, 256) + spread[0:4], q)

    flags = jnp.stack([16 * child + r >= 2, q > 0]).astype(jnp.int32)
    root_factor, trailing = pl.pallas_call(
        last_kernel,
        out_shape=(sds((2048, 512)), sds((2048, 256))),
        grid=(8,),
        in_specs=[
            smem(),
            pl.BlockSpec((256, 512), lambda i: (i, 0)),
            pl.BlockSpec((512, 512), lambda i: (0, 0)),
            pl.BlockSpec((4, 4, 32, 256), lambda i: (0, 0, 0, 0)),
            pl.BlockSpec((256, 256), lambda i: (i, 0)),
            pl.BlockSpec((4, 2, 32, 256), lambda i: (0, i, 0, 0)),
        ],
        out_specs=(pl.BlockSpec((256, 512), lambda i: (i, 0)), pl.BlockSpec((256, 256), lambda i: (i, 0))),
        scratch_shapes=[pltpu.VMEM((512, 256), BF16), pltpu.VMEM((512, 256), F32)],
        compiler_params=VM,
        name="last",
    )(flags, panel, inv_root, head_cols, root_front, arrived)
    return (child_factor, root_factor, trailing)


def solution(mesh):
    return jax.shard_map(
        local,
        mesh=mesh,
        in_specs=(P("child", "row", "col"), P("col", ("child", "row")), P()),
        out_specs=(P("child", "row", None), P("col", None), P("col", ("child", "row"))),
        check_vma=False,
    )
```

```python
import functools

import jax
import jax.numpy as jnp
from jax import lax
from jax.experimental import pallas as pl
from jax.experimental.pallas import tpu as pltpu
from jax.sharding import PartitionSpec as P

F32 = jnp.float32
BF16 = jnp.bfloat16
HI = lax.Precision.HIGHEST
ROWS, COLS = 16, 4
NCB = 24
VM = pltpu.CompilerParams(vmem_limit_bytes=56 << 20)


def lane_copy(v, k):
    return jnp.broadcast_to(v[:, k:k + 1], (8, 128))


def sub_copy(v, k):
    return jnp.broadcast_to(v[k:k + 1, :], (8, 128))


def dot(a, b, ca, cb):
    return lax.dot_general(a, b, (((ca,), (cb,)), ((), ())), precision=HI, preferred_element_type=F32)


def dot16(a, b, ca, cb):
    return lax.dot_general(a, b, (((ca,), (cb,)), ((), ())), preferred_element_type=F32)


def inverse_factor128(block):
    lane = lax.broadcasted_iota(jnp.int32, (8, 128), 1)
    sub = lax.broadcasted_iota(jnp.int32, (8, 128), 0)
    w = [block[8 * t:8 * t + 8, :] for t in range(16)]
    for s in range(16):
        c = {t: [lane_copy(w[t], 8 * s + j) for j in range(8)] for t in range(s, 16)}
        inside = (lane >= 8 * s) & (lane < 8 * s + 8)
        w[s] = jnp.where(inside, (lane - 8 * s == sub).astype(F32), w[s])
        for t in range(s + 1, 16):
            w[t] = jnp.where(inside, 0.0, w[t])
        for j in range(8):
            scale = lax.rsqrt(sub_copy(c[s][j], j))
            pivot_row = sub_copy(w[s], j) * scale
            ahead = {k: sub_copy(c[s][j], k) * scale for k in range(j + 1, 8)}
            for t in range(s, 16):
                l = c[t][j] * scale
                if t == s:
                    l = jnp.where(sub > j, l, 0.0)
                for k in range(j + 1, 8):
                    c[t][k] = c[t][k] - l * ahead[k]
                w[t] = w[t] - l * pivot_row
            w[s] = jnp.where(sub == j, pivot_row, w[s])
    return jnp.concatenate([jnp.where(lane <= sub + 8 * t, w[t], 0.0) for t in range(16)], axis=0)


def inverse_factor512(a, b, g):
    n = 512
    b[...] = jnp.zeros((n, n), F32)

    def block(k, carry):
        o = pl.multiple_of(128 * k, 128)
        g[...] = inverse_factor128(a[pl.ds(o, 128), pl.ds(o, 128)])
        for step in range(n // 128):
            pl.when(k == step)(functools.partial(outer, 128 * step))
        return carry

    def outer(o):
        inv = g[...]
        if o > 0:
            b[o:o + 128, 0:o] = dot(inv, b[o:o + 128, 0:o], 1, 0)
        b[o:o + 128, o:o + 128] = inv
        r = o + 128
        if r < n:
            l = dot(a[r:n, o:o + 128], inv, 1, 1)
            a[r:n, r:n] = a[r:n, r:n] - dot(l, l, 1, 1)
            b[r:n, 0:r] = b[r:n, 0:r] - dot(l, b[o:o + 128, 0:r], 1, 0)

    lax.fori_loop(0, n // 128, block, 0)


def head_rows():
    for s in range(16):
        for q in range(4):
            for h in range(2):
                yield 256 * h + 128 * (s // 8) + 32 * q + 4 * (s % 8), (s, 2 * q + h)


def head_kernel(d_ref, c_ref, inv_ref, p_ref, u_ref, a, g):
    for o, piece in head_rows():
        a[o:o + 4, :] = d_ref[piece]
    inverse_factor512(a, inv_ref, g)
    p = dot(c_ref[...], inv_ref[...], 1, 1)
    p_ref[...] = p
    u_ref[...] = p.astype(BF16)


def second_kernel(mask_ref, d_ref, inv0_ref, c_ref, u0_ref, p_ref, u_ref, d10, inv1, a, g):
    for o, (s, i) in head_rows():
        d10[o:o + 4, :] = d_ref[s, i, :, 0:512]
        a[o:o + 4, :] = d_ref[s, i, :, 512:1024]
    u10 = dot(d10[...], inv0_ref[...], 1, 1).astype(BF16)
    a[...] = a[...] - dot16(u10, u10, 1, 1)
    c1 = c_ref[...] - dot16(u0_ref[...], u10, 1, 1)
    inverse_factor512(a, inv1, g)
    p1 = dot(c1, inv1[...], 1, 1)
    p_ref[...] = jnp.where(mask_ref[0] > 0, p1, 0.0)
    u_ref[...] = p1.astype(BF16)


def place(b, y_ref):
    col = pl.multiple_of(jnp.maximum(b, 0) * 128, 128)
    return jnp.where(b >= 0, y_ref[:, pl.ds(col, 128)], 0.0)


def place_panel_kernel(panel_ref, y_ref, p_ref):
    for m in range(4):
        p_ref[:, 128 * m:128 * m + 128] = place(panel_ref[m], y_ref)


def place_kernel(bulk_ref, y_ref, o_ref):
    def one(slot, carry):
        out = pl.multiple_of((slot % 4) * 128, 128)
        o_ref[slot // 4, :, pl.ds(out, 128)] = place(bulk_ref[slot], y_ref)
        return carry

    lax.fori_loop(0, 64, one, 0)


def picked(b, ref):
    v = ref[jnp.maximum(b, 0) + 8]
    return jnp.where(b >= 0, v, jnp.zeros_like(v))


def select_kernel(panel_ref, bulk_ref, u0_ref, u1_ref, p_ref, o_ref):
    for ref, out in ((panel_ref, p_ref), (bulk_ref, o_ref)):
        for i in range(4):
            out[i, :, 0:512] = picked(ref[i], u0_ref)
            out[i, :, 512:1024] = picked(ref[i], u1_ref)


def panel_kernel(rows_ref, panel_ref, u0_ref, u1_ref, ucol_ref, fp_ref, z_ref, t_ref):
    upan = jnp.concatenate([ucol_ref[q, m] for m in range(4) for q in range(4)], axis=0)
    for ref, out in ((panel_ref, t_ref), (rows_ref, z_ref)):
        f, u0, u1 = [jnp.concatenate([picked(ref[i], x) for i in range(4)], axis=0) for x in (fp_ref, u0_ref, u1_ref)]
        out[...] = f - dot16(jnp.concatenate([u0, u1], axis=1), upan, 1, 1)


def bulk_kernel(u0_ref, u1_ref, ucol_ref, f_ref, own_ref, other_ref):
    ubulk = jnp.concatenate([ucol_ref[q, j] for j in range(4) for q in range(4)], axis=0)
    rows = jnp.concatenate([u0_ref[8:32].reshape(768, 512), u1_ref[8:32].reshape(768, 512)], axis=1)
    s = f_ref[8:32].reshape(768, 512) - dot16(rows, ubulk, 1, 1)
    own_ref[...] = s[:, 0:256]
    other_ref[...] = s[:, 256:512]


def root_kernel(t_ref, inv_ref, a, g):
    for q in range(4):
        for m in range(4):
            a[128 * m + 32 * q:128 * m + 32 * q + 32, :] = t_ref[q, m]
    inverse_factor512(a, inv_ref, g)


def spread_kernel(mine_ref, theirs_ref, own_ref, got_ref, o_ref):
    def one(m, carry):
        i = mine_ref[m]
        j = theirs_ref[m]
        v = own_ref[jnp.maximum(i, 0)]
        w = got_ref[jnp.maximum(j, 0)]
        o_ref[m] = jnp.where(i >= 0, v, 0.0) + jnp.where(j >= 0, w, 0.0)
        return carry

    lax.fori_loop(0, 64, one, 0)


def factor_kernel(flag_ref, panel_ref, inv_ref, cp_ref, p_ref, u_ref, ug_ref, cps):
    step = pl.program_id(0)

    @pl.when(step == 0)
    def _():
        for q in range(4):
            for m in range(4):
                cps[128 * m + 32 * q:128 * m + 32 * q + 32, :] = cp_ref[q, m]
        v = dot(inv_ref[...], cps[...], 1, 0).astype(BF16)
        ug_ref[...] = jnp.where(flag_ref[0] > 0, v, jnp.zeros_like(v))

    p = dot(panel_ref[...], inv_ref[...], 1, 1)
    p_ref[...] = p
    u = p.astype(BF16)
    u_ref[...] = jnp.where((flag_ref[1] > 0) | (step >= 1), u, jnp.zeros_like(u))


def last_kernel(u_ref, ug_ref, root_ref, got_ref, o_ref):
    upd = dot16(u_ref[...], ug_ref[...], 1, 0)
    for m in range(4):
        for q in range(4):
            o = 128 * m + 32 * q
            o_ref[o:o + 32, :] = root_ref[o:o + 32, :] + got_ref[q, m] - upd[o:o + 32, :]


def vmem():
    return pl.BlockSpec(memory_space=pltpu.VMEM)


def smem():
    return pl.BlockSpec(memory_space=pltpu.SMEM)


def call(kernel, outs, n_scalar, n_vector, scratch=(), flops=0, name=None):
    return pl.pallas_call(
        kernel,
        out_shape=outs,
        in_specs=[smem()] * n_scalar + [vmem()] * n_vector,
        out_specs=jax.tree.map(lambda _: vmem(), outs),
        scratch_shapes=list(scratch),
        compiler_params=VM,
        cost_estimate=pl.CostEstimate(flops=flops, transcendentals=0, bytes_accessed=1 << 20),
        name=name,
    )


def sds(shape, dtype=F32):
    return jax.ShapeDtypeStruct(shape, dtype)


CHOL = [pltpu.VMEM((512, 512), F32), pltpu.VMEM((128, 128), F32)]


def exchange(x, axis):
    return lax.all_to_all(x, axis, split_axis=0, concat_axis=0, tiled=True)


def gather(x, axis, n):
    return exchange(jnp.broadcast_to(x[None], (n,) + x.shape), axis)


def in_order(own, near, far, corner, q):
    even = q % 2 == 0
    low = q < 2
    a0, a1 = jnp.where(even, own, near), jnp.where(even, near, own)
    b0, b1 = jnp.where(even, far, corner), jnp.where(even, corner, far)
    return jnp.stack([jnp.where(low, a0, b0), jnp.where(low, a1, b1), jnp.where(low, b0, a0), jnp.where(low, b1, a1)])


def across(x, k):
    return lax.ppermute(x, "col", [(i, i ^ k) for i in range(4)])


def spread_far(x):
    return jnp.stack([x, across(x, 2)])


def spread_near(pair, q):
    near = across(pair, 1)
    return in_order(pair[0], near[0], pair[1], near[1], q)


def gather_col(x, q):
    return spread_near(spread_far(x), q)


def from_first_col(x, q):
    sent = [lax.ppermute(x[k], "col", [(0, k)]) for k in (1, 2, 3)]
    return jnp.where(q == 0, x[0], sent[0] + sent[1] + sent[2])


def exchange_col(x, q):
    return in_order(*sent_col(x, q), q)


def sent_col(x, q):
    parts = [lax.dynamic_index_in_dim(x, q ^ k, 0, keepdims=False) for k in range(4)]
    return [parts[0]] + [across(parts[k], k) for k in (1, 2, 3)]


def after(x, *earlier):
    return lax.optimization_barrier((x,) + earlier)[0]


def swap_child(x):
    return lax.ppermute(x, "child", [(0, 1), (1, 0)])


def local(child_fronts, root_front, block_maps):
    front = child_fronts[0]
    child = lax.axis_index("child")
    r = lax.axis_index("row")
    q = lax.axis_index("col")
    blocks = jnp.arange(64, dtype=jnp.int32)
    order = jnp.arange(1, NCB + 1, dtype=jnp.int32)
    inverse = jnp.sum(jnp.where(block_maps[:, :, None] == blocks, order[None, :, None], 0), axis=1) - 1
    mine = jnp.where(child == 0, inverse[0], inverse[1])
    theirs = jnp.where(child == 0, inverse[1], inverse[0])

    def pick(idx):
        return jnp.sum(jnp.where(idx[:, None] == blocks[None, :], mine[None, :], 0), axis=1)

    slot = jnp.arange(64, dtype=jnp.int32)
    half = jnp.where(slot % 4 >= 2, 1 - child, child)
    bulk_idx = pick(32 * half + 2 * (slot // 4) + slot % 2)
    panel_idx = mine[0:4]
    four = jnp.arange(4, dtype=jnp.int32)
    col_idx = pick(32 * jnp.where(four >= 2, 1 - child, child) + 2 * r + four % 2)
    row_idx = pick(16 * four + r)

    quarters = front.reshape(2, 4, 32, 1024).transpose(1, 0, 2, 3).reshape(4, 64, 1024)
    raw_top = root_front[0:512].reshape(4, 4, 32, 256).transpose(1, 0, 2, 3).reshape(4, 2, 64, 256)
    pack = from_first_col(jnp.concatenate([quarters, raw_top[:, 0], raw_top[:, 1]], axis=2), q)
    left = pack[:, 0:512]
    top = jnp.concatenate([pack[:, 1024:1280], pack[:, 1280:1536]], axis=0)

    heads = exchange(pack.reshape(16, 4, 1536), "row")
    first, second, corner0, corner1 = lax.optimization_barrier(
        (heads[0:2, :, 0:512], heads[2:4, :, 0:1024], heads[0:1, :, 1024:1536], heads[1:2, :, 1024:1536]))
    d00 = gather(gather_col(first, q).reshape(8, 4, 512), "row", ROWS)
    corner = jnp.concatenate([corner0, corner1], axis=2)
    second = jnp.concatenate([gather_col(second, q).reshape(8, 4, 1024), corner], axis=0)
    second = jnp.broadcast_to(second[None], (ROWS,) + second.shape)
    d00, second = lax.optimization_barrier((d00, second))
    d1 = exchange(second, "row")
    raw_diag = jnp.concatenate([
        jnp.concatenate([d1[:, 8, :, c:c + 256] for c in (o, o + 512)], axis=2).reshape(64, 512) for o in (0, 256)
    ], axis=0)
    raw_diag = jnp.where(child == 0, raw_diag, 0.0)

    y = exchange_col(after(quarters, heads), q)
    panel_y = y[1][:, 0:512]
    placed_panel = call(place_panel_kernel, sds((64, 512)), 1, 1, name="place_panel")(panel_idx, panel_y)

    d00, placed_panel = lax.optimization_barrier((d00, placed_panel))
    inv0, p0, u0 = call(
        head_kernel, (sds((512, 512)), sds((64, 512)), sds((64, 512), BF16)), 0, 2, CHOL, 2 * 10**10, "head")(d00, left)
    f_panel = lax.all_gather(placed_panel, "row").reshape(32, 32, 512)
    u0_all = jnp.broadcast_to(u0.reshape(1, 2, 32, 512), (ROWS, 2, 32, 512))
    d1, u0_all = lax.optimization_barrier((d1, u0_all))
    u0_all = exchange(u0_all, "row").reshape(32, 32, 512)

    below = (r >= 2).astype(jnp.int32)[None]
    p1, u1 = call(
        second_kernel, (sds((64, 512)), sds((64, 512), BF16)), 1, 4,
        [pltpu.VMEM((512, 512), F32)] * 2 + CHOL, 3 * 10**10, "second")(below, d1, inv0, pack[:, 512:1024], u0)
    u1, u0_all = lax.optimization_barrier((u1, u0_all))
    u1_all = gather(u1.reshape(2, 32, 512), "row", ROWS).reshape(32, 32, 512)
    raw_rows = 0.0
    tile_top = after(root_front[0:512], u1)
    for j in range(2):
        pairs = []
        for g in range(32):
            m = 2 * g + j
            pairs.append((4 * g, (m // 32 * 16 + m % 16) * 4 + m // 16))
        raw_rows += lax.ppermute(tile_top[:, 128 * j:128 * j + 128], ("child", "row", "col"), pairs)
    wide = after(jnp.concatenate([y[1], y[2], y[3]], axis=1), u1)
    placed = call(place_kernel, sds((16, 64, 512)), 1, 1, name="place")(bulk_idx, wide)
    u1_all, placed, raw_rows = lax.optimization_barrier((u1_all, placed, raw_rows))
    raw_rows = raw_rows.T
    f_bulk = exchange(placed, "row").reshape(32, 32, 512)

    some = sds((4, 32, 1024), BF16)
    u_panel, u_bulk = call(select_kernel, (some, some), 2, 2, name="select")(panel_idx, col_idx, u0_all, u1_all)
    u_panel = spread_far(u_panel)
    u_bulk = spread_far(after(u_bulk, u_panel))
    z, t = call(panel_kernel, (sds((128, 512)), sds((128, 512))), 2, 4, flops=10**9, name="panel")(
        row_idx, panel_idx, u0_all, u1_all, spread_near(u_panel, q), f_panel)
    z, t, u_bulk = lax.optimization_barrier((z, t, u_bulk))
    t = t + raw_diag
    t = t + swap_child(t)
    u_bulk = spread_near(u_bulk, q)
    z = exchange_col(z.reshape(4, 32, 512), q).reshape(128, 512) + raw_rows
    z, t, u_bulk = lax.optimization_barrier((z, t, u_bulk))
    t = spread_far(t.reshape(4, 32, 512))
    z_swapped, f_bulk, t = lax.optimization_barrier((swap_child(z), f_bulk, t))
    z = z + z_swapped
    panel = lax.all_gather(z, "row", tiled=True)
    t_all = spread_near(t, q)

    own, other = call(bulk_kernel, (sds((768, 256)), sds((768, 256))), 0, 4, flops=2 * 10**9, name="bulk")(
        u0_all, u1_all, u_bulk, f_bulk)
    t_all, z, other = lax.optimization_barrier((t_all, z, other))
    inv_root = call(root_kernel, sds((512, 512)), 0, 1, CHOL, 2 * 10**10, "root")(t_all)
    got, inv_root = lax.optimization_barrier((swap_child(other), inv_root))
    spread = call(spread_kernel, sds((64, 32, 256)), 2, 2, name="spread")(
        mine, theirs, own.reshape(24, 32, 256), got.reshape(24, 32, 256))
    arrived = sent_col(spread.reshape(4, 16, 32, 256), q)
    head_cols = gather_col(top.reshape(4, 32, 256) + spread[0:4], q)
    p = after(jnp.concatenate([p0, p1], axis=1), spread)
    child_factor = gather_col(p.reshape(2, 32, 1024), q).transpose(1, 0, 2, 3).reshape(1, 256, 1024)

    flags = jnp.stack([16 * child + r >= 2, q > 0]).astype(jnp.int32)
    rows = pl.BlockSpec((512, 512), lambda i: (i, 0))
    whole = pl.BlockSpec((512, 512), lambda i: (0, 0))
    narrow = pl.BlockSpec((512, 256), lambda i: (i, 0))
    fixed = pl.BlockSpec((512, 256), lambda i: (0, 0))
    root_factor, u_root, u_cols = pl.pallas_call(
        factor_kernel,
        out_shape=(sds((2048, 512)), sds((2048, 512), BF16), sds((512, 256), BF16)),
        grid=(4,),
        in_specs=[smem(), rows, whole, pl.BlockSpec((4, 4, 32, 256), lambda i: (0, 0, 0, 0))],
        out_specs=(rows, rows, fixed),
        scratch_shapes=[pltpu.VMEM((512, 256), F32)],
        compiler_params=VM,
        cost_estimate=pl.CostEstimate(flops=10**10, transcendentals=0, bytes_accessed=1 << 20),
        name="factor",
    )(flags, panel, inv_root, head_cols)
    arrived, u_root = lax.optimization_barrier((arrived, u_root))
    trailing = pl.pallas_call(
        last_kernel,
        out_shape=sds((2048, 256)),
        grid=(4,),
        in_specs=[rows, fixed, narrow, pl.BlockSpec((4, 4, 32, 256), lambda i: (0, i, 0, 0))],
        out_specs=narrow,
        compiler_params=VM,
        name="last",
    )(u_root, u_cols, root_front, in_order(*arrived, q))
    return (child_factor, root_factor, trailing)


def solution(mesh):
    return jax.shard_map(
        local,
        mesh=mesh,
        in_specs=(P("child", "row", "col"), P("col", ("child", "row")), P()),
        out_specs=(P("child", "row", None), P("col", None), P("col", ("child", "row"))),
        check_vma=False,
    )
```

```python
import functools

import jax
import jax.numpy as jnp
from jax import lax
from jax.experimental import pallas as pl
from jax.experimental.pallas import tpu as pltpu
from jax.sharding import PartitionSpec as P

F32 = jnp.float32
BF16 = jnp.bfloat16
HI = lax.Precision.HIGHEST
ROWS, COLS = 16, 4
NCB = 24
VM = pltpu.CompilerParams(vmem_limit_bytes=56 << 20)


def lane_copy(v, k):
    return jnp.broadcast_to(v[:, k:k + 1], (8, 128))


def sub_copy(v, k):
    return jnp.broadcast_to(v[k:k + 1, :], (8, 128))


def dot(a, b, ca, cb):
    return lax.dot_general(a, b, (((ca,), (cb,)), ((), ())), precision=HI, preferred_element_type=F32)


def dot16(a, b, ca, cb):
    return lax.dot_general(a, b, (((ca,), (cb,)), ((), ())), preferred_element_type=F32)


def inverse_factor128(block):
    lane = lax.broadcasted_iota(jnp.int32, (8, 128), 1)
    sub = lax.broadcasted_iota(jnp.int32, (8, 128), 0)
    w = [block[8 * t:8 * t + 8, :] for t in range(16)]
    for s in range(16):
        c = {t: [lane_copy(w[t], 8 * s + j) for j in range(8)] for t in range(s, 16)}
        inside = (lane >= 8 * s) & (lane < 8 * s + 8)
        w[s] = jnp.where(inside, (lane - 8 * s == sub).astype(F32), w[s])
        for t in range(s + 1, 16):
            w[t] = jnp.where(inside, 0.0, w[t])
        for j in range(8):
            scale = lax.rsqrt(sub_copy(c[s][j], j))
            pivot_row = sub_copy(w[s], j) * scale
            ahead = {k: sub_copy(c[s][j], k) * scale for k in range(j + 1, 8)}
            for t in range(s, 16):
                l = c[t][j] * scale
                if t == s:
                    l = jnp.where(sub > j, l, 0.0)
                for k in range(j + 1, 8):
                    c[t][k] = c[t][k] - l * ahead[k]
                w[t] = w[t] - l * pivot_row
            w[s] = jnp.where(sub == j, pivot_row, w[s])
    return jnp.concatenate([jnp.where(lane <= sub + 8 * t, w[t], 0.0) for t in range(16)], axis=0)


def inverse_factor512(a, b, g):
    n = 512
    b[...] = jnp.zeros((n, n), F32)

    def block(k, carry):
        o = pl.multiple_of(128 * k, 128)
        g[...] = inverse_factor128(a[pl.ds(o, 128), pl.ds(o, 128)])
        for step in range(n // 128):
            pl.when(k == step)(functools.partial(outer, 128 * step))
        return carry

    def outer(o):
        inv = g[...]
        if o > 0:
            b[o:o + 128, 0:o] = dot(inv, b[o:o + 128, 0:o], 1, 0)
        b[o:o + 128, o:o + 128] = inv
        r = o + 128
        if r < n:
            l = dot(a[r:n, o:o + 128], inv, 1, 1)
            a[r:n, r:n] = a[r:n, r:n] - dot(l, l, 1, 1)
            b[r:n, 0:r] = b[r:n, 0:r] - dot(l, b[o:o + 128, 0:r], 1, 0)

    lax.fori_loop(0, n // 128, block, 0)


def head_rows():
    for s in range(16):
        for q in range(4):
            for h in range(2):
                yield 256 * h + 128 * (s // 8) + 32 * q + 4 * (s % 8), (s, 2 * q + h)


def head_kernel(d_ref, c_ref, inv_ref, p_ref, u_ref, a, g):
    for o, piece in head_rows():
        a[o:o + 4, :] = d_ref[piece]
    inverse_factor512(a, inv_ref, g)
    p = dot(c_ref[...], inv_ref[...], 1, 1)
    p_ref[...] = p
    u_ref[...] = p.astype(BF16)


def second_kernel(mask_ref, d_ref, inv0_ref, c_ref, u0_ref, p_ref, u_ref, d10, inv1, a, g):
    for o, (s, i) in head_rows():
        d10[o:o + 4, :] = d_ref[s, i, :, 0:512]
        a[o:o + 4, :] = d_ref[s, i, :, 512:1024]
    u10 = dot(d10[...], inv0_ref[...], 1, 1).astype(BF16)
    a[...] = a[...] - dot16(u10, u10, 1, 1)
    c1 = c_ref[...] - dot16(u0_ref[...], u10, 1, 1)
    inverse_factor512(a, inv1, g)
    p1 = dot(c1, inv1[...], 1, 1)
    p_ref[...] = jnp.where(mask_ref[0] > 0, p1, 0.0)
    u_ref[...] = p1.astype(BF16)


def place(b, y_ref):
    col = pl.multiple_of(jnp.maximum(b, 0) * 128, 128)
    return jnp.where(b >= 0, y_ref[:, pl.ds(col, 128)], 0.0)


def place_panel_kernel(panel_ref, y_ref, p_ref):
    for m in range(4):
        p_ref[:, 128 * m:128 * m + 128] = place(panel_ref[m], y_ref)


def place_kernel(bulk_ref, y_ref, o_ref):
    def one(slot, carry):
        out = pl.multiple_of((slot % 4) * 128, 128)
        o_ref[slot // 4, :, pl.ds(out, 128)] = place(bulk_ref[slot], y_ref)
        return carry

    lax.fori_loop(0, 64, one, 0)


def picked(b, ref):
    v = ref[jnp.maximum(b, 0) + 8]
    return jnp.where(b >= 0, v, jnp.zeros_like(v))


def sender(refs, q_ref, p):
    j = p ^ q_ref[0]

    def read(i):
        x, near, far, corner = [ref[i] for ref in refs]
        return jnp.where(j >= 2, jnp.where(j == 3, corner, far), jnp.where(j == 1, near, x))

    return read


def columns_of(refs, q_ref):
    return jnp.concatenate([sender(refs, q_ref, q)(m) for m in range(4) for q in range(4)], axis=0)


def select_kernel(panel_ref, bulk_ref, u0_ref, u1_ref, p_ref, o_ref):
    for ref, out in ((panel_ref, p_ref), (bulk_ref, o_ref)):
        for i in range(4):
            out[i, :, 0:512] = picked(ref[i], u0_ref)
            out[i, :, 512:1024] = picked(ref[i], u1_ref)


def panel_kernel(q_ref, rows_ref, panel_ref, u0_ref, u1_ref, fp_ref, c0, c1, c2, c3, z_ref, t_ref):
    upan = columns_of((c0, c1, c2, c3), q_ref)
    for ref, out in ((panel_ref, t_ref), (rows_ref, z_ref)):
        f, u0, u1 = [jnp.concatenate([picked(ref[i], x) for i in range(4)], axis=0) for x in (fp_ref, u0_ref, u1_ref)]
        out[...] = f - dot16(jnp.concatenate([u0, u1], axis=1), upan, 1, 1)


def bulk_kernel(q_ref, panel_ref, u0_ref, u1_ref, f_ref, c0, c1, c2, c3, own_ref, other_ref, first_ref, send_ref):
    ubulk = columns_of((c0, c1, c2, c3), q_ref)
    rows = jnp.concatenate([u0_ref[8:32].reshape(768, 512), u1_ref[8:32].reshape(768, 512)], axis=1)
    s = f_ref[8:32].reshape(768, 512) - dot16(rows, ubulk, 1, 1)
    own_ref[...] = s[:, 0:256]
    other_ref[...] = s[:, 256:512]
    for m in range(4):
        b = panel_ref[m]
        rows = pl.ds(pl.multiple_of(32 * jnp.maximum(b, 0), 32), 32)
        first_ref[m] = jnp.where(b >= 0, own_ref[rows, :], 0.0)
        send_ref[m] = jnp.where(b >= 0, other_ref[rows, :], 0.0)


def root_kernel(q_ref, t0, t1, t2, t3, inv_ref, a, g):
    for q in range(4):
        read = sender((t0, t1, t2, t3), q_ref, q)
        for m in range(4):
            a[128 * m + 32 * q:128 * m + 32 * q + 32, :] = read(m)
    inverse_factor512(a, inv_ref, g)


def spread_kernel(mine_ref, theirs_ref, own_ref, got_ref, o_ref):
    def one(m, carry):
        i = mine_ref[m]
        j = theirs_ref[m]
        v = own_ref[jnp.maximum(i, 0)]
        w = got_ref[jnp.maximum(j, 0)]
        o_ref[m] = jnp.where(i >= 0, v, 0.0) + jnp.where(j >= 0, w, 0.0)
        return carry

    lax.fori_loop(0, 64, one, 0)


def factor_kernel(flag_ref, panel_ref, inv_ref, cp_ref, p_ref, u_ref, ug_ref, cps):
    step = pl.program_id(0)

    @pl.when(step == 0)
    def _():
        for q in range(4):
            for m in range(4):
                cps[128 * m + 32 * q:128 * m + 32 * q + 32, :] = cp_ref[q, m]
        v = dot(inv_ref[...], cps[...], 1, 0).astype(BF16)
        ug_ref[...] = jnp.where(flag_ref[0] > 0, v, jnp.zeros_like(v))

    p = dot(panel_ref[...], inv_ref[...], 1, 1)
    p_ref[...] = p
    u = p.astype(BF16)
    u_ref[...] = jnp.where((flag_ref[1] > 0) | (step >= 1), u, jnp.zeros_like(u))


def last_kernel(q_ref, u_ref, ug_ref, root_ref, g0, g1, g2, g3, o_ref):
    upd = dot16(u_ref[...], ug_ref[...], 1, 0)
    for q in range(4):
        read = sender((g0, g1, g2, g3), q_ref, q)
        for m in range(4):
            o = 128 * m + 32 * q
            o_ref[o:o + 32, :] = root_ref[o:o + 32, :] + read(m) - upd[o:o + 32, :]


def vmem():
    return pl.BlockSpec(memory_space=pltpu.VMEM)


def smem():
    return pl.BlockSpec(memory_space=pltpu.SMEM)


def call(kernel, outs, n_scalar, n_vector, scratch=(), flops=0, name=None):
    return pl.pallas_call(
        kernel,
        out_shape=outs,
        in_specs=[smem()] * n_scalar + [vmem()] * n_vector,
        out_specs=jax.tree.map(lambda _: vmem(), outs),
        scratch_shapes=list(scratch),
        compiler_params=VM,
        cost_estimate=pl.CostEstimate(flops=flops, transcendentals=0, bytes_accessed=1 << 20),
        name=name,
    )


def sds(shape, dtype=F32):
    return jax.ShapeDtypeStruct(shape, dtype)


CHOL = [pltpu.VMEM((512, 512), F32), pltpu.VMEM((128, 128), F32)]


def exchange(x, axis):
    return lax.all_to_all(x, axis, split_axis=0, concat_axis=0, tiled=True)


def gather(x, axis, n):
    return exchange(jnp.broadcast_to(x[None], (n,) + x.shape), axis)


def in_order(own, near, far, corner, q):
    even = q % 2 == 0
    low = q < 2
    a0, a1 = jnp.where(even, own, near), jnp.where(even, near, own)
    b0, b1 = jnp.where(even, far, corner), jnp.where(even, corner, far)
    return jnp.stack([jnp.where(low, a0, b0), jnp.where(low, a1, b1), jnp.where(low, b0, a0), jnp.where(low, b1, a1)])


def across(x, k):
    return lax.ppermute(x, "col", [(i, i ^ k) for i in range(4)])


def around(x):
    far = across(x, 2)
    return [x, across(x, 1), far, across(far, 1)]


def gather_col(x, q):
    return in_order(*around(x), q)


def from_first_col(x, q):
    sent = [lax.ppermute(x[k], "col", [(0, k)]) for k in (1, 2, 3)]
    return jnp.where(q == 0, x[0], sent[0] + sent[1] + sent[2])


def exchange_col(x, q):
    return in_order(*sent_col(x, q), q)


def sent_col(x, q):
    parts = [lax.dynamic_index_in_dim(x, q ^ k, 0, keepdims=False) for k in range(4)]
    return [parts[0]] + [across(parts[k], k) for k in (1, 2, 3)]


def after(x, *earlier):
    return lax.optimization_barrier((x,) + earlier)[0]


def swap_child(x):
    return lax.ppermute(x, "child", [(0, 1), (1, 0)])


def local(child_fronts, root_front, block_maps):
    front = child_fronts[0]
    child = lax.axis_index("child")
    r = lax.axis_index("row")
    q = lax.axis_index("col")
    blocks = jnp.arange(64, dtype=jnp.int32)
    order = jnp.arange(1, NCB + 1, dtype=jnp.int32)
    inverse = jnp.sum(jnp.where(block_maps[:, :, None] == blocks, order[None, :, None], 0), axis=1) - 1
    mine = jnp.where(child == 0, inverse[0], inverse[1])
    theirs = jnp.where(child == 0, inverse[1], inverse[0])

    def pick(idx):
        return jnp.sum(jnp.where(idx[:, None] == blocks[None, :], mine[None, :], 0), axis=1)

    slot = jnp.arange(64, dtype=jnp.int32)
    half = jnp.where(slot % 4 >= 2, 1 - child, child)
    bulk_idx = pick(32 * half + 2 * (slot // 4) + slot % 2)
    panel_idx = mine[0:4]
    at = q[None]
    four = jnp.arange(4, dtype=jnp.int32)
    col_idx = pick(32 * jnp.where(four >= 2, 1 - child, child) + 2 * r + four % 2)
    row_idx = pick(16 * four + r)

    quarters = front.reshape(2, 4, 32, 1024).transpose(1, 0, 2, 3).reshape(4, 64, 1024)
    raw_top = root_front[0:512].reshape(4, 4, 32, 256).transpose(1, 0, 2, 3).reshape(4, 2, 64, 256)
    pack = from_first_col(jnp.concatenate([quarters, raw_top[:, 0], raw_top[:, 1]], axis=2), q)
    left = pack[:, 0:512]
    top = jnp.concatenate([pack[:, 1024:1280], pack[:, 1280:1536]], axis=0)

    heads = exchange(pack.reshape(16, 4, 1536), "row")
    first, second, corner0, corner1 = lax.optimization_barrier(
        (heads[0:2, :, 0:512], heads[2:4, :, 0:1024], heads[0:1, :, 1024:1536], heads[1:2, :, 1024:1536]))
    d00 = gather(gather_col(first, q).reshape(8, 4, 512), "row", ROWS)
    corner = jnp.concatenate([corner0, corner1], axis=2)
    second = jnp.concatenate([gather_col(second, q).reshape(8, 4, 1024), corner], axis=0)
    second = jnp.broadcast_to(second[None], (ROWS,) + second.shape)
    d00, second = lax.optimization_barrier((d00, second))
    d1 = exchange(second, "row")
    raw_diag = jnp.concatenate([
        jnp.concatenate([d1[:, 8, :, c:c + 256] for c in (o, o + 512)], axis=2).reshape(64, 512) for o in (0, 256)
    ], axis=0)
    raw_diag = jnp.where(child == 0, raw_diag, 0.0)

    y = exchange_col(after(quarters, pack), q)
    panel_y = y[1][:, 0:512]
    placed_panel = call(place_panel_kernel, sds((64, 512)), 1, 1, name="place_panel")(panel_idx, panel_y)

    raw_rows = 0.0
    tile_top = after(root_front[0:512], pack)
    for j in range(2):
        pairs = []
        for g in range(32):
            m = 2 * g + j
            pairs.append((4 * g, (m // 32 * 16 + m % 16) * 4 + m // 16))
        raw_rows += lax.ppermute(tile_top[:, 128 * j:128 * j + 128], ("child", "row", "col"), pairs)
    d00, placed_panel, raw_rows = lax.optimization_barrier((d00, placed_panel, raw_rows))
    raw_rows = raw_rows.T
    inv0, p0, u0 = call(
        head_kernel, (sds((512, 512)), sds((64, 512)), sds((64, 512), BF16)), 0, 2, CHOL, 2 * 10**10, "head")(d00, left)
    f_panel = lax.all_gather(placed_panel, "row").reshape(32, 32, 512)
    u0_all = jnp.broadcast_to(u0.reshape(1, 2, 32, 512), (ROWS, 2, 32, 512))
    d1, u0_all = lax.optimization_barrier((d1, u0_all))
    u0_all = exchange(u0_all, "row").reshape(32, 32, 512)

    below = (r >= 2).astype(jnp.int32)[None]
    p1, u1 = call(
        second_kernel, (sds((64, 512)), sds((64, 512), BF16)), 1, 4,
        [pltpu.VMEM((512, 512), F32)] * 2 + CHOL, 3 * 10**10, "second")(below, d1, inv0, pack[:, 512:1024], u0)
    factor0 = p0.reshape(2, 32, 512)
    u1, u0_all, far0 = lax.optimization_barrier((u1, u0_all, across(factor0, 2)))
    u1_all = gather(u1.reshape(2, 32, 512), "row", ROWS).reshape(32, 32, 512)
    wide = after(jnp.concatenate([y[1], y[2], y[3]], axis=1), u1)
    placed = call(place_kernel, sds((16, 64, 512)), 1, 1, name="place")(bulk_idx, wide)
    factor0 = after(factor0, u1)
    factor0 = in_order(factor0, across(factor0, 1), far0, across(far0, 1), q)
    u1_all, placed, factor0 = lax.optimization_barrier((u1_all, placed, factor0))
    f_bulk = exchange(placed, "row").reshape(32, 32, 512)

    some = sds((4, 32, 1024), BF16)
    u_panel, u_bulk = call(select_kernel, (some, some), 2, 2, name="select")(panel_idx, col_idx, u0_all, u1_all)
    u_panel = around(u_panel)
    u_bulk = after(u_bulk, u_panel[2])
    bulk_far = across(u_bulk, 2)
    z, t = call(panel_kernel, (sds((128, 512)), sds((128, 512))), 3, 7, flops=10**9, name="panel")(
        at, row_idx, panel_idx, u0_all, u1_all, f_panel, *u_panel)
    z, t, bulk_far = lax.optimization_barrier((z, t, bulk_far))
    t = t + raw_diag
    t = t + swap_child(t)
    u_bulk = [u_bulk, across(u_bulk, 1), bulk_far, across(bulk_far, 1)]
    z = exchange_col(z.reshape(4, 32, 512), q).reshape(128, 512) + raw_rows
    z, t, u_bulk, f_bulk = lax.optimization_barrier((z, t, u_bulk, f_bulk))
    z_swapped = swap_child(z)
    z = z + z_swapped
    panel = lax.all_gather(z, "row", tiled=True)
    t_all = around(t.reshape(4, 32, 512))

    half, block = sds((768, 256)), sds((4, 32, 256))
    own, other, first, sent = call(bulk_kernel, (half, half, block, block), 2, 7, flops=2 * 10**9, name="bulk")(
        at, panel_idx, u0_all, u1_all, f_bulk, *u_bulk)
    head_cols = top.reshape(4, 32, 256) + first + swap_child(sent)
    t_all, z, other, head_cols = lax.optimization_barrier((t_all, z, other, head_cols))
    factor1 = p1.reshape(2, 32, 512)
    far1 = across(after(factor1, other), 2)
    head_far = across(head_cols, 2)
    inv_root = call(root_kernel, sds((512, 512)), 1, 4, CHOL, 2 * 10**10, "root")(at, *t_all)
    got, inv_root, far1, head_far = lax.optimization_barrier((swap_child(other), inv_root, far1, head_far))
    spread = call(spread_kernel, sds((64, 32, 256)), 2, 2, name="spread")(
        mine, theirs, own.reshape(24, 32, 256), got.reshape(24, 32, 256))
    arrived = sent_col(spread.reshape(4, 16, 32, 256), q)
    head_cols = in_order(head_cols, across(head_cols, 1), head_far, across(head_far, 1), q)

    flags = jnp.stack([16 * child + r >= 2, q > 0]).astype(jnp.int32)
    rows = pl.BlockSpec((512, 512), lambda i: (i, 0))
    whole = pl.BlockSpec((512, 512), lambda i: (0, 0))
    narrow = pl.BlockSpec((512, 256), lambda i: (i, 0))
    fixed = pl.BlockSpec((512, 256), lambda i: (0, 0))
    root_factor, u_root, u_cols = pl.pallas_call(
        factor_kernel,
        out_shape=(sds((2048, 512)), sds((2048, 512), BF16), sds((512, 256), BF16)),
        grid=(4,),
        in_specs=[smem(), rows, whole, pl.BlockSpec((4, 4, 32, 256), lambda i: (0, 0, 0, 0))],
        out_specs=(rows, rows, fixed),
        scratch_shapes=[pltpu.VMEM((512, 256), F32)],
        compiler_params=VM,
        cost_estimate=pl.CostEstimate(flops=10**10, transcendentals=0, bytes_accessed=1 << 20),
        name="factor",
    )(flags, panel, inv_root, head_cols)
    arrived, u_root = lax.optimization_barrier((arrived, u_root))
    factor1 = after(factor1, u_root)
    factor1 = in_order(factor1, across(factor1, 1), far1, across(after(far1, u_root), 1), q)
    child_factor = jnp.concatenate([factor0, factor1], axis=3).transpose(1, 0, 2, 3).reshape(1, 256, 1024)
    trailing = pl.pallas_call(
        last_kernel,
        out_shape=sds((2048, 256)),
        grid=(4,),
        in_specs=[smem(), rows, fixed, narrow] + [pl.BlockSpec((4, 32, 256), lambda i: (i, 0, 0))] * 4,
        out_specs=narrow,
        compiler_params=VM,
        name="last",
    )(at, u_root, u_cols, root_front, *arrived)
    return (child_factor, root_factor, trailing)


def solution(mesh):
    return jax.shard_map(
        local,
        mesh=mesh,
        in_specs=(P("child", "row", "col"), P("col", ("child", "row")), P()),
        out_specs=(P("child", "row", None), P("col", None), P("col", ("child", "row"))),
        check_vma=False,
    )
```

```python
import functools

import jax
import jax.numpy as jnp
from jax import lax
from jax.experimental import pallas as pl
from jax.experimental.pallas import tpu as pltpu
from jax.sharding import PartitionSpec as P

F32 = jnp.float32
BF16 = jnp.bfloat16
HI = lax.Precision.HIGHEST
ROWS, COLS = 16, 4
NCB = 24
VM = pltpu.CompilerParams(vmem_limit_bytes=56 << 20)


def lane_copy(v, k):
    return jnp.broadcast_to(v[:, k:k + 1], (8, 128))


def sub_copy(v, k):
    return jnp.broadcast_to(v[k:k + 1, :], (8, 128))


def dot(a, b, ca, cb):
    return lax.dot_general(a, b, (((ca,), (cb,)), ((), ())), precision=HI, preferred_element_type=F32)


def dot16(a, b, ca, cb):
    return lax.dot_general(a, b, (((ca,), (cb,)), ((), ())), preferred_element_type=F32)


def inverse_factor128(block):
    lane = lax.broadcasted_iota(jnp.int32, (8, 128), 1)
    sub = lax.broadcasted_iota(jnp.int32, (8, 128), 0)
    w = [block[8 * t:8 * t + 8, :] for t in range(16)]
    for s in range(16):
        c = {t: [lane_copy(w[t], 8 * s + j) for j in range(8)] for t in range(s, 16)}
        inside = (lane >= 8 * s) & (lane < 8 * s + 8)
        w[s] = jnp.where(inside, (lane - 8 * s == sub).astype(F32), w[s])
        for t in range(s + 1, 16):
            w[t] = jnp.where(inside, 0.0, w[t])
        for j in range(8):
            scale = lax.rsqrt(sub_copy(c[s][j], j))
            pivot_row = sub_copy(w[s], j) * scale
            ahead = {k: sub_copy(c[s][j], k) * scale for k in range(j + 1, 8)}
            for t in range(s, 16):
                l = c[t][j] * scale
                if t == s:
                    l = jnp.where(sub > j, l, 0.0)
                for k in range(j + 1, 8):
                    c[t][k] = c[t][k] - l * ahead[k]
                w[t] = w[t] - l * pivot_row
            w[s] = jnp.where(sub == j, pivot_row, w[s])
    return jnp.concatenate([jnp.where(lane <= sub + 8 * t, w[t], 0.0) for t in range(16)], axis=0)


def inverse_factor512(a, b, g):
    n = 512
    b[...] = jnp.zeros((n, n), F32)

    def block(k, carry):
        o = pl.multiple_of(128 * k, 128)
        g[...] = inverse_factor128(a[pl.ds(o, 128), pl.ds(o, 128)])
        for step in range(n // 128):
            pl.when(k == step)(functools.partial(outer, 128 * step))
        return carry

    def outer(o):
        inv = g[...]
        if o > 0:
            b[o:o + 128, 0:o] = dot(inv, b[o:o + 128, 0:o], 1, 0)
        b[o:o + 128, o:o + 128] = inv
        r = o + 128
        if r < n:
            l = dot(a[r:n, o:o + 128], inv, 1, 1)
            a[r:n, r:n] = a[r:n, r:n] - dot(l, l, 1, 1)
            b[r:n, 0:r] = b[r:n, 0:r] - dot(l, b[o:o + 128, 0:r], 1, 0)

    lax.fori_loop(0, n // 128, block, 0)


def head_rows():
    for s in range(16):
        for q in range(4):
            for h in range(2):
                yield 256 * h + 128 * (s // 8) + 32 * q + 4 * (s % 8), (s, 2 * q + h)


def head_kernel(d_ref, c_ref, inv_ref, p_ref, u_ref, a, g):
    for o, piece in head_rows():
        a[o:o + 4, :] = d_ref[piece]
    inverse_factor512(a, inv_ref, g)
    p = dot(c_ref[...], inv_ref[...], 1, 1)
    p_ref[...] = p
    u_ref[...] = p.astype(BF16)


def second_kernel(mask_ref, d_ref, inv0_ref, c_ref, u0_ref, p_ref, u_ref, d10, inv1, a, g):
    for o, (s, i) in head_rows():
        d10[o:o + 4, :] = d_ref[s, i, :, 0:512]
        a[o:o + 4, :] = d_ref[s, i, :, 512:1024]
    u10 = dot(d10[...], inv0_ref[...], 1, 1).astype(BF16)
    a[...] = a[...] - dot16(u10, u10, 1, 1)
    c1 = c_ref[...] - dot16(u0_ref[...], u10, 1, 1)
    inverse_factor512(a, inv1, g)
    p1 = dot(c1, inv1[...], 1, 1)
    p_ref[...] = jnp.where(mask_ref[0] > 0, p1, 0.0)
    u_ref[...] = p1.astype(BF16)


def place(b, y_ref):
    col = pl.multiple_of(jnp.maximum(b, 0) * 128, 128)
    return jnp.where(b >= 0, y_ref[:, pl.ds(col, 128)], 0.0)


def place_panel_kernel(panel_ref, y_ref, p_ref):
    for m in range(4):
        p_ref[:, 128 * m:128 * m + 128] = place(panel_ref[m], y_ref)


def place_kernel(bulk_ref, y_ref, o_ref):
    def one(slot, carry):
        out = pl.multiple_of((slot % 4) * 128, 128)
        o_ref[slot // 4, :, pl.ds(out, 128)] = place(bulk_ref[slot], y_ref)
        return carry

    lax.fori_loop(0, 64, one, 0)


def picked(b, ref):
    v = ref[jnp.maximum(b, 0) + 8]
    return jnp.where(b >= 0, v, jnp.zeros_like(v))


def sender(refs, q_ref, p):
    j = p ^ q_ref[0]

    def read(i):
        x, near, far, corner = [ref[i] for ref in refs]
        return jnp.where(j >= 2, jnp.where(j == 3, corner, far), jnp.where(j == 1, near, x))

    return read


def columns_of(refs, q_ref):
    return jnp.concatenate([sender(refs, q_ref, q)(m) for m in range(4) for q in range(4)], axis=0)


def select_kernel(panel_ref, bulk_ref, u0_ref, u1_ref, p_ref, o_ref):
    for ref, out in ((panel_ref, p_ref), (bulk_ref, o_ref)):
        for i in range(4):
            out[i, :, 0:512] = picked(ref[i], u0_ref)
            out[i, :, 512:1024] = picked(ref[i], u1_ref)


def panel_kernel(q_ref, rows_ref, panel_ref, u0_ref, u1_ref, fp_ref, c0, c1, c2, c3, z_ref, t_ref):
    upan = columns_of((c0, c1, c2, c3), q_ref)
    for ref, out in ((panel_ref, t_ref), (rows_ref, z_ref)):
        f, u0, u1 = [jnp.concatenate([picked(ref[i], x) for i in range(4)], axis=0) for x in (fp_ref, u0_ref, u1_ref)]
        out[...] = f - dot16(jnp.concatenate([u0, u1], axis=1), upan, 1, 1)


def corner_kernel(q_ref, panel_ref, u0_ref, u1_ref, f_ref, c0, c1, c2, c3, first_ref, send_ref):
    f, u0, u1 = [jnp.concatenate([picked(panel_ref[i], x) for i in range(4)], axis=0) for x in (f_ref, u0_ref, u1_ref)]
    s = f - dot16(jnp.concatenate([u0, u1], axis=1), columns_of((c0, c1, c2, c3), q_ref), 1, 1)
    first_ref[...] = s[:, 0:256]
    send_ref[...] = s[:, 256:512]


def bulk_kernel(q_ref, u0_ref, u1_ref, f_ref, c0, c1, c2, c3, own_ref, other_ref):
    rows = jnp.concatenate([u0_ref[8:32].reshape(768, 512), u1_ref[8:32].reshape(768, 512)], axis=1)
    s = f_ref[8:32].reshape(768, 512) - dot16(rows, columns_of((c0, c1, c2, c3), q_ref), 1, 1)
    own_ref[...] = s[:, 0:256]
    other_ref[...] = s[:, 256:512]


def root_kernel(q_ref, t0, t1, t2, t3, inv_ref, a, g):
    for q in range(4):
        read = sender((t0, t1, t2, t3), q_ref, q)
        for m in range(4):
            a[128 * m + 32 * q:128 * m + 32 * q + 32, :] = read(m)
    inverse_factor512(a, inv_ref, g)


def spread_kernel(mine_ref, theirs_ref, own_ref, got_ref, o_ref):
    def one(m, carry):
        i = mine_ref[m]
        j = theirs_ref[m]
        v = own_ref[jnp.maximum(i, 0)]
        w = got_ref[jnp.maximum(j, 0)]
        o_ref[m] = jnp.where(i >= 0, v, 0.0) + jnp.where(j >= 0, w, 0.0)
        return carry

    lax.fori_loop(0, 64, one, 0)


def factor_kernel(flag_ref, panel_ref, inv_ref, cp_ref, p_ref, u_ref, ug_ref, cps):
    step = pl.program_id(0)

    @pl.when(step == 0)
    def _():
        for q in range(4):
            for m in range(4):
                cps[128 * m + 32 * q:128 * m + 32 * q + 32, :] = cp_ref[q, m]
        v = dot(inv_ref[...], cps[...], 1, 0).astype(BF16)
        ug_ref[...] = jnp.where(flag_ref[0] > 0, v, jnp.zeros_like(v))

    p = dot(panel_ref[...], inv_ref[...], 1, 1)
    p_ref[...] = p
    u = p.astype(BF16)
    u_ref[...] = jnp.where((flag_ref[1] > 0) | (step >= 1), u, jnp.zeros_like(u))


def last_kernel(q_ref, u_ref, ug_ref, root_ref, g0, g1, g2, g3, o_ref):
    upd = dot16(u_ref[...], ug_ref[...], 1, 0)
    for q in range(4):
        read = sender((g0, g1, g2, g3), q_ref, q)
        for m in range(4):
            o = 128 * m + 32 * q
            o_ref[o:o + 32, :] = root_ref[o:o + 32, :] + read(m) - upd[o:o + 32, :]


def vmem():
    return pl.BlockSpec(memory_space=pltpu.VMEM)


def smem():
    return pl.BlockSpec(memory_space=pltpu.SMEM)


def call(kernel, outs, n_scalar, n_vector, scratch=(), flops=0, name=None):
    return pl.pallas_call(
        kernel,
        out_shape=outs,
        in_specs=[smem()] * n_scalar + [vmem()] * n_vector,
        out_specs=jax.tree.map(lambda _: vmem(), outs),
        scratch_shapes=list(scratch),
        compiler_params=VM,
        cost_estimate=pl.CostEstimate(flops=flops, transcendentals=0, bytes_accessed=1 << 20),
        name=name,
    )


def sds(shape, dtype=F32):
    return jax.ShapeDtypeStruct(shape, dtype)


CHOL = [pltpu.VMEM((512, 512), F32), pltpu.VMEM((128, 128), F32)]


def exchange(x, axis):
    return lax.all_to_all(x, axis, split_axis=0, concat_axis=0, tiled=True)


def gather(x, axis, n):
    return exchange(jnp.broadcast_to(x[None], (n,) + x.shape), axis)


def in_order(own, near, far, corner, q):
    even = q % 2 == 0
    low = q < 2
    a0, a1 = jnp.where(even, own, near), jnp.where(even, near, own)
    b0, b1 = jnp.where(even, far, corner), jnp.where(even, corner, far)
    return jnp.stack([jnp.where(low, a0, b0), jnp.where(low, a1, b1), jnp.where(low, b0, a0), jnp.where(low, b1, a1)])


def across(x, k):
    return lax.ppermute(x, "col", [(i, i ^ k) for i in range(4)])


def around(x):
    far = across(x, 2)
    return [x, across(x, 1), far, across(far, 1)]


def gather_col(x, q):
    return in_order(*around(x), q)


def from_first_col(x, q):
    sent = [lax.ppermute(x[k], "col", [(0, k)]) for k in (1, 2, 3)]
    return jnp.where(q == 0, x[0], sent[0] + sent[1] + sent[2])


def exchange_col(x, q):
    return in_order(*sent_col(x, q), q)


def sent_col(x, q):
    parts = [lax.dynamic_index_in_dim(x, q ^ k, 0, keepdims=False) for k in range(4)]
    return [parts[0]] + [across(parts[k], k) for k in (1, 2, 3)]


def after(x, *earlier):
    return lax.optimization_barrier((x,) + earlier)[0]


def swap_child(x):
    return lax.ppermute(x, "child", [(0, 1), (1, 0)])


def local(child_fronts, root_front, block_maps):
    front = child_fronts[0]
    child = lax.axis_index("child")
    r = lax.axis_index("row")
    q = lax.axis_index("col")
    blocks = jnp.arange(64, dtype=jnp.int32)
    order = jnp.arange(1, NCB + 1, dtype=jnp.int32)
    inverse = jnp.sum(jnp.where(block_maps[:, :, None] == blocks, order[None, :, None], 0), axis=1) - 1
    mine = jnp.where(child == 0, inverse[0], inverse[1])
    theirs = jnp.where(child == 0, inverse[1], inverse[0])

    def pick(idx):
        return jnp.sum(jnp.where(idx[:, None] == blocks[None, :], mine[None, :], 0), axis=1)

    slot = jnp.arange(64, dtype=jnp.int32)
    half = jnp.where(slot % 4 >= 2, 1 - child, child)
    bulk_idx = pick(32 * half + 2 * (slot // 4) + slot % 2)
    panel_idx = mine[0:4]
    at = q[None]
    four = jnp.arange(4, dtype=jnp.int32)
    col_idx = pick(32 * jnp.where(four >= 2, 1 - child, child) + 2 * r + four % 2)
    row_idx = pick(16 * four + r)

    quarters = front.reshape(2, 4, 32, 1024).transpose(1, 0, 2, 3).reshape(4, 64, 1024)
    raw_top = root_front[0:512].reshape(4, 4, 32, 256).transpose(1, 0, 2, 3).reshape(4, 2, 64, 256)
    pack = from_first_col(jnp.concatenate([quarters, raw_top[:, 0], raw_top[:, 1]], axis=2), q)
    left = pack[:, 0:512]
    top = jnp.concatenate([pack[:, 1024:1280], pack[:, 1280:1536]], axis=0)

    heads = exchange(pack.reshape(16, 4, 1536), "row")
    first, second, corner0, corner1 = lax.optimization_barrier(
        (heads[0:2, :, 0:512], heads[2:4, :, 0:1024], heads[0:1, :, 1024:1536], heads[1:2, :, 1024:1536]))
    d00 = gather(gather_col(first, q).reshape(8, 4, 512), "row", ROWS)
    corner = jnp.concatenate([corner0, corner1], axis=2)
    second = jnp.concatenate([gather_col(second, q).reshape(8, 4, 1024), corner], axis=0)
    second = jnp.broadcast_to(second[None], (ROWS,) + second.shape)
    d00, second = lax.optimization_barrier((d00, second))
    d1 = exchange(second, "row")
    raw_diag = jnp.concatenate([
        jnp.concatenate([d1[:, 8, :, c:c + 256] for c in (o, o + 512)], axis=2).reshape(64, 512) for o in (0, 256)
    ], axis=0)
    raw_diag = jnp.where(child == 0, raw_diag, 0.0)

    y = exchange_col(after(quarters, pack), q)
    panel_y = y[1][:, 0:512]
    placed_panel = call(place_panel_kernel, sds((64, 512)), 1, 1, name="place_panel")(panel_idx, panel_y)

    d00, placed_panel = lax.optimization_barrier((d00, placed_panel))
    inv0, p0, u0 = call(
        head_kernel, (sds((512, 512)), sds((64, 512)), sds((64, 512), BF16)), 0, 2, CHOL, 2 * 10**10, "head")(d00, left)
    f_panel = lax.all_gather(placed_panel, "row").reshape(32, 32, 512)
    u0_all = jnp.broadcast_to(u0.reshape(1, 2, 32, 512), (ROWS, 2, 32, 512))
    d1, u0_all = lax.optimization_barrier((d1, u0_all))
    u0_all = exchange(u0_all, "row").reshape(32, 32, 512)

    below = (r >= 2).astype(jnp.int32)[None]
    p1, u1 = call(
        second_kernel, (sds((64, 512)), sds((64, 512), BF16)), 1, 4,
        [pltpu.VMEM((512, 512), F32)] * 2 + CHOL, 3 * 10**10, "second")(below, d1, inv0, pack[:, 512:1024], u0)
    factor0 = p0.reshape(2, 32, 512)
    u1, u0_all, far0 = lax.optimization_barrier((u1, u0_all, across(factor0, 2)))
    u1_all = gather(u1.reshape(2, 32, 512), "row", ROWS).reshape(32, 32, 512)
    wide = after(jnp.concatenate([y[1], y[2], y[3]], axis=1), u1)
    placed = call(place_kernel, sds((16, 64, 512)), 1, 1, name="place")(bulk_idx, wide)
    factor0 = after(factor0, u1)
    factor0 = in_order(factor0, across(factor0, 1), far0, across(far0, 1), q)
    raw_rows = 0.0
    tile_top = after(root_front[0:512], u1)
    for j in range(2):
        pairs = []
        for g in range(32):
            m = 2 * g + j
            pairs.append((4 * g, (m // 32 * 16 + m % 16) * 4 + m // 16))
        raw_rows += lax.ppermute(tile_top[:, 128 * j:128 * j + 128], ("child", "row", "col"), pairs)
    u1_all, placed, factor0, raw_rows = lax.optimization_barrier((u1_all, placed, factor0, raw_rows))
    raw_rows = raw_rows.T
    f_bulk = exchange(placed, "row").reshape(32, 32, 512)

    some = sds((4, 32, 1024), BF16)
    u_panel, u_bulk = call(select_kernel, (some, some), 2, 2, name="select")(panel_idx, col_idx, u0_all, u1_all)
    u_panel = around(u_panel)
    u_bulk = after(u_bulk, u_panel[2])
    bulk_far = across(u_bulk, 2)
    z, t = call(panel_kernel, (sds((128, 512)), sds((128, 512))), 3, 7, flops=10**9, name="panel")(
        at, row_idx, panel_idx, u0_all, u1_all, f_panel, *u_panel)
    z, t, bulk_far = lax.optimization_barrier((z, t, bulk_far))
    t = t + raw_diag
    t = t + swap_child(t)
    u_bulk = [u_bulk, across(u_bulk, 1), bulk_far, across(bulk_far, 1)]
    z = exchange_col(z.reshape(4, 32, 512), q).reshape(128, 512) + raw_rows
    z, t, u_bulk, f_bulk = lax.optimization_barrier((z, t, u_bulk, f_bulk))
    z_swapped = swap_child(z)
    z = z + z_swapped
    panel = lax.all_gather(z, "row", tiled=True)
    t_all = around(t.reshape(4, 32, 512))

    half, block = sds((768, 256)), sds((128, 256))
    first, sent = call(corner_kernel, (block, block), 2, 7, flops=10**9, name="corner")(
        at, panel_idx, u0_all, u1_all, f_bulk, *u_bulk)
    own, other = call(bulk_kernel, (half, half), 1, 7, flops=4 * 10**9, name="bulk")(
        at, u0_all, u1_all, after(f_bulk, sent), *u_bulk)
    head_cols = (top + first + swap_child(sent)).reshape(4, 32, 256)
    t_all, z, other, head_cols = lax.optimization_barrier((t_all, z, other, head_cols))
    factor1 = p1.reshape(2, 32, 512)
    far1 = across(after(factor1, other), 2)
    head_far = across(head_cols, 2)
    inv_root = call(root_kernel, sds((512, 512)), 1, 4, CHOL, 2 * 10**10, "root")(at, *t_all)
    got, inv_root, far1, head_far = lax.optimization_barrier((swap_child(other), inv_root, far1, head_far))
    spread = call(spread_kernel, sds((64, 32, 256)), 2, 2, name="spread")(
        mine, theirs, own.reshape(24, 32, 256), got.reshape(24, 32, 256))
    arrived = sent_col(spread.reshape(4, 16, 32, 256), q)
    head_cols = in_order(head_cols, across(head_cols, 1), head_far, across(head_far, 1), q)

    flags = jnp.stack([16 * child + r >= 2, q > 0]).astype(jnp.int32)
    rows = pl.BlockSpec((512, 512), lambda i: (i, 0))
    whole = pl.BlockSpec((512, 512), lambda i: (0, 0))
    narrow = pl.BlockSpec((512, 256), lambda i: (i, 0))
    fixed = pl.BlockSpec((512, 256), lambda i: (0, 0))
    root_factor, u_root, u_cols = pl.pallas_call(
        factor_kernel,
        out_shape=(sds((2048, 512)), sds((2048, 512), BF16), sds((512, 256), BF16)),
        grid=(4,),
        in_specs=[smem(), rows, whole, pl.BlockSpec((4, 4, 32, 256), lambda i: (0, 0, 0, 0))],
        out_specs=(rows, rows, fixed),
        scratch_shapes=[pltpu.VMEM((512, 256), F32)],
        compiler_params=VM,
        cost_estimate=pl.CostEstimate(flops=10**10, transcendentals=0, bytes_accessed=1 << 20),
        name="factor",
    )(flags, panel, inv_root, head_cols)
    arrived, u_root = lax.optimization_barrier((arrived, u_root))
    factor1 = after(factor1, u_root)
    factor1 = in_order(factor1, across(factor1, 1), far1, across(after(far1, u_root), 1), q)
    child_factor = jnp.concatenate([factor0, factor1], axis=3).transpose(1, 0, 2, 3).reshape(1, 256, 1024)
    trailing = pl.pallas_call(
        last_kernel,
        out_shape=sds((2048, 256)),
        grid=(4,),
        in_specs=[smem(), rows, fixed, narrow] + [pl.BlockSpec((4, 32, 256), lambda i: (i, 0, 0))] * 4,
        out_specs=narrow,
        compiler_params=VM,
        name="last",
    )(at, u_root, u_cols, root_front, *arrived)
    return (child_factor, root_factor, trailing)


def solution(mesh):
    return jax.shard_map(
        local,
        mesh=mesh,
        in_specs=(P("child", "row", "col"), P("col", ("child", "row")), P()),
        out_specs=(P("child", "row", None), P("col", None), P("col", ("child", "row"))),
        check_vma=False,
    )
```

```python
import functools

import jax
import jax.numpy as jnp
from jax import lax
from jax.experimental import pallas as pl
from jax.experimental.pallas import tpu as pltpu
from jax.sharding import PartitionSpec as P

F32 = jnp.float32
BF16 = jnp.bfloat16
HI = lax.Precision.HIGHEST
ROWS, COLS = 16, 4
NCB = 24
VM = pltpu.CompilerParams(vmem_limit_bytes=56 << 20)


def lane_copy(v, k):
    return jnp.broadcast_to(v[:, k:k + 1], (8, 128))


def sub_copy(v, k):
    return jnp.broadcast_to(v[k:k + 1, :], (8, 128))


def dot(a, b, ca, cb):
    return lax.dot_general(a, b, (((ca,), (cb,)), ((), ())), precision=HI, preferred_element_type=F32)


def dot16(a, b, ca, cb):
    return lax.dot_general(a, b, (((ca,), (cb,)), ((), ())), preferred_element_type=F32)


def inverse_factor128(block):
    lane = lax.broadcasted_iota(jnp.int32, (8, 128), 1)
    sub = lax.broadcasted_iota(jnp.int32, (8, 128), 0)
    w = [block[8 * t:8 * t + 8, :] for t in range(16)]
    for s in range(16):
        c = {t: [lane_copy(w[t], 8 * s + j) for j in range(8)] for t in range(s, 16)}
        inside = (lane >= 8 * s) & (lane < 8 * s + 8)
        w[s] = jnp.where(inside, (lane - 8 * s == sub).astype(F32), w[s])
        for t in range(s + 1, 16):
            w[t] = jnp.where(inside, 0.0, w[t])
        for j in range(8):
            scale = lax.rsqrt(sub_copy(c[s][j], j))
            pivot_row = sub_copy(w[s], j) * scale
            ahead = {k: sub_copy(c[s][j], k) * scale for k in range(j + 1, 8)}
            for t in range(s, 16):
                l = c[t][j] * scale
                if t == s:
                    l = jnp.where(sub > j, l, 0.0)
                for k in range(j + 1, 8):
                    c[t][k] = c[t][k] - l * ahead[k]
                w[t] = w[t] - l * pivot_row
            w[s] = jnp.where(sub == j, pivot_row, w[s])
    return jnp.concatenate([jnp.where(lane <= sub + 8 * t, w[t], 0.0) for t in range(16)], axis=0)


def inverse_factor512(a, b, g):
    n = 512
    b[...] = jnp.zeros((n, n), F32)

    def block(k, carry):
        o = pl.multiple_of(128 * k, 128)
        g[...] = inverse_factor128(a[pl.ds(o, 128), pl.ds(o, 128)])
        for step in range(n // 128):
            pl.when(k == step)(functools.partial(outer, 128 * step))
        return carry

    def outer(o):
        inv = g[...]
        if o > 0:
            b[o:o + 128, 0:o] = dot(inv, b[o:o + 128, 0:o], 1, 0)
        b[o:o + 128, o:o + 128] = inv
        r = o + 128
        if r < n:
            l = dot(a[r:n, o:o + 128], inv, 1, 1)
            a[r:n, r:n] = a[r:n, r:n] - dot(l, l, 1, 1)
            b[r:n, 0:r] = b[r:n, 0:r] - dot(l, b[o:o + 128, 0:r], 1, 0)

    lax.fori_loop(0, n // 128, block, 0)


def head_rows():
    for s in range(16):
        for q in range(4):
            for h in range(2):
                yield 256 * h + 128 * (s // 8) + 32 * q + 4 * (s % 8), (s, 2 * q + h)


def head_kernel(d_ref, c_ref, inv_ref, p_ref, u_ref, a, g):
    for o, piece in head_rows():
        a[o:o + 4, :] = d_ref[piece]
    inverse_factor512(a, inv_ref, g)
    p = dot(c_ref[...], inv_ref[...], 1, 1)
    p_ref[...] = p
    u_ref[...] = jnp.broadcast_to(p.astype(BF16)[None], u_ref.shape)


def second_kernel(mask_ref, d_ref, inv0_ref, c_ref, u0_ref, p_ref, u_ref, d10, inv1, a, g):
    for o, (s, i) in head_rows():
        d10[o:o + 4, :] = d_ref[s, i, :, 0:512]
        a[o:o + 4, :] = d_ref[s, i, :, 512:1024]
    u10 = dot(d10[...], inv0_ref[...], 1, 1).astype(BF16)
    a[...] = a[...] - dot16(u10, u10, 1, 1)
    c1 = c_ref[...] - dot16(u0_ref[0], u10, 1, 1)
    inverse_factor512(a, inv1, g)
    p1 = dot(c1, inv1[...], 1, 1)
    p_ref[...] = jnp.where(mask_ref[0] > 0, p1, 0.0)
    u_ref[...] = jnp.broadcast_to(p1.astype(BF16)[None], u_ref.shape)


def place(b, y_ref):
    col = pl.multiple_of(jnp.maximum(b, 0) * 128, 128)
    return jnp.where(b >= 0, y_ref[:, pl.ds(col, 128)], 0.0)


def place_panel_kernel(panel_ref, y_ref, p_ref):
    for m in range(4):
        p_ref[:, 128 * m:128 * m + 128] = place(panel_ref[m], y_ref)


def place_kernel(bulk_ref, y_ref, o_ref):
    def one(slot, carry):
        out = pl.multiple_of((slot % 4) * 128, 128)
        o_ref[slot // 4, :, pl.ds(out, 128)] = place(bulk_ref[slot], y_ref)
        return carry

    lax.fori_loop(0, 64, one, 0)


def picked(b, ref):
    v = ref[jnp.maximum(b, 0) + 8]
    return jnp.where(b >= 0, v, jnp.zeros_like(v))


def sender(refs, q_ref, p):
    j = p ^ q_ref[0]

    def read(i):
        x, near, far, corner = [ref[i] for ref in refs]
        return jnp.where(j >= 2, jnp.where(j == 3, corner, far), jnp.where(j == 1, near, x))

    return read


def columns_of(refs, q_ref):
    return jnp.concatenate([sender(refs, q_ref, q)(m) for m in range(4) for q in range(4)], axis=0)


def select_kernel(panel_ref, bulk_ref, u0_ref, u1_ref, p_ref, o_ref):
    for ref, out in ((panel_ref, p_ref), (bulk_ref, o_ref)):
        for i in range(4):
            out[i, :, 0:512] = picked(ref[i], u0_ref)
            out[i, :, 512:1024] = picked(ref[i], u1_ref)


def panel_kernel(q_ref, rows_ref, panel_ref, u0_ref, u1_ref, fp_ref, c0, c1, c2, c3, z_ref, t_ref):
    upan = columns_of((c0, c1, c2, c3), q_ref)
    for ref, out in ((panel_ref, t_ref), (rows_ref, z_ref)):
        f, u0, u1 = [jnp.concatenate([picked(ref[i], x) for i in range(4)], axis=0) for x in (fp_ref, u0_ref, u1_ref)]
        out[...] = f - dot16(jnp.concatenate([u0, u1], axis=1), upan, 1, 1)


def corner_kernel(q_ref, panel_ref, u0_ref, u1_ref, f_ref, c0, c1, c2, c3, first_ref, send_ref):
    f, u0, u1 = [jnp.concatenate([picked(panel_ref[i], x) for i in range(4)], axis=0) for x in (f_ref, u0_ref, u1_ref)]
    s = f - dot16(jnp.concatenate([u0, u1], axis=1), columns_of((c0, c1, c2, c3), q_ref), 1, 1)
    first_ref[...] = s[:, 0:256]
    send_ref[...] = s[:, 256:512]


def bulk_kernel(q_ref, u0_ref, u1_ref, f_ref, c0, c1, c2, c3, own_ref, other_ref):
    rows = jnp.concatenate([u0_ref[8:32].reshape(768, 512), u1_ref[8:32].reshape(768, 512)], axis=1)
    s = f_ref[8:32].reshape(768, 512) - dot16(rows, columns_of((c0, c1, c2, c3), q_ref), 1, 1)
    own_ref[...] = s[:, 0:256]
    other_ref[...] = s[:, 256:512]


def root_kernel(q_ref, t0, t1, t2, t3, inv_ref, a, g):
    for q in range(4):
        read = sender((t0, t1, t2, t3), q_ref, q)
        for m in range(4):
            a[128 * m + 32 * q:128 * m + 32 * q + 32, :] = read(m)
    inverse_factor512(a, inv_ref, g)


def spread_kernel(mine_ref, theirs_ref, own_ref, got_ref, o_ref):
    def one(m, carry):
        i = mine_ref[m]
        j = theirs_ref[m]
        v = own_ref[jnp.maximum(i, 0)]
        w = got_ref[jnp.maximum(j, 0)]
        o_ref[m] = jnp.where(i >= 0, v, 0.0) + jnp.where(j >= 0, w, 0.0)
        return carry

    lax.fori_loop(0, 64, one, 0)


def factor_kernel(flag_ref, panel_ref, inv_ref, cp_ref, p_ref, u_ref, ug_ref, cps):
    step = pl.program_id(0)

    @pl.when(step == 0)
    def _():
        for q in range(4):
            for m in range(4):
                cps[128 * m + 32 * q:128 * m + 32 * q + 32, :] = cp_ref[q, m]
        v = dot(inv_ref[...], cps[...], 1, 0).astype(BF16)
        ug_ref[...] = jnp.where(flag_ref[0] > 0, v, jnp.zeros_like(v))

    p = dot(panel_ref[...], inv_ref[...], 1, 1)
    p_ref[...] = p
    u = p.astype(BF16)
    u_ref[...] = jnp.where((flag_ref[1] > 0) | (step >= 1), u, jnp.zeros_like(u))


def last_kernel(q_ref, u_ref, ug_ref, root_ref, g0, g1, g2, g3, o_ref):
    upd = dot16(u_ref[...], ug_ref[...], 1, 0)
    for q in range(4):
        read = sender((g0, g1, g2, g3), q_ref, q)
        for m in range(4):
            o = 128 * m + 32 * q
            o_ref[o:o + 32, :] = root_ref[o:o + 32, :] + read(m) - upd[o:o + 32, :]


def vmem():
    return pl.BlockSpec(memory_space=pltpu.VMEM)


def smem():
    return pl.BlockSpec(memory_space=pltpu.SMEM)


def call(kernel, outs, n_scalar, n_vector, scratch=(), flops=0, name=None):
    return pl.pallas_call(
        kernel,
        out_shape=outs,
        in_specs=[smem()] * n_scalar + [vmem()] * n_vector,
        out_specs=jax.tree.map(lambda _: vmem(), outs),
        scratch_shapes=list(scratch),
        compiler_params=VM,
        cost_estimate=pl.CostEstimate(flops=flops, transcendentals=0, bytes_accessed=1 << 20),
        name=name,
    )


def sds(shape, dtype=F32):
    return jax.ShapeDtypeStruct(shape, dtype)


CHOL = [pltpu.VMEM((512, 512), F32), pltpu.VMEM((128, 128), F32)]


def exchange(x, axis):
    return lax.all_to_all(x, axis, split_axis=0, concat_axis=0, tiled=True)


def gather(x, axis, n):
    return exchange(jnp.broadcast_to(x[None], (n,) + x.shape), axis)


def in_order(own, near, far, corner, q):
    even = q % 2 == 0
    low = q < 2
    a0, a1 = jnp.where(even, own, near), jnp.where(even, near, own)
    b0, b1 = jnp.where(even, far, corner), jnp.where(even, corner, far)
    return jnp.stack([jnp.where(low, a0, b0), jnp.where(low, a1, b1), jnp.where(low, b0, a0), jnp.where(low, b1, a1)])


def across(x, k):
    return lax.ppermute(x, "col", [(i, i ^ k) for i in range(4)])


def around(x):
    far = across(x, 2)
    return [x, across(x, 1), far, across(far, 1)]


def gather_col(x, q):
    return in_order(*around(x), q)


def from_first_col(x, q):
    sent = [lax.ppermute(x[k], "col", [(0, k)]) for k in (1, 2, 3)]
    return jnp.where(q == 0, x[0], sent[0] + sent[1] + sent[2])


def exchange_col(x, q):
    return in_order(*sent_col(x, q), q)


def sent_col(x, q):
    parts = [lax.dynamic_index_in_dim(x, q ^ k, 0, keepdims=False) for k in range(4)]
    return [parts[0]] + [across(parts[k], k) for k in (1, 2, 3)]


def after(x, *earlier):
    return lax.optimization_barrier((x,) + earlier)[0]


def swap_child(x):
    return lax.ppermute(x, "child", [(0, 1), (1, 0)])


def local(child_fronts, root_front, block_maps):
    front = child_fronts[0]
    child = lax.axis_index("child")
    r = lax.axis_index("row")
    q = lax.axis_index("col")
    blocks = jnp.arange(64, dtype=jnp.int32)
    order = jnp.arange(1, NCB + 1, dtype=jnp.int32)
    inverse = jnp.sum(jnp.where(block_maps[:, :, None] == blocks, order[None, :, None], 0), axis=1) - 1
    mine = jnp.where(child == 0, inverse[0], inverse[1])
    theirs = jnp.where(child == 0, inverse[1], inverse[0])

    def pick(idx):
        return jnp.sum(jnp.where(idx[:, None] == blocks[None, :], mine[None, :], 0), axis=1)

    slot = jnp.arange(64, dtype=jnp.int32)
    half = jnp.where(slot % 4 >= 2, 1 - child, child)
    bulk_idx = pick(32 * half + 2 * (slot // 4) + slot % 2)
    panel_idx = mine[0:4]
    at = q[None]
    four = jnp.arange(4, dtype=jnp.int32)
    col_idx = pick(32 * jnp.where(four >= 2, 1 - child, child) + 2 * r + four % 2)
    row_idx = pick(16 * four + r)

    quarters = front.reshape(2, 4, 32, 1024).transpose(1, 0, 2, 3).reshape(4, 64, 1024)
    raw_top = root_front[0:512].reshape(4, 4, 32, 256).transpose(1, 0, 2, 3).reshape(4, 2, 64, 256)
    pack = from_first_col(jnp.concatenate([quarters, raw_top[:, 0], raw_top[:, 1]], axis=2), q)
    left = pack[:, 0:512]
    top = jnp.concatenate([pack[:, 1024:1280], pack[:, 1280:1536]], axis=0)

    heads = exchange(pack.reshape(16, 4, 1536), "row")
    first, second, corner0, corner1 = lax.optimization_barrier(
        (heads[0:2, :, 0:512], heads[2:4, :, 0:1024], heads[0:1, :, 1024:1536], heads[1:2, :, 1024:1536]))
    d00 = gather(gather_col(first, q).reshape(8, 4, 512), "row", ROWS)
    corner = jnp.concatenate([corner0, corner1], axis=2)
    second = jnp.concatenate([gather_col(second, q).reshape(8, 4, 1024), corner], axis=0)
    second = jnp.broadcast_to(second[None], (ROWS,) + second.shape)
    d00, second = lax.optimization_barrier((d00, second))
    d1 = exchange(second, "row")
    raw_diag = jnp.concatenate([
        jnp.concatenate([d1[:, 8, :, c:c + 256] for c in (o, o + 512)], axis=2).reshape(64, 512) for o in (0, 256)
    ], axis=0)
    raw_diag = jnp.where(child == 0, raw_diag, 0.0)

    y = exchange_col(after(quarters, pack), q)
    panel_y = y[1][:, 0:512]
    placed_panel = call(place_panel_kernel, sds((64, 512)), 1, 1, name="place_panel")(panel_idx, panel_y)

    d00, placed_panel = lax.optimization_barrier((d00, placed_panel))
    inv0, p0, u0 = call(
        head_kernel, (sds((512, 512)), sds((64, 512)), sds((ROWS, 64, 512), BF16)), 0, 2, CHOL, 2 * 10**10, "head")(d00, left)
    f_panel = lax.all_gather(placed_panel, "row").reshape(32, 32, 512)
    d1, u0 = lax.optimization_barrier((d1, u0))
    u0_all = exchange(u0, "row").reshape(32, 32, 512)

    below = (r >= 2).astype(jnp.int32)[None]
    p1, u1 = call(
        second_kernel, (sds((64, 512)), sds((ROWS, 64, 512), BF16)), 1, 4,
        [pltpu.VMEM((512, 512), F32)] * 2 + CHOL, 3 * 10**10, "second")(below, d1, inv0, pack[:, 512:1024], u0)
    factor0 = p0.reshape(2, 32, 512)
    u1, u0_all, far0 = lax.optimization_barrier((u1, u0_all, across(factor0, 2)))
    u1_all = exchange(u1, "row").reshape(32, 32, 512)
    wide = after(jnp.concatenate([y[1], y[2], y[3]], axis=1), u1)
    placed = call(place_kernel, sds((16, 64, 512)), 1, 1, name="place")(bulk_idx, wide)
    factor0 = after(factor0, u1)
    factor0 = in_order(factor0, across(factor0, 1), far0, across(far0, 1), q)
    raw_rows = 0.0
    tile_top = after(root_front[0:512], u1)
    for j in range(2):
        pairs = []
        for g in range(32):
            m = 2 * g + j
            pairs.append((4 * g, (m // 32 * 16 + m % 16) * 4 + m // 16))
        raw_rows += lax.ppermute(tile_top[:, 128 * j:128 * j + 128], ("child", "row", "col"), pairs)
    u1_all, placed, factor0, raw_rows = lax.optimization_barrier((u1_all, placed, factor0, raw_rows))
    raw_rows = raw_rows.T
    f_bulk = exchange(placed, "row").reshape(32, 32, 512)

    some = sds((4, 32, 1024), BF16)
    u_panel, u_bulk = call(select_kernel, (some, some), 2, 2, name="select")(panel_idx, col_idx, u0_all, u1_all)
    u_panel = around(u_panel)
    u_bulk = after(u_bulk, u_panel[2])
    bulk_far = across(u_bulk, 2)
    z, t = call(panel_kernel, (sds((128, 512)), sds((128, 512))), 3, 7, flops=10**9, name="panel")(
        at, row_idx, panel_idx, u0_all, u1_all, f_panel, *u_panel)
    z, t, bulk_far = lax.optimization_barrier((z, t, bulk_far))
    t = t + raw_diag
    t = t + swap_child(t)
    u_bulk = [u_bulk, across(u_bulk, 1), bulk_far, across(bulk_far, 1)]
    z = exchange_col(z.reshape(4, 32, 512), q).reshape(128, 512) + raw_rows
    half, block = sds((768, 256)), sds((128, 256))
    z, t, u_bulk, f_bulk = lax.optimization_barrier((z, t, u_bulk, f_bulk))
    first, sent = call(corner_kernel, (block, block), 2, 7, flops=10**9, name="corner")(
        at, panel_idx, u0_all, u1_all, f_bulk, *u_bulk)
    z_swapped = swap_child(z)
    own, other = call(bulk_kernel, (half, half), 1, 7, flops=4 * 10**9, name="bulk")(
        at, u0_all, u1_all, after(f_bulk, sent), *u_bulk)
    z_swapped, own, other = lax.optimization_barrier((z_swapped, own, other))
    z = z + z_swapped
    panel = lax.all_gather(z, "row", tiled=True)

    t_all = around(t.reshape(4, 32, 512))
    head_cols = (top + first + swap_child(sent)).reshape(4, 32, 256)
    t_all, z, other, head_cols = lax.optimization_barrier((t_all, z, other, head_cols))
    factor1 = p1.reshape(2, 32, 512)
    far1 = across(after(factor1, other), 2)
    head_far = across(head_cols, 2)
    inv_root = call(root_kernel, sds((512, 512)), 1, 4, CHOL, 2 * 10**10, "root")(at, *t_all)
    got, inv_root, far1, head_far = lax.optimization_barrier((swap_child(other), inv_root, far1, head_far))
    spread = call(spread_kernel, sds((64, 32, 256)), 2, 2, name="spread")(
        mine, theirs, own.reshape(24, 32, 256), got.reshape(24, 32, 256))
    arrived = sent_col(spread.reshape(4, 16, 32, 256), q)
    head_cols = in_order(head_cols, across(head_cols, 1), head_far, across(head_far, 1), q)

    flags = jnp.stack([16 * child + r >= 2, q > 0]).astype(jnp.int32)
    rows = pl.BlockSpec((512, 512), lambda i: (i, 0))
    whole = pl.BlockSpec((512, 512), lambda i: (0, 0))
    narrow = pl.BlockSpec((512, 256), lambda i: (i, 0))
    fixed = pl.BlockSpec((512, 256), lambda i: (0, 0))
    root_factor, u_root, u_cols = pl.pallas_call(
        factor_kernel,
        out_shape=(sds((2048, 512)), sds((2048, 512), BF16), sds((512, 256), BF16)),
        grid=(4,),
        in_specs=[smem(), rows, whole, pl.BlockSpec((4, 4, 32, 256), lambda i: (0, 0, 0, 0))],
        out_specs=(rows, rows, fixed),
        scratch_shapes=[pltpu.VMEM((512, 256), F32)],
        compiler_params=VM,
        cost_estimate=pl.CostEstimate(flops=10**10, transcendentals=0, bytes_accessed=1 << 20),
        name="factor",
    )(flags, panel, inv_root, head_cols)
    arrived, u_root = lax.optimization_barrier((arrived, u_root))
    factor1 = after(factor1, u_root)
    factor1 = in_order(factor1, across(factor1, 1), far1, across(after(far1, u_root), 1), q)
    child_factor = jnp.concatenate([factor0, factor1], axis=3).transpose(1, 0, 2, 3).reshape(1, 256, 1024)
    trailing = pl.pallas_call(
        last_kernel,
        out_shape=sds((2048, 256)),
        grid=(4,),
        in_specs=[smem(), rows, fixed, narrow] + [pl.BlockSpec((4, 32, 256), lambda i: (i, 0, 0))] * 4,
        out_specs=narrow,
        compiler_params=VM,
        name="last",
    )(at, u_root, u_cols, root_front, *arrived)
    return (child_factor, root_factor, trailing)


def solution(mesh):
    return jax.shard_map(
        local,
        mesh=mesh,
        in_specs=(P("child", "row", "col"), P("col", ("child", "row")), P()),
        out_specs=(P("child", "row", None), P("col", None), P("col", ("child", "row"))),
        check_vma=False,
    )
```

```python
import functools

import jax
import jax.numpy as jnp
from jax import lax
from jax.experimental import pallas as pl
from jax.experimental.pallas import tpu as pltpu
from jax.sharding import PartitionSpec as P

F32 = jnp.float32
BF16 = jnp.bfloat16
HI = lax.Precision.HIGHEST
ROWS, COLS = 16, 4
NCB = 24
VM = pltpu.CompilerParams(vmem_limit_bytes=56 << 20)


def lane_copy(v, k):
    return jnp.broadcast_to(v[:, k:k + 1], (8, 128))


def sub_copy(v, k):
    return jnp.broadcast_to(v[k:k + 1, :], (8, 128))


def dot(a, b, ca, cb):
    return lax.dot_general(a, b, (((ca,), (cb,)), ((), ())), precision=HI, preferred_element_type=F32)


def dot16(a, b, ca, cb):
    return lax.dot_general(a, b, (((ca,), (cb,)), ((), ())), preferred_element_type=F32)


def inverse_factor128(block):
    lane = lax.broadcasted_iota(jnp.int32, (8, 128), 1)
    sub = lax.broadcasted_iota(jnp.int32, (8, 128), 0)
    w = [block[8 * t:8 * t + 8, :] for t in range(16)]
    for s in range(16):
        c = {t: [lane_copy(w[t], 8 * s + j) for j in range(8)] for t in range(s, 16)}
        inside = (lane >= 8 * s) & (lane < 8 * s + 8)
        w[s] = jnp.where(inside, (lane - 8 * s == sub).astype(F32), w[s])
        for t in range(s + 1, 16):
            w[t] = jnp.where(inside, 0.0, w[t])
        for j in range(8):
            scale = lax.rsqrt(sub_copy(c[s][j], j))
            pivot_row = sub_copy(w[s], j) * scale
            ahead = {k: sub_copy(c[s][j], k) * scale for k in range(j + 1, 8)}
            for t in range(s, 16):
                l = c[t][j] * scale
                if t == s:
                    l = jnp.where(sub > j, l, 0.0)
                for k in range(j + 1, 8):
                    c[t][k] = c[t][k] - l * ahead[k]
                w[t] = w[t] - l * pivot_row
            w[s] = jnp.where(sub == j, pivot_row, w[s])
    return jnp.concatenate([jnp.where(lane <= sub + 8 * t, w[t], 0.0) for t in range(16)], axis=0)


def inverse_factor512(a, b, g):
    n = 512
    b[...] = jnp.zeros((n, n), F32)

    def block(k, carry):
        o = pl.multiple_of(128 * k, 128)
        g[...] = inverse_factor128(a[pl.ds(o, 128), pl.ds(o, 128)])
        for step in range(n // 128):
            pl.when(k == step)(functools.partial(outer, 128 * step))
        return carry

    def outer(o):
        inv = g[...]
        if o > 0:
            b[o:o + 128, 0:o] = dot(inv, b[o:o + 128, 0:o], 1, 0)
        b[o:o + 128, o:o + 128] = inv
        r = o + 128
        if r < n:
            l = dot(a[r:n, o:o + 128], inv, 1, 1)
            a[r:n, r:n] = a[r:n, r:n] - dot(l, l, 1, 1)
            b[r:n, 0:r] = b[r:n, 0:r] - dot(l, b[o:o + 128, 0:r], 1, 0)

    lax.fori_loop(0, n // 128, block, 0)


def head_rows():
    for s in range(16):
        for q in range(4):
            for h in range(2):
                yield 256 * h + 128 * (s // 8) + 32 * q + 4 * (s % 8), (s, 2 * q + h)


def head_kernel(d_ref, c_ref, inv_ref, p_ref, u_ref, a, g):
    for o, piece in head_rows():
        a[o:o + 4, :] = d_ref[piece]
    inverse_factor512(a, inv_ref, g)
    p = dot(c_ref[...], inv_ref[...], 1, 1)
    p_ref[...] = p
    u_ref[...] = jnp.broadcast_to(p.astype(BF16)[None], u_ref.shape)


def second_kernel(mask_ref, d_ref, inv0_ref, c_ref, u0_ref, p_ref, u_ref, d10, inv1, a, g):
    for o, (s, i) in head_rows():
        d10[o:o + 4, :] = d_ref[s, i, :, 0:512]
        a[o:o + 4, :] = d_ref[s, i, :, 512:1024]
    u10 = dot(d10[...], inv0_ref[...], 1, 1).astype(BF16)
    a[...] = a[...] - dot16(u10, u10, 1, 1)
    c1 = c_ref[...] - dot16(u0_ref[0], u10, 1, 1)
    inverse_factor512(a, inv1, g)
    p1 = dot(c1, inv1[...], 1, 1)
    p_ref[...] = jnp.where(mask_ref[0] > 0, p1, 0.0)
    u_ref[...] = jnp.broadcast_to(p1.astype(BF16)[None], u_ref.shape)


def place(b, y_ref):
    col = pl.multiple_of(jnp.maximum(b, 0) * 128, 128)
    return jnp.where(b >= 0, y_ref[:, pl.ds(col, 128)], 0.0)


def place_panel_kernel(panel_ref, y_ref, p_ref):
    for m in range(4):
        p_ref[:, 128 * m:128 * m + 128] = place(panel_ref[m], y_ref)


def place_kernel(bulk_ref, y_ref, o_ref):
    def one(slot, carry):
        out = pl.multiple_of((slot % 4) * 128, 128)
        o_ref[slot // 4, :, pl.ds(out, 128)] = place(bulk_ref[slot], y_ref)
        return carry

    lax.fori_loop(0, 64, one, 0)


def picked(b, ref):
    v = ref[jnp.maximum(b, 0) + 8]
    return jnp.where(b >= 0, v, jnp.zeros_like(v))


def sender(refs, q_ref, p):
    j = p ^ q_ref[0]

    def read(i):
        x, near, far, corner = [ref[i] for ref in refs]
        return jnp.where(j >= 2, jnp.where(j == 3, corner, far), jnp.where(j == 1, near, x))

    return read


def columns_of(refs, q_ref):
    return jnp.concatenate([sender(refs, q_ref, q)(m) for m in range(4) for q in range(4)], axis=0)


def select_kernel(panel_ref, bulk_ref, u0_ref, u1_ref, p_ref, o_ref):
    for ref, out in ((panel_ref, p_ref), (bulk_ref, o_ref)):
        for i in range(4):
            out[i, :, 0:512] = picked(ref[i], u0_ref)
            out[i, :, 512:1024] = picked(ref[i], u1_ref)


def panel_kernel(q_ref, rows_ref, panel_ref, u0_ref, u1_ref, fp_ref, c0, c1, c2, c3, z_ref, t_ref):
    upan = columns_of((c0, c1, c2, c3), q_ref)
    for ref, out in ((panel_ref, t_ref), (rows_ref, z_ref)):
        f, u0, u1 = [jnp.concatenate([picked(ref[i], x) for i in range(4)], axis=0) for x in (fp_ref, u0_ref, u1_ref)]
        out[...] = f - dot16(jnp.concatenate([u0, u1], axis=1), upan, 1, 1)


def bulk_kernel(q_ref, panel_ref, u0_ref, u1_ref, f_ref, c0, c1, c2, c3, own_ref, other_ref, first_ref, send_ref):
    rows = jnp.concatenate([u0_ref[8:32].reshape(768, 512), u1_ref[8:32].reshape(768, 512)], axis=1)
    s = f_ref[8:32].reshape(768, 512) - dot16(rows, columns_of((c0, c1, c2, c3), q_ref), 1, 1)
    own_ref[...] = s[:, 0:256]
    other_ref[...] = s[:, 256:512]
    for m in range(4):
        b = panel_ref[m]
        rows = pl.ds(pl.multiple_of(32 * jnp.maximum(b, 0), 32), 32)
        first_ref[32 * m:32 * m + 32, :] = jnp.where(b >= 0, own_ref[rows, :], 0.0)
        send_ref[32 * m:32 * m + 32, :] = jnp.where(b >= 0, other_ref[rows, :], 0.0)


def root_kernel(q_ref, t0, t1, t2, t3, inv_ref, a, g):
    for q in range(4):
        read = sender((t0, t1, t2, t3), q_ref, q)
        for m in range(4):
            a[128 * m + 32 * q:128 * m + 32 * q + 32, :] = read(m)
    inverse_factor512(a, inv_ref, g)


def spread_kernel(mine_ref, theirs_ref, own_ref, got_ref, o_ref):
    def one(m, carry):
        i = mine_ref[m]
        j = theirs_ref[m]
        v = own_ref[jnp.maximum(i, 0)]
        w = got_ref[jnp.maximum(j, 0)]
        o_ref[m] = jnp.where(i >= 0, v, 0.0) + jnp.where(j >= 0, w, 0.0)
        return carry

    lax.fori_loop(0, 64, one, 0)


def factor_kernel(flag_ref, panel_ref, inv_ref, cp_ref, p_ref, u_ref, ug_ref, cps):
    step = pl.program_id(0)

    @pl.when(step == 0)
    def _():
        for q in range(4):
            for m in range(4):
                cps[128 * m + 32 * q:128 * m + 32 * q + 32, :] = cp_ref[q, m]
        v = dot(inv_ref[...], cps[...], 1, 0).astype(BF16)
        ug_ref[...] = jnp.where(flag_ref[0] > 0, v, jnp.zeros_like(v))

    p = dot(panel_ref[...], inv_ref[...], 1, 1)
    p_ref[...] = p
    u = p.astype(BF16)
    u_ref[...] = jnp.where((flag_ref[1] > 0) | (step >= 1), u, jnp.zeros_like(u))


def last_kernel(q_ref, u_ref, ug_ref, root_ref, g0, g1, g2, g3, o_ref):
    upd = dot16(u_ref[...], ug_ref[...], 1, 0)
    for q in range(4):
        read = sender((g0, g1, g2, g3), q_ref, q)
        for m in range(4):
            o = 128 * m + 32 * q
            o_ref[o:o + 32, :] = root_ref[o:o + 32, :] + read(m) - upd[o:o + 32, :]


def vmem():
    return pl.BlockSpec(memory_space=pltpu.VMEM)


def smem():
    return pl.BlockSpec(memory_space=pltpu.SMEM)


def call(kernel, outs, n_scalar, n_vector, scratch=(), flops=0, name=None):
    return pl.pallas_call(
        kernel,
        out_shape=outs,
        in_specs=[smem()] * n_scalar + [vmem()] * n_vector,
        out_specs=jax.tree.map(lambda _: vmem(), outs),
        scratch_shapes=list(scratch),
        compiler_params=VM,
        cost_estimate=pl.CostEstimate(flops=flops, transcendentals=0, bytes_accessed=1 << 20),
        name=name,
    )


def sds(shape, dtype=F32):
    return jax.ShapeDtypeStruct(shape, dtype)


CHOL = [pltpu.VMEM((512, 512), F32), pltpu.VMEM((128, 128), F32)]


def exchange(x, axis):
    return lax.all_to_all(x, axis, split_axis=0, concat_axis=0, tiled=True)


def gather(x, axis, n):
    return exchange(jnp.broadcast_to(x[None], (n,) + x.shape), axis)


def in_order(own, near, far, corner, q):
    even = q % 2 == 0
    low = q < 2
    a0, a1 = jnp.where(even, own, near), jnp.where(even, near, own)
    b0, b1 = jnp.where(even, far, corner), jnp.where(even, corner, far)
    return jnp.stack([jnp.where(low, a0, b0), jnp.where(low, a1, b1), jnp.where(low, b0, a0), jnp.where(low, b1, a1)])


def across(x, k):
    return lax.ppermute(x, "col", [(i, i ^ k) for i in range(4)])


def around(x):
    far = across(x, 2)
    return [x, across(x, 1), far, across(far, 1)]


def gather_col(x, q):
    return in_order(*around(x), q)


def from_first_col(x, q):
    sent = [lax.ppermute(x[k], "col", [(0, k)]) for k in (1, 2, 3)]
    return jnp.where(q == 0, x[0], sent[0] + sent[1] + sent[2])


def exchange_col(x, q):
    return in_order(*sent_col(x, q), q)


def sent_col(x, q):
    parts = [lax.dynamic_index_in_dim(x, q ^ k, 0, keepdims=False) for k in range(4)]
    return [parts[0]] + [across(parts[k], k) for k in (1, 2, 3)]


def after(x, *earlier):
    return lax.optimization_barrier((x,) + earlier)[0]


def swap_child(x):
    return lax.ppermute(x, "child", [(0, 1), (1, 0)])


def local(child_fronts, root_front, block_maps):
    front = child_fronts[0]
    child = lax.axis_index("child")
    r = lax.axis_index("row")
    q = lax.axis_index("col")
    blocks = jnp.arange(64, dtype=jnp.int32)
    order = jnp.arange(1, NCB + 1, dtype=jnp.int32)
    inverse = jnp.sum(jnp.where(block_maps[:, :, None] == blocks, order[None, :, None], 0), axis=1) - 1
    mine = jnp.where(child == 0, inverse[0], inverse[1])
    theirs = jnp.where(child == 0, inverse[1], inverse[0])

    def pick(idx):
        return jnp.sum(jnp.where(idx[:, None] == blocks[None, :], mine[None, :], 0), axis=1)

    slot = jnp.arange(64, dtype=jnp.int32)
    half = jnp.where(slot % 4 >= 2, 1 - child, child)
    bulk_idx = pick(32 * half + 2 * (slot // 4) + slot % 2)
    panel_idx = mine[0:4]
    at = q[None]
    four = jnp.arange(4, dtype=jnp.int32)
    col_idx = pick(32 * jnp.where(four >= 2, 1 - child, child) + 2 * r + four % 2)
    row_idx = pick(16 * four + r)

    quarters = front.reshape(2, 4, 32, 1024).transpose(1, 0, 2, 3).reshape(4, 64, 1024)
    raw_top = root_front[0:512].reshape(4, 4, 32, 256).transpose(1, 0, 2, 3).reshape(4, 2, 64, 256)
    pack = from_first_col(jnp.concatenate([quarters, raw_top[:, 0], raw_top[:, 1]], axis=2), q)
    left = pack[:, 0:512]
    top = jnp.concatenate([pack[:, 1024:1280], pack[:, 1280:1536]], axis=0)

    heads = exchange(pack.reshape(16, 4, 1536), "row")
    first, second, corner0, corner1 = lax.optimization_barrier(
        (heads[0:2, :, 0:512], heads[2:4, :, 0:1024], heads[0:1, :, 1024:1536], heads[1:2, :, 1024:1536]))
    d00 = gather(gather_col(first, q).reshape(8, 4, 512), "row", ROWS)
    corner = jnp.concatenate([corner0, corner1], axis=2)
    second = jnp.concatenate([gather_col(second, q).reshape(8, 4, 1024), corner], axis=0)
    second = jnp.broadcast_to(second[None], (ROWS,) + second.shape)
    d00, second = lax.optimization_barrier((d00, second))
    d1 = exchange(second, "row")
    raw_diag = jnp.concatenate([
        jnp.concatenate([d1[:, 8, :, c:c + 256] for c in (o, o + 512)], axis=2).reshape(64, 512) for o in (0, 256)
    ], axis=0)
    raw_diag = jnp.where(child == 0, raw_diag, 0.0)

    y = exchange_col(after(quarters, pack), q)
    panel_y = y[1][:, 0:512]
    placed_panel = call(place_panel_kernel, sds((64, 512)), 1, 1, name="place_panel")(panel_idx, panel_y)

    d00, placed_panel = lax.optimization_barrier((d00, placed_panel))
    inv0, p0, u0 = call(
        head_kernel, (sds((512, 512)), sds((64, 512)), sds((ROWS, 64, 512), BF16)), 0, 2, CHOL, 2 * 10**10, "head")(d00, left)
    f_panel = lax.all_gather(placed_panel, "row").reshape(32, 32, 512)
    d1, u0 = lax.optimization_barrier((d1, u0))
    u0_all = exchange(u0, "row").reshape(32, 32, 512)

    below = (r >= 2).astype(jnp.int32)[None]
    p1, u1 = call(
        second_kernel, (sds((64, 512)), sds((ROWS, 64, 512), BF16)), 1, 4,
        [pltpu.VMEM((512, 512), F32)] * 2 + CHOL, 3 * 10**10, "second")(below, d1, inv0, pack[:, 512:1024], u0)
    factor0 = p0.reshape(2, 32, 512)
    u1, u0_all, far0 = lax.optimization_barrier((u1, u0_all, across(factor0, 2)))
    u1_all = exchange(u1, "row").reshape(32, 32, 512)
    wide = after(jnp.concatenate([y[1], y[2], y[3]], axis=1), u1)
    placed = call(place_kernel, sds((16, 64, 512)), 1, 1, name="place")(bulk_idx, wide)
    factor0 = after(factor0, u1)
    factor0 = in_order(factor0, across(factor0, 1), far0, across(far0, 1), q)
    raw_rows = 0.0
    tile_top = after(root_front[0:512], u1)
    for j in range(2):
        pairs = []
        for g in range(32):
            m = 2 * g + j
            pairs.append((4 * g, (m // 32 * 16 + m % 16) * 4 + m // 16))
        raw_rows += lax.ppermute(tile_top[:, 128 * j:128 * j + 128], ("child", "row", "col"), pairs)
    factor1 = p1.reshape(2, 32, 512)
    u1_all, placed, factor0, raw_rows, far1 = lax.optimization_barrier(
        (u1_all, placed, factor0, raw_rows, across(after(factor1, u1), 2)))
    raw_rows = raw_rows.T
    f_bulk = exchange(placed, "row").reshape(32, 32, 512)

    some = sds((4, 32, 1024), BF16)
    u_panel, u_bulk = call(select_kernel, (some, some), 2, 2, name="select")(panel_idx, col_idx, u0_all, u1_all)
    u_panel = around(u_panel)
    u_bulk = after(u_bulk, u_panel[2])
    bulk_far = across(u_bulk, 2)
    z, t = call(panel_kernel, (sds((128, 512)), sds((128, 512))), 3, 7, flops=10**9, name="panel")(
        at, row_idx, panel_idx, u0_all, u1_all, f_panel, *u_panel)
    z, t, bulk_far = lax.optimization_barrier((z, t, bulk_far))
    t = t + raw_diag
    t = t + swap_child(t)
    u_bulk = [u_bulk, across(u_bulk, 1), bulk_far, across(bulk_far, 1)]
    z = exchange_col(z.reshape(4, 32, 512), q).reshape(128, 512) + raw_rows
    half, block = sds((768, 256)), sds((128, 256))
    z, t, u_bulk, f_bulk = lax.optimization_barrier((z, t, u_bulk, f_bulk))
    z_swapped = swap_child(z)
    t = t.reshape(4, 32, 512)
    t_far = across(t, 2)
    own, other, first, sent = call(
        bulk_kernel, (half, half, block, block), 2, 7, flops=4 * 10**9, name="bulk")(
        at, panel_idx, u0_all, u1_all, f_bulk, *u_bulk)
    z_swapped, own, other, t_far = lax.optimization_barrier((z_swapped, own, other, t_far))
    z = z + z_swapped
    panel = lax.all_gather(z, "row", tiled=True)

    t_all = [t, across(t, 1), t_far, across(t_far, 1)]
    head_cols = (top + first + swap_child(sent)).reshape(4, 32, 256)
    t_all, z, other, head_cols = lax.optimization_barrier((t_all, z, other, head_cols))
    head_far = across(head_cols, 2)
    inv_root = call(root_kernel, sds((512, 512)), 1, 4, CHOL, 2 * 10**10, "root")(at, *t_all)
    got, inv_root, head_far = lax.optimization_barrier((swap_child(other), inv_root, head_far))
    spread = call(spread_kernel, sds((64, 32, 256)), 2, 2, name="spread")(
        mine, theirs, own.reshape(24, 32, 256), got.reshape(24, 32, 256))
    arrived = sent_col(spread.reshape(4, 16, 32, 256), q)
    head_cols = in_order(head_cols, across(head_cols, 1), head_far, across(head_far, 1), q)

    flags = jnp.stack([16 * child + r >= 2, q > 0]).astype(jnp.int32)
    rows = pl.BlockSpec((512, 512), lambda i: (i, 0))
    whole = pl.BlockSpec((512, 512), lambda i: (0, 0))
    narrow = pl.BlockSpec((512, 256), lambda i: (i, 0))
    fixed = pl.BlockSpec((512, 256), lambda i: (0, 0))
    root_factor, u_root, u_cols = pl.pallas_call(
        factor_kernel,
        out_shape=(sds((2048, 512)), sds((2048, 512), BF16), sds((512, 256), BF16)),
        grid=(4,),
        in_specs=[smem(), rows, whole, pl.BlockSpec((4, 4, 32, 256), lambda i: (0, 0, 0, 0))],
        out_specs=(rows, rows, fixed),
        scratch_shapes=[pltpu.VMEM((512, 256), F32)],
        compiler_params=VM,
        cost_estimate=pl.CostEstimate(flops=10**10, transcendentals=0, bytes_accessed=1 << 20),
        name="factor",
    )(flags, panel, inv_root, head_cols)
    arrived, u_root = lax.optimization_barrier((arrived, u_root))
    factor1 = after(factor1, u_root)
    factor1 = in_order(factor1, across(factor1, 1), far1, across(after(far1, u_root), 1), q)
    child_factor = jnp.concatenate([factor0, factor1], axis=3).transpose(1, 0, 2, 3).reshape(1, 256, 1024)
    trailing = pl.pallas_call(
        last_kernel,
        out_shape=sds((2048, 256)),
        grid=(4,),
        in_specs=[smem(), rows, fixed, narrow] + [pl.BlockSpec((4, 32, 256), lambda i: (i, 0, 0))] * 4,
        out_specs=narrow,
        compiler_params=VM,
        name="last",
    )(at, u_root, u_cols, root_front, *arrived)
    return (child_factor, root_factor, trailing)


def solution(mesh):
    return jax.shard_map(
        local,
        mesh=mesh,
        in_specs=(P("child", "row", "col"), P("col", ("child", "row")), P()),
        out_specs=(P("child", "row", None), P("col", None), P("col", ("child", "row"))),
        check_vma=False,
    )
```

```python
import functools

import jax
import jax.numpy as jnp
from jax import lax
from jax.experimental import pallas as pl
from jax.experimental.pallas import tpu as pltpu
from jax.sharding import PartitionSpec as P

F32 = jnp.float32
BF16 = jnp.bfloat16
HI = lax.Precision.HIGHEST
ROWS, COLS = 16, 4
NCB = 24
VM = pltpu.CompilerParams(vmem_limit_bytes=56 << 20)


def lane_copy(v, k):
    return jnp.broadcast_to(v[:, k:k + 1], (8, 128))


def sub_copy(v, k):
    return jnp.broadcast_to(v[k:k + 1, :], (8, 128))


def dot(a, b, ca, cb):
    return lax.dot_general(a, b, (((ca,), (cb,)), ((), ())), precision=HI, preferred_element_type=F32)


def dot16(a, b, ca, cb):
    return lax.dot_general(a, b, (((ca,), (cb,)), ((), ())), preferred_element_type=F32)


def inverse_factor128(block):
    lane = lax.broadcasted_iota(jnp.int32, (8, 128), 1)
    sub = lax.broadcasted_iota(jnp.int32, (8, 128), 0)
    w = [block[8 * t:8 * t + 8, :] for t in range(16)]
    for s in range(16):
        c = {t: [lane_copy(w[t], 8 * s + j) for j in range(8)] for t in range(s, 16)}
        inside = (lane >= 8 * s) & (lane < 8 * s + 8)
        w[s] = jnp.where(inside, (lane - 8 * s == sub).astype(F32), w[s])
        for t in range(s + 1, 16):
            w[t] = jnp.where(inside, 0.0, w[t])
        for j in range(8):
            scale = lax.rsqrt(sub_copy(c[s][j], j))
            pivot_row = sub_copy(w[s], j) * scale
            ahead = {k: sub_copy(c[s][j], k) * scale for k in range(j + 1, 8)}
            for t in range(s, 16):
                l = c[t][j] * scale
                if t == s:
                    l = jnp.where(sub > j, l, 0.0)
                for k in range(j + 1, 8):
                    c[t][k] = c[t][k] - l * ahead[k]
                w[t] = w[t] - l * pivot_row
            w[s] = jnp.where(sub == j, pivot_row, w[s])
    return jnp.concatenate([jnp.where(lane <= sub + 8 * t, w[t], 0.0) for t in range(16)], axis=0)


def inverse_factor512(a, b, g):
    n = 512
    b[...] = jnp.zeros((n, n), F32)

    def block(k, carry):
        o = pl.multiple_of(128 * k, 128)
        g[...] = inverse_factor128(a[pl.ds(o, 128), pl.ds(o, 128)])
        for step in range(n // 128):
            pl.when(k == step)(functools.partial(outer, 128 * step))
        return carry

    def outer(o):
        inv = g[...]
        if o > 0:
            b[o:o + 128, 0:o] = dot(inv, b[o:o + 128, 0:o], 1, 0)
        b[o:o + 128, o:o + 128] = inv
        r = o + 128
        if r < n:
            l = dot(a[r:n, o:o + 128], inv, 1, 1)
            a[r:n, r:n] = a[r:n, r:n] - dot(l, l, 1, 1)
            b[r:n, 0:r] = b[r:n, 0:r] - dot(l, b[o:o + 128, 0:r], 1, 0)

    lax.fori_loop(0, n // 128, block, 0)


def head_rows():
    for s in range(16):
        for q in range(4):
            for h in range(2):
                yield 256 * h + 128 * (s // 8) + 32 * q + 4 * (s % 8), (s, 2 * q + h)


def head_kernel(d_ref, c_ref, inv_ref, p_ref, u_ref, a, g):
    for o, piece in head_rows():
        a[o:o + 4, :] = d_ref[piece]
    inverse_factor512(a, inv_ref, g)
    p = dot(c_ref[...], inv_ref[...], 1, 1)
    p_ref[...] = p
    u_ref[...] = jnp.broadcast_to(p.astype(BF16)[None], u_ref.shape)


def second_kernel(mask_ref, d_ref, inv0_ref, c_ref, u0_ref, p_ref, u_ref, d10, inv1, a, g):
    for o, (s, i) in head_rows():
        d10[o:o + 4, :] = d_ref[s, i, :, 0:512]
        a[o:o + 4, :] = d_ref[s, i, :, 512:1024]
    u10 = dot(d10[...], inv0_ref[...], 1, 1).astype(BF16)
    a[...] = a[...] - dot16(u10, u10, 1, 1)
    c1 = c_ref[...] - dot16(u0_ref[0], u10, 1, 1)
    inverse_factor512(a, inv1, g)
    p1 = dot(c1, inv1[...], 1, 1)
    p_ref[...] = jnp.where(mask_ref[0] > 0, p1, 0.0)
    u_ref[...] = jnp.broadcast_to(p1.astype(BF16)[None], u_ref.shape)


def place(b, y_ref):
    col = pl.multiple_of(jnp.maximum(b, 0) * 128, 128)
    return jnp.where(b >= 0, y_ref[:, pl.ds(col, 128)], 0.0)


def place_panel_kernel(panel_ref, y_ref, p_ref):
    for m in range(4):
        p_ref[:, 128 * m:128 * m + 128] = place(panel_ref[m], y_ref)


def place_kernel(bulk_ref, y_ref, o_ref):
    def one(slot, carry):
        out = pl.multiple_of((slot % 4) * 128, 128)
        o_ref[slot // 4, :, pl.ds(out, 128)] = place(bulk_ref[slot], y_ref)
        return carry

    lax.fori_loop(0, 64, one, 0)


def picked(b, ref):
    v = ref[jnp.maximum(b, 0) + 8]
    return jnp.where(b >= 0, v, jnp.zeros_like(v))


def sender(refs, q_ref, p):
    j = p ^ q_ref[0]

    def read(i):
        x, near, far, corner = [ref[i] for ref in refs]
        return jnp.where(j >= 2, jnp.where(j == 3, corner, far), jnp.where(j == 1, near, x))

    return read


def columns_of(refs, q_ref):
    return jnp.concatenate([sender(refs, q_ref, q)(m) for m in range(4) for q in range(4)], axis=0)


def select_kernel(panel_ref, bulk_ref, u0_ref, u1_ref, p_ref, o_ref):
    for ref, out in ((panel_ref, p_ref), (bulk_ref, o_ref)):
        for i in range(4):
            out[i, :, 0:512] = picked(ref[i], u0_ref)
            out[i, :, 512:1024] = picked(ref[i], u1_ref)


def panel_kernel(q_ref, rows_ref, panel_ref, u0_ref, u1_ref, fp_ref, c0, c1, c2, c3, z_ref, t_ref):
    upan = columns_of((c0, c1, c2, c3), q_ref)
    for ref, out in ((panel_ref, t_ref), (rows_ref, z_ref)):
        f, u0, u1 = [jnp.concatenate([picked(ref[i], x) for i in range(4)], axis=0) for x in (fp_ref, u0_ref, u1_ref)]
        out[...] = f - dot16(jnp.concatenate([u0, u1], axis=1), upan, 1, 1)


def bulk_kernel(q_ref, panel_ref, u0_ref, u1_ref, f_ref, c0, c1, c2, c3, own_ref, other_ref, first_ref, send_ref):
    rows = jnp.concatenate([u0_ref[8:32].reshape(768, 512), u1_ref[8:32].reshape(768, 512)], axis=1)
    s = f_ref[8:32].reshape(768, 512) - dot16(rows, columns_of((c0, c1, c2, c3), q_ref), 1, 1)
    own_ref[...] = s[:, 0:256]
    other_ref[...] = s[:, 256:512]
    for m in range(4):
        b = panel_ref[m]
        rows = pl.ds(pl.multiple_of(32 * jnp.maximum(b, 0), 32), 32)
        first_ref[32 * m:32 * m + 32, :] = jnp.where(b >= 0, own_ref[rows, :], 0.0)
        send_ref[32 * m:32 * m + 32, :] = jnp.where(b >= 0, other_ref[rows, :], 0.0)


def root_kernel(q_ref, t0, t1, t2, t3, inv_ref, a, g):
    for q in range(4):
        read = sender((t0, t1, t2, t3), q_ref, q)
        for m in range(4):
            a[128 * m + 32 * q:128 * m + 32 * q + 32, :] = read(m)
    inverse_factor512(a, inv_ref, g)


def spread_kernel(mine_ref, theirs_ref, own_ref, got_ref, o_ref):
    def one(m, carry):
        i = mine_ref[m]
        j = theirs_ref[m]
        v = own_ref[jnp.maximum(i, 0)]
        w = got_ref[jnp.maximum(j, 0)]
        o_ref[m] = jnp.where(i >= 0, v, 0.0) + jnp.where(j >= 0, w, 0.0)
        return carry

    lax.fori_loop(0, 64, one, 0)


def factor_kernel(flag_ref, panel_ref, inv_ref, cp_ref, p_ref, u_ref, ug_ref, cps):
    step = pl.program_id(0)

    @pl.when(step == 0)
    def _():
        for q in range(4):
            for m in range(4):
                cps[128 * m + 32 * q:128 * m + 32 * q + 32, :] = cp_ref[q, m]
        v = dot(inv_ref[...], cps[...], 1, 0).astype(BF16)
        ug_ref[...] = jnp.where(flag_ref[0] > 0, v, jnp.zeros_like(v))

    p = dot(panel_ref[...], inv_ref[...], 1, 1)
    p_ref[...] = p
    u = p.astype(BF16)
    u_ref[...] = jnp.where((flag_ref[1] > 0) | (step >= 1), u, jnp.zeros_like(u))


def last_kernel(q_ref, u_ref, ug_ref, root_ref, g0, g1, g2, g3, o_ref):
    upd = dot16(u_ref[...], ug_ref[...], 1, 0)
    for q in range(4):
        read = sender((g0, g1, g2, g3), q_ref, q)
        for m in range(4):
            o = 128 * m + 32 * q
            o_ref[o:o + 32, :] = root_ref[o:o + 32, :] + read(m) - upd[o:o + 32, :]


def vmem():
    return pl.BlockSpec(memory_space=pltpu.VMEM)


def smem():
    return pl.BlockSpec(memory_space=pltpu.SMEM)


def call(kernel, outs, n_scalar, n_vector, scratch=(), flops=0, name=None):
    return pl.pallas_call(
        kernel,
        out_shape=outs,
        in_specs=[smem()] * n_scalar + [vmem()] * n_vector,
        out_specs=jax.tree.map(lambda _: vmem(), outs),
        scratch_shapes=list(scratch),
        compiler_params=VM,
        cost_estimate=pl.CostEstimate(flops=flops, transcendentals=0, bytes_accessed=1 << 20),
        name=name,
    )


def sds(shape, dtype=F32):
    return jax.ShapeDtypeStruct(shape, dtype)


CHOL = [pltpu.VMEM((512, 512), F32), pltpu.VMEM((128, 128), F32)]


def exchange(x, axis):
    return lax.all_to_all(x, axis, split_axis=0, concat_axis=0, tiled=True)


def gather(x, axis, n):
    return exchange(jnp.broadcast_to(x[None], (n,) + x.shape), axis)


def in_order(own, near, far, corner, q):
    even = q % 2 == 0
    low = q < 2
    a0, a1 = jnp.where(even, own, near), jnp.where(even, near, own)
    b0, b1 = jnp.where(even, far, corner), jnp.where(even, corner, far)
    return jnp.stack([jnp.where(low, a0, b0), jnp.where(low, a1, b1), jnp.where(low, b0, a0), jnp.where(low, b1, a1)])


def across(x, k):
    return lax.ppermute(x, "col", [(i, i ^ k) for i in range(4)])


def around(x):
    far = across(x, 2)
    return [x, across(x, 1), far, across(far, 1)]


def gather_col(x, q):
    return in_order(*around(x), q)


def from_first_col(x, q):
    sent = [lax.ppermute(x[k], "col", [(0, k)]) for k in (1, 2, 3)]
    return jnp.where(q == 0, x[0], sent[0] + sent[1] + sent[2])


def exchange_col(x, q):
    return in_order(*sent_col(x, q), q)


def sent_col(x, q):
    parts = [lax.dynamic_index_in_dim(x, q ^ k, 0, keepdims=False) for k in range(4)]
    return [parts[0]] + [across(parts[k], k) for k in (1, 2, 3)]


def after(x, *earlier):
    return lax.optimization_barrier((x,) + earlier)[0]


def swap_child(x):
    return lax.ppermute(x, "child", [(0, 1), (1, 0)])


def local(child_fronts, root_front, block_maps):
    front = child_fronts[0]
    child = lax.axis_index("child")
    r = lax.axis_index("row")
    q = lax.axis_index("col")
    blocks = jnp.arange(64, dtype=jnp.int32)
    order = jnp.arange(1, NCB + 1, dtype=jnp.int32)
    inverse = jnp.sum(jnp.where(block_maps[:, :, None] == blocks, order[None, :, None], 0), axis=1) - 1
    mine = jnp.where(child == 0, inverse[0], inverse[1])
    theirs = jnp.where(child == 0, inverse[1], inverse[0])

    def pick(idx):
        return jnp.sum(jnp.where(idx[:, None] == blocks[None, :], mine[None, :], 0), axis=1)

    slot = jnp.arange(64, dtype=jnp.int32)
    half = jnp.where(slot % 4 >= 2, 1 - child, child)
    bulk_idx = pick(32 * half + 2 * (slot // 4) + slot % 2)
    panel_idx = mine[0:4]
    at = q[None]
    four = jnp.arange(4, dtype=jnp.int32)
    col_idx = pick(32 * jnp.where(four >= 2, 1 - child, child) + 2 * r + four % 2)
    row_idx = pick(16 * four + r)

    quarters = front.reshape(2, 4, 32, 1024).transpose(1, 0, 2, 3).reshape(4, 64, 1024)
    raw_top = root_front[0:512].reshape(4, 4, 32, 256).transpose(1, 0, 2, 3).reshape(4, 2, 64, 256)
    pack = from_first_col(jnp.concatenate([quarters, raw_top[:, 0], raw_top[:, 1]], axis=2), q)
    left = pack[:, 0:512]
    top = jnp.concatenate([pack[:, 1024:1280], pack[:, 1280:1536]], axis=0)

    heads = exchange(pack.reshape(16, 4, 1536), "row")
    first, second, corner0, corner1 = lax.optimization_barrier(
        (heads[0:2, :, 0:512], heads[2:4, :, 0:1024], heads[0:1, :, 1024:1536], heads[1:2, :, 1024:1536]))
    d00 = gather(gather_col(first, q).reshape(8, 4, 512), "row", ROWS)
    corner = jnp.concatenate([corner0, corner1], axis=2)
    second = jnp.concatenate([gather_col(second, q).reshape(8, 4, 1024), corner], axis=0)
    second = jnp.broadcast_to(second[None], (ROWS,) + second.shape)
    d00, second = lax.optimization_barrier((d00, second))
    d1 = exchange(second, "row")
    raw_diag = jnp.concatenate([
        jnp.concatenate([d1[:, 8, :, c:c + 256] for c in (o, o + 512)], axis=2).reshape(64, 512) for o in (0, 256)
    ], axis=0)
    raw_diag = jnp.where(child == 0, raw_diag, 0.0)

    y = exchange_col(after(quarters, pack), q)
    panel_y = y[1][:, 0:512]
    placed_panel = call(place_panel_kernel, sds((64, 512)), 1, 1, name="place_panel")(panel_idx, panel_y)

    d00, placed_panel = lax.optimization_barrier((d00, placed_panel))
    inv0, p0, u0 = call(
        head_kernel, (sds((512, 512)), sds((64, 512)), sds((ROWS, 64, 512), BF16)), 0, 2, CHOL, 2 * 10**10, "head")(d00, left)
    f_panel = lax.all_gather(placed_panel, "row").reshape(32, 32, 512)
    d1, u0 = lax.optimization_barrier((d1, u0))
    u0_all = exchange(u0, "row").reshape(32, 32, 512)

    raw_rows = []
    tile_top = after(root_front[0:512], inv0)
    for j in range(2):
        pairs = []
        for g in range(32):
            m = 2 * g + j
            pairs.append((4 * g, (m // 32 * 16 + m % 16) * 4 + m // 16))
        raw_rows.append(lax.ppermute(tile_top[:, 128 * j:128 * j + 128], ("child", "row", "col"), pairs))

    below = (r >= 2).astype(jnp.int32)[None]
    p1, u1 = call(
        second_kernel, (sds((64, 512)), sds((ROWS, 64, 512), BF16)), 1, 4,
        [pltpu.VMEM((512, 512), F32)] * 2 + CHOL, 3 * 10**10, "second")(below, d1, inv0, pack[:, 512:1024], u0)
    factor0 = p0.reshape(2, 32, 512)
    u1, u0_all, far0, raw_rows = lax.optimization_barrier((u1, u0_all, across(factor0, 2), raw_rows))
    raw_rows = (raw_rows[0] + raw_rows[1]).T
    u1_all = exchange(u1, "row").reshape(32, 32, 512)
    wide = after(jnp.concatenate([y[1], y[2], y[3]], axis=1), u1)
    placed = call(place_kernel, sds((16, 64, 512)), 1, 1, name="place")(bulk_idx, wide)
    factor0 = after(factor0, u1)
    factor0 = in_order(factor0, across(factor0, 1), far0, across(far0, 1), q)
    factor1 = p1.reshape(2, 32, 512)
    u1_all, placed, factor0, far1 = lax.optimization_barrier(
        (u1_all, placed, factor0, across(after(factor1, u1), 2)))
    f_bulk = exchange(placed, "row").reshape(32, 32, 512)

    some = sds((4, 32, 1024), BF16)
    u_panel, u_bulk = call(select_kernel, (some, some), 2, 2, name="select")(panel_idx, col_idx, u0_all, u1_all)
    u_panel = around(u_panel)
    u_bulk = after(u_bulk, u_panel[2])
    bulk_far = across(u_bulk, 2)
    z, t = call(panel_kernel, (sds((128, 512)), sds((128, 512))), 3, 7, flops=10**9, name="panel")(
        at, row_idx, panel_idx, u0_all, u1_all, f_panel, *u_panel)
    z, t, bulk_far = lax.optimization_barrier((z, t, bulk_far))
    t = t + raw_diag
    t = t + swap_child(t)
    u_bulk = [u_bulk, across(u_bulk, 1), bulk_far, across(bulk_far, 1)]
    z = exchange_col(z.reshape(4, 32, 512), q).reshape(128, 512) + raw_rows
    half, block = sds((768, 256)), sds((128, 256))
    z, t, u_bulk, f_bulk = lax.optimization_barrier((z, t, u_bulk, f_bulk))
    z_swapped = swap_child(z)
    t = t.reshape(4, 32, 512)
    t_far = across(t, 2)
    own, other, first, sent = call(
        bulk_kernel, (half, half, block, block), 2, 7, flops=4 * 10**9, name="bulk")(
        at, panel_idx, u0_all, u1_all, f_bulk, *u_bulk)
    z_swapped, own, other, t_far = lax.optimization_barrier((z_swapped, own, other, t_far))
    z = z + z_swapped
    panel = lax.all_gather(z, "row", tiled=True)

    t_all = [t, across(t, 1), t_far, across(t_far, 1)]
    head_cols = (top + first + swap_child(sent)).reshape(4, 32, 256)
    t_all, z, other, head_cols = lax.optimization_barrier((t_all, z, other, head_cols))
    head_far = across(head_cols, 2)
    inv_root = call(root_kernel, sds((512, 512)), 1, 4, CHOL, 2 * 10**10, "root")(at, *t_all)
    got, inv_root, head_far = lax.optimization_barrier((swap_child(other), inv_root, head_far))
    spread = call(spread_kernel, sds((64, 32, 256)), 2, 2, name="spread")(
        mine, theirs, own.reshape(24, 32, 256), got.reshape(24, 32, 256))
    arrived = sent_col(spread.reshape(4, 16, 32, 256), q)
    head_cols = in_order(head_cols, across(head_cols, 1), head_far, across(head_far, 1), q)

    flags = jnp.stack([16 * child + r >= 2, q > 0]).astype(jnp.int32)
    rows = pl.BlockSpec((512, 512), lambda i: (i, 0))
    whole = pl.BlockSpec((512, 512), lambda i: (0, 0))
    narrow = pl.BlockSpec((512, 256), lambda i: (i, 0))
    fixed = pl.BlockSpec((512, 256), lambda i: (0, 0))
    root_factor, u_root, u_cols = pl.pallas_call(
        factor_kernel,
        out_shape=(sds((2048, 512)), sds((2048, 512), BF16), sds((512, 256), BF16)),
        grid=(4,),
        in_specs=[smem(), rows, whole, pl.BlockSpec((4, 4, 32, 256), lambda i: (0, 0, 0, 0))],
        out_specs=(rows, rows, fixed),
        scratch_shapes=[pltpu.VMEM((512, 256), F32)],
        compiler_params=VM,
        cost_estimate=pl.CostEstimate(flops=10**10, transcendentals=0, bytes_accessed=1 << 20),
        name="factor",
    )(flags, panel, inv_root, head_cols)
    arrived, u_root = lax.optimization_barrier((arrived, u_root))
    factor1 = after(factor1, u_root)
    factor1 = in_order(factor1, across(factor1, 1), far1, across(after(far1, u_root), 1), q)
    child_factor = jnp.concatenate([factor0, factor1], axis=3).transpose(1, 0, 2, 3).reshape(1, 256, 1024)
    trailing = pl.pallas_call(
        last_kernel,
        out_shape=sds((2048, 256)),
        grid=(4,),
        in_specs=[smem(), rows, fixed, narrow] + [pl.BlockSpec((4, 32, 256), lambda i: (i, 0, 0))] * 4,
        out_specs=narrow,
        compiler_params=VM,
        name="last",
    )(at, u_root, u_cols, root_front, *arrived)
    return (child_factor, root_factor, trailing)


def solution(mesh):
    return jax.shard_map(
        local,
        mesh=mesh,
        in_specs=(P("child", "row", "col"), P("col", ("child", "row")), P()),
        out_specs=(P("child", "row", None), P("col", None), P("col", ("child", "row"))),
        check_vma=False,
    )
```

```python
import functools

import jax
import jax.numpy as jnp
from jax import lax
from jax.experimental import pallas as pl
from jax.experimental.pallas import tpu as pltpu
from jax.sharding import PartitionSpec as P

F32 = jnp.float32
BF16 = jnp.bfloat16
HI = lax.Precision.HIGHEST
ROWS, COLS = 16, 4
NCB = 24
VM = pltpu.CompilerParams(vmem_limit_bytes=56 << 20)


def lane_copy(v, k):
    return jnp.broadcast_to(v[:, k:k + 1], (8, 128))


def sub_copy(v, k):
    return jnp.broadcast_to(v[k:k + 1, :], (8, 128))


def dot(a, b, ca, cb):
    return lax.dot_general(a, b, (((ca,), (cb,)), ((), ())), precision=HI, preferred_element_type=F32)


def dot16(a, b, ca, cb):
    return lax.dot_general(a, b, (((ca,), (cb,)), ((), ())), preferred_element_type=F32)


def inverse_factor128(block):
    lane = lax.broadcasted_iota(jnp.int32, (8, 128), 1)
    sub = lax.broadcasted_iota(jnp.int32, (8, 128), 0)
    w = [block[8 * t:8 * t + 8, :] for t in range(16)]
    for s in range(16):
        c = {t: [lane_copy(w[t], 8 * s + j) for j in range(8)] for t in range(s, 16)}
        inside = (lane >= 8 * s) & (lane < 8 * s + 8)
        w[s] = jnp.where(inside, (lane - 8 * s == sub).astype(F32), w[s])
        for t in range(s + 1, 16):
            w[t] = jnp.where(inside, 0.0, w[t])
        for j in range(8):
            scale = lax.rsqrt(sub_copy(c[s][j], j))
            pivot_row = sub_copy(w[s], j) * scale
            ahead = {k: sub_copy(c[s][j], k) * scale for k in range(j + 1, 8)}
            for t in range(s, 16):
                l = c[t][j] * scale
                if t == s:
                    l = jnp.where(sub > j, l, 0.0)
                for k in range(j + 1, 8):
                    c[t][k] = c[t][k] - l * ahead[k]
                w[t] = w[t] - l * pivot_row
            w[s] = jnp.where(sub == j, pivot_row, w[s])
    return jnp.concatenate([jnp.where(lane <= sub + 8 * t, w[t], 0.0) for t in range(16)], axis=0)


def inverse_factor512(a, b, g):
    n = 512
    b[...] = jnp.zeros((n, n), F32)

    def block(k, carry):
        o = pl.multiple_of(128 * k, 128)
        g[...] = inverse_factor128(a[pl.ds(o, 128), pl.ds(o, 128)])
        for step in range(n // 128):
            pl.when(k == step)(functools.partial(outer, 128 * step))
        return carry

    def outer(o):
        inv = g[...]
        if o > 0:
            b[o:o + 128, 0:o] = dot(inv, b[o:o + 128, 0:o], 1, 0)
        b[o:o + 128, o:o + 128] = inv
        r = o + 128
        if r < n:
            l = dot(a[r:n, o:o + 128], inv, 1, 1)
            a[r:n, r:n] = a[r:n, r:n] - dot(l, l, 1, 1)
            b[r:n, 0:r] = b[r:n, 0:r] - dot(l, b[o:o + 128, 0:r], 1, 0)

    lax.fori_loop(0, n // 128, block, 0)


def head_rows():
    for s in range(16):
        for q in range(4):
            for h in range(2):
                yield 256 * h + 128 * (s // 8) + 32 * q + 4 * (s % 8), (s, 2 * q + h)


def head_kernel(d_ref, c_ref, inv_ref, p_ref, u_ref, a, g):
    for o, piece in head_rows():
        a[o:o + 4, :] = d_ref[piece]
    inverse_factor512(a, inv_ref, g)
    p = dot(c_ref[...], inv_ref[...], 1, 1)
    p_ref[...] = p
    u_ref[...] = jnp.broadcast_to(p.astype(BF16)[None], u_ref.shape)


def second_kernel(mask_ref, d_ref, inv0_ref, c_ref, u0_ref, p_ref, u_ref, d10, inv1, a, g):
    for o, (s, i) in head_rows():
        d10[o:o + 4, :] = d_ref[s, i, :, 0:512]
        a[o:o + 4, :] = d_ref[s, i, :, 512:1024]
    u10 = dot(d10[...], inv0_ref[...], 1, 1).astype(BF16)
    a[...] = a[...] - dot16(u10, u10, 1, 1)
    c1 = c_ref[...] - dot16(u0_ref[0], u10, 1, 1)
    inverse_factor512(a, inv1, g)
    p1 = dot(c1, inv1[...], 1, 1)
    p_ref[...] = jnp.where(mask_ref[0] > 0, p1, 0.0)
    u_ref[...] = jnp.broadcast_to(p1.astype(BF16)[None], u_ref.shape)


def place(b, y_ref):
    col = pl.multiple_of(jnp.maximum(b, 0) * 128, 128)
    return jnp.where(b >= 0, y_ref[:, pl.ds(col, 128)], 0.0)


def place_panel_kernel(panel_ref, y_ref, p_ref):
    for m in range(4):
        p_ref[:, 128 * m:128 * m + 128] = place(panel_ref[m], y_ref)


def place_kernel(bulk_ref, y_ref, o_ref):
    def one(slot, carry):
        out = pl.multiple_of((slot % 4) * 128, 128)
        o_ref[slot // 4, :, pl.ds(out, 128)] = place(bulk_ref[slot], y_ref)
        return carry

    lax.fori_loop(0, 64, one, 0)


def picked(b, ref):
    v = ref[jnp.maximum(b, 0) + 8]
    return jnp.where(b >= 0, v, jnp.zeros_like(v))


def sender(refs, q_ref, p):
    j = p ^ q_ref[0]

    def read(i):
        x, near, far, corner = [ref[i] for ref in refs]
        return jnp.where(j >= 2, jnp.where(j == 3, corner, far), jnp.where(j == 1, near, x))

    return read


def columns_of(refs, q_ref):
    return jnp.concatenate([sender(refs, q_ref, q)(m) for m in range(4) for q in range(4)], axis=0)


def select_kernel(panel_ref, bulk_ref, u0_ref, u1_ref, p_ref, o_ref):
    for ref, out in ((panel_ref, p_ref), (bulk_ref, o_ref)):
        for i in range(4):
            out[i, :, 0:512] = picked(ref[i], u0_ref)
            out[i, :, 512:1024] = picked(ref[i], u1_ref)


def panel_kernel(q_ref, rows_ref, panel_ref, u0_ref, u1_ref, fp_ref, c0, c1, c2, c3, z_ref, t_ref):
    upan = columns_of((c0, c1, c2, c3), q_ref)
    for ref, out in ((panel_ref, t_ref), (rows_ref, z_ref)):
        f, u0, u1 = [jnp.concatenate([picked(ref[i], x) for i in range(4)], axis=0) for x in (fp_ref, u0_ref, u1_ref)]
        out[...] = f - dot16(jnp.concatenate([u0, u1], axis=1), upan, 1, 1)


def bulk_kernel(q_ref, panel_ref, u0_ref, u1_ref, f_ref, c0, c1, c2, c3, own_ref, other_ref, first_ref, send_ref):
    rows = jnp.concatenate([u0_ref[8:32].reshape(768, 512), u1_ref[8:32].reshape(768, 512)], axis=1)
    s = f_ref[8:32].reshape(768, 512) - dot16(rows, columns_of((c0, c1, c2, c3), q_ref), 1, 1)
    own_ref[...] = s[:, 0:256]
    other_ref[...] = s[:, 256:512]
    for m in range(4):
        b = panel_ref[m]
        rows = pl.ds(pl.multiple_of(32 * jnp.maximum(b, 0), 32), 32)
        first_ref[32 * m:32 * m + 32, :] = jnp.where(b >= 0, own_ref[rows, :], 0.0)
        send_ref[32 * m:32 * m + 32, :] = jnp.where(b >= 0, other_ref[rows, :], 0.0)


def root_kernel(q_ref, t0, t1, t2, t3, inv_ref, a, g):
    for q in range(4):
        read = sender((t0, t1, t2, t3), q_ref, q)
        for m in range(4):
            a[128 * m + 32 * q:128 * m + 32 * q + 32, :] = read(m)
    inverse_factor512(a, inv_ref, g)


def spread_kernel(mine_ref, theirs_ref, own_ref, got_ref, o_ref):
    def one(m, carry):
        i = mine_ref[m]
        j = theirs_ref[m]
        v = own_ref[jnp.maximum(i, 0)]
        w = got_ref[jnp.maximum(j, 0)]
        o_ref[m] = jnp.where(i >= 0, v, 0.0) + jnp.where(j >= 0, w, 0.0)
        return carry

    lax.fori_loop(0, 64, one, 0)


def factor_kernel(flag_ref, panel_ref, inv_ref, cp_ref, p_ref, u_ref, ug_ref, cps):
    step = pl.program_id(0)

    @pl.when(step == 0)
    def _():
        for q in range(4):
            for m in range(4):
                cps[128 * m + 32 * q:128 * m + 32 * q + 32, :] = cp_ref[q, m]
        v = dot(inv_ref[...], cps[...], 1, 0).astype(BF16)
        ug_ref[...] = jnp.where(flag_ref[0] > 0, v, jnp.zeros_like(v))

    p = dot(panel_ref[...], inv_ref[...], 1, 1)
    p_ref[...] = p
    u = p.astype(BF16)
    u_ref[...] = jnp.where((flag_ref[1] > 0) | (step >= 1), u, jnp.zeros_like(u))


def last_kernel(q_ref, u_ref, ug_ref, root_ref, g0, g1, g2, g3, o_ref):
    upd = dot16(u_ref[...], ug_ref[...], 1, 0)
    for q in range(4):
        read = sender((g0, g1, g2, g3), q_ref, q)
        for m in range(4):
            o = 128 * m + 32 * q
            o_ref[o:o + 32, :] = root_ref[o:o + 32, :] + read(m) - upd[o:o + 32, :]


def vmem():
    return pl.BlockSpec(memory_space=pltpu.VMEM)


def smem():
    return pl.BlockSpec(memory_space=pltpu.SMEM)


def call(kernel, outs, n_scalar, n_vector, scratch=(), flops=0, name=None):
    return pl.pallas_call(
        kernel,
        out_shape=outs,
        in_specs=[smem()] * n_scalar + [vmem()] * n_vector,
        out_specs=jax.tree.map(lambda _: vmem(), outs),
        scratch_shapes=list(scratch),
        compiler_params=VM,
        cost_estimate=pl.CostEstimate(flops=flops, transcendentals=0, bytes_accessed=1 << 20),
        name=name,
    )


def sds(shape, dtype=F32):
    return jax.ShapeDtypeStruct(shape, dtype)


CHOL = [pltpu.VMEM((512, 512), F32), pltpu.VMEM((128, 128), F32)]


def exchange(x, axis):
    return lax.all_to_all(x, axis, split_axis=0, concat_axis=0, tiled=True)


def gather(x, axis, n):
    return exchange(jnp.broadcast_to(x[None], (n,) + x.shape), axis)


def in_order(own, near, far, corner, q):
    even = q % 2 == 0
    low = q < 2
    a0, a1 = jnp.where(even, own, near), jnp.where(even, near, own)
    b0, b1 = jnp.where(even, far, corner), jnp.where(even, corner, far)
    return jnp.stack([jnp.where(low, a0, b0), jnp.where(low, a1, b1), jnp.where(low, b0, a0), jnp.where(low, b1, a1)])


def across(x, k):
    return lax.ppermute(x, "col", [(i, i ^ k) for i in range(4)])


def around(x):
    far = across(x, 2)
    return [x, across(x, 1), far, across(far, 1)]


def gather_col(x, q):
    return in_order(*around(x), q)


def from_first_col(x, q):
    sent = [lax.ppermute(x[k], "col", [(0, k)]) for k in (1, 2, 3)]
    return jnp.where(q == 0, x[0], sent[0] + sent[1] + sent[2])


def exchange_col(x, q):
    return in_order(*sent_col(x, q), q)


def sent_col(x, q):
    parts = [lax.dynamic_index_in_dim(x, q ^ k, 0, keepdims=False) for k in range(4)]
    return [parts[0]] + [across(parts[k], k) for k in (1, 2, 3)]


def after(x, *earlier):
    return lax.optimization_barrier((x,) + earlier)[0]


def swap_child(x):
    return lax.ppermute(x, "child", [(0, 1), (1, 0)])


def local(child_fronts, root_front, block_maps):
    front = child_fronts[0]
    child = lax.axis_index("child")
    r = lax.axis_index("row")
    q = lax.axis_index("col")
    blocks = jnp.arange(64, dtype=jnp.int32)
    order = jnp.arange(1, NCB + 1, dtype=jnp.int32)
    inverse = jnp.sum(jnp.where(block_maps[:, :, None] == blocks, order[None, :, None], 0), axis=1) - 1
    mine = jnp.where(child == 0, inverse[0], inverse[1])
    theirs = jnp.where(child == 0, inverse[1], inverse[0])

    def pick(idx):
        return jnp.sum(jnp.where(idx[:, None] == blocks[None, :], mine[None, :], 0), axis=1)

    slot = jnp.arange(64, dtype=jnp.int32)
    half = jnp.where(slot % 4 >= 2, 1 - child, child)
    bulk_idx = pick(32 * half + 2 * (slot // 4) + slot % 2)
    panel_idx = mine[0:4]
    at = q[None]
    four = jnp.arange(4, dtype=jnp.int32)
    col_idx = pick(32 * jnp.where(four >= 2, 1 - child, child) + 2 * r + four % 2)
    row_idx = pick(16 * four + r)

    quarters = front.reshape(2, 4, 32, 1024).transpose(1, 0, 2, 3).reshape(4, 64, 1024)
    raw_top = root_front[0:512].reshape(4, 4, 32, 256).transpose(1, 0, 2, 3).reshape(4, 2, 64, 256)
    pack = from_first_col(jnp.concatenate([quarters, raw_top[:, 0], raw_top[:, 1]], axis=2), q)
    left = pack[:, 0:512]
    top = jnp.concatenate([pack[:, 1024:1280], pack[:, 1280:1536]], axis=0)

    heads = exchange(pack.reshape(16, 4, 1536), "row")
    first, second, corner0, corner1 = lax.optimization_barrier(
        (heads[0:2, :, 0:512], heads[2:4, :, 0:1024], heads[0:1, :, 1024:1536], heads[1:2, :, 1024:1536]))
    d00 = gather(gather_col(first, q).reshape(8, 4, 512), "row", ROWS)
    corner = jnp.concatenate([corner0, corner1], axis=2)
    second = jnp.concatenate([gather_col(second, q).reshape(8, 4, 1024), corner], axis=0)
    second = jnp.broadcast_to(second[None], (ROWS,) + second.shape)
    d00, second = lax.optimization_barrier((d00, second))
    d1 = exchange(second, "row")
    raw_diag = jnp.concatenate([
        jnp.concatenate([d1[:, 8, :, c:c + 256] for c in (o, o + 512)], axis=2).reshape(64, 512) for o in (0, 256)
    ], axis=0)
    raw_diag = jnp.where(child == 0, raw_diag, 0.0)

    y = exchange_col(after(quarters, pack), q)
    panel_y = y[1][:, 0:512]
    placed_panel = call(place_panel_kernel, sds((64, 512)), 1, 1, name="place_panel")(panel_idx, panel_y)

    d00, placed_panel = lax.optimization_barrier((d00, placed_panel))
    inv0, p0, u0 = call(
        head_kernel, (sds((512, 512)), sds((64, 512)), sds((ROWS, 64, 512), BF16)), 0, 2, CHOL, 2 * 10**10, "head")(d00, left)
    f_panel = lax.all_gather(placed_panel, "row").reshape(32, 32, 512)
    d1, u0 = lax.optimization_barrier((d1, u0))
    u0_all = exchange(u0, "row").reshape(32, 32, 512)

    raw_rows = []
    tile_top = after(root_front[0:512], inv0)
    for j in range(2):
        pairs = []
        for g in range(32):
            m = 2 * g + j
            pairs.append((4 * g, (m // 32 * 16 + m % 16) * 4 + m // 16))
        raw_rows.append(lax.ppermute(tile_top[:, 128 * j:128 * j + 128], ("child", "row", "col"), pairs))

    below = (r >= 2).astype(jnp.int32)[None]
    p1, u1 = call(
        second_kernel, (sds((64, 512)), sds((ROWS, 64, 512), BF16)), 1, 4,
        [pltpu.VMEM((512, 512), F32)] * 2 + CHOL, 3 * 10**10, "second")(below, d1, inv0, pack[:, 512:1024], u0)
    factor0 = p0.reshape(2, 32, 512)
    u1, u0_all, far0, raw_rows = lax.optimization_barrier((u1, u0_all, across(factor0, 2), raw_rows))
    raw_rows = (raw_rows[0] + raw_rows[1]).T
    u1_all = exchange(u1, "row").reshape(32, 32, 512)
    wide = after(jnp.concatenate([y[1], y[2], y[3]], axis=1), u1)
    placed = call(place_kernel, sds((16, 64, 512)), 1, 1, name="place")(bulk_idx, wide)
    factor0 = after(factor0, u1)
    factor0 = in_order(factor0, across(factor0, 1), far0, across(far0, 1), q)
    factor1 = p1.reshape(2, 32, 512)
    u1_all, placed, factor0, far1 = lax.optimization_barrier(
        (u1_all, placed, factor0, across(after(factor1, u1), 2)))
    f_bulk = exchange(placed, "row").reshape(32, 32, 512)

    some = sds((4, 32, 1024), BF16)
    u_panel, u_bulk = call(select_kernel, (some, some), 2, 2, name="select")(panel_idx, col_idx, u0_all, u1_all)
    u_panel = around(u_panel)
    u_bulk = after(u_bulk, u_panel[2])
    bulk_far = across(u_bulk, 2)
    z, t = call(panel_kernel, (sds((128, 512)), sds((128, 512))), 3, 7, flops=10**9, name="panel")(
        at, row_idx, panel_idx, u0_all, u1_all, f_panel, *u_panel)
    z, t, bulk_far = lax.optimization_barrier((z, t, bulk_far))
    t = t + raw_diag
    t = t + swap_child(t)
    u_bulk = [u_bulk, across(u_bulk, 1), bulk_far, across(bulk_far, 1)]
    z = exchange_col(z.reshape(4, 32, 512), q).reshape(128, 512) + raw_rows
    half, block = sds((768, 256)), sds((128, 256))
    z, t, u_bulk, f_bulk = lax.optimization_barrier((z, t, u_bulk, f_bulk))
    z_swapped = swap_child(z)
    t = t.reshape(4, 32, 512)
    t_far = across(t, 2)
    own, other, first, sent = call(
        bulk_kernel, (half, half, block, block), 2, 7, flops=4 * 10**9, name="bulk")(
        at, panel_idx, u0_all, u1_all, f_bulk, *u_bulk)
    z_swapped, own, other, t_far = lax.optimization_barrier((z_swapped, own, other, t_far))
    z = z + z_swapped
    panel = lax.all_gather(z, "row", tiled=True)

    t_all = [t, across(t, 1), t_far, across(t_far, 1)]
    sent = swap_child(sent)
    t_all, z, other = lax.optimization_barrier((t_all, z, other))
    inv_root = call(root_kernel, sds((512, 512)), 1, 4, CHOL, 2 * 10**10, "root")(at, *t_all)
    got, inv_root, sent = lax.optimization_barrier((swap_child(other), inv_root, sent))
    head_cols = (top + first + sent).reshape(4, 32, 256)
    head_far = across(head_cols, 2)
    spread = call(spread_kernel, sds((64, 32, 256)), 2, 2, name="spread")(
        mine, theirs, own.reshape(24, 32, 256), got.reshape(24, 32, 256))
    arrived = sent_col(spread.reshape(4, 16, 32, 256), q)
    head_cols = in_order(head_cols, across(head_cols, 1), head_far, across(head_far, 1), q)

    flags = jnp.stack([16 * child + r >= 2, q > 0]).astype(jnp.int32)
    rows = pl.BlockSpec((512, 512), lambda i: (i, 0))
    whole = pl.BlockSpec((512, 512), lambda i: (0, 0))
    narrow = pl.BlockSpec((512, 256), lambda i: (i, 0))
    fixed = pl.BlockSpec((512, 256), lambda i: (0, 0))
    root_factor, u_root, u_cols = pl.pallas_call(
        factor_kernel,
        out_shape=(sds((2048, 512)), sds((2048, 512), BF16), sds((512, 256), BF16)),
        grid=(4,),
        in_specs=[smem(), rows, whole, pl.BlockSpec((4, 4, 32, 256), lambda i: (0, 0, 0, 0))],
        out_specs=(rows, rows, fixed),
        scratch_shapes=[pltpu.VMEM((512, 256), F32)],
        compiler_params=VM,
        cost_estimate=pl.CostEstimate(flops=10**10, transcendentals=0, bytes_accessed=1 << 20),
        name="factor",
    )(flags, panel, inv_root, head_cols)
    arrived, u_root = lax.optimization_barrier((arrived, u_root))
    factor1 = after(factor1, u_root)
    factor1 = in_order(factor1, across(factor1, 1), far1, across(after(far1, u_root), 1), q)
    child_factor = jnp.concatenate([factor0, factor1], axis=3).transpose(1, 0, 2, 3).reshape(1, 256, 1024)
    trailing = pl.pallas_call(
        last_kernel,
        out_shape=sds((2048, 256)),
        grid=(4,),
        in_specs=[smem(), rows, fixed, narrow] + [pl.BlockSpec((4, 32, 256), lambda i: (i, 0, 0))] * 4,
        out_specs=narrow,
        compiler_params=VM,
        name="last",
    )(at, u_root, u_cols, root_front, *arrived)
    return (child_factor, root_factor, trailing)


def solution(mesh):
    return jax.shard_map(
        local,
        mesh=mesh,
        in_specs=(P("child", "row", "col"), P("col", ("child", "row")), P()),
        out_specs=(P("child", "row", None), P("col", None), P("col", ("child", "row"))),
        check_vma=False,
    )
```
